32 devices in a mesh: section: 4 (over y, x), frame: 4 (over z), row: 2 (over core).
Axes of the slice: x: 2, y: 2, z: 4, core: 2. Of those that a mesh axis runs over, the one named last changes fastest.
Arguments:
- x_saved: bfloat16 [4, 8, 16, 64, 128], P('section', 'frame', 'row'), may hold values from -6 to 6
- cotangent: bfloat16 [8, 16, 64, 128], P('frame', 'row'), may hold values from -6 to 6
- w_spatial: bfloat16 [4, 3, 3, 128, 128], P('section'), may hold values from -0.1875 to 0.1875
- w_temporal: bfloat16 [4, 3, 128, 128], P('section'), may hold values from -0.3125 to 0.3125
Outputs:
- grad_inputs: bfloat16 [4, 8, 16, 64, 128], P('section', 'frame', 'row')
- grad_spatial: float32 [4, 3, 3, 128, 128], P('section')
- grad_temporal: float32 [4, 3, 128, 128], P('section')
The draws below stay inside these ranges and needn't reach their ends.
All inputs are finite; a program needn't handle non-finite values.
Results may differ from the reference program's by a relative error of at most 0.014.
Values may be sent and summed in bfloat16 or wider, within the bound.
No kernel may reach another device: no remote copies, remote signals or barrier semaphores. Data moves between devices by JAX's collectives and lax.ppermute only.
A program may use at most 64 MiB of HBM per device.

```python
import jax
import jax.numpy as jnp
from jax import lax

C = 128
COLS = 64
SECTIONS = 4
FRAMES = 8
ROWS = 16


def block_levels(key, dims, cuts, least, top_value):
    loudness, own = 1.0, jax.random.fold_in(key, 6)
    for axis_at, shards_of in cuts:
        steps = jnp.exp(jax.random.uniform(jax.random.fold_in(own, axis_at), (shards_of,), jnp.float32, least / len(cuts), top_value / len(cuts)))
        loudness = loudness * jnp.repeat(steps, dims[axis_at] // shards_of).reshape([-1 if axis == axis_at else 1 for axis in range(len(dims))])
    return loudness


def bell_draw(stream_key, shape, spread, reach, split=(), kind=jnp.bfloat16):
    array = jax.random.normal(stream_key, shape, jnp.float32) * spread
    if len(split) > 0:
        array = block_levels(stream_key, shape, split, -0.22, 0.18) * array
    return jnp.clip(array, min=-reach, max=reach).astype(kind)


def setup_inputs(seed: int = 0) -> dict:
    key_list = jax.random.split(jax.random.key(seed), 5)
    x_saved = bell_draw(key_list[0], (SECTIONS, FRAMES, ROWS, COLS, C), 1.0, 6.0, ((0, 4), (1, 4), (2, 2)))
    cotangent = bell_draw(key_list[1], (FRAMES, ROWS, COLS, C), 1.0, 6.0, ((0, 4), (1, 2)))
    w_spatial = bell_draw(key_list[2], (SECTIONS, 3, 3, C, C), (9 * C) ** -0.5, 0.1875, ((0, 4),))
    w_temporal = bell_draw(key_list[3], (SECTIONS, 3, C, C), (3 * C) ** -0.5, 0.3125, ((0, 4),))
    return dict(x_saved=x_saved, cotangent=cotangent, w_spatial=w_spatial, w_temporal=w_temporal)


def slope_of(pre_act):
    sigma = jax.nn.sigmoid(pre_act)
    return sigma * (1.0 + pre_act * (1.0 - sigma))


def inner_sum(first_arg, second_arg):
    return lax.dot_general(first_arg, second_arg, (((0,), (0,)), ((), ())), preferred_element_type=jnp.float32)


def pad_image(values):
    return jnp.pad(values, ((0, 0), (1, 1), (1, 1), (0, 0)))


def frame_shift(values, offset, max_reach):
    widths = [(max_reach, max_reach)] + [(0, 0)] * (values.ndim - 1)
    padded = jnp.pad(values, widths)
    return lax.dynamic_slice_in_dim(padded, max_reach + offset, values.shape[0], 0)


def apply_taps(padded, taps, row_count, col_count, transpose):
    channels = padded.shape[-1]
    running = jnp.zeros((padded.shape[0] * row_count * col_count, taps.shape[-1]), jnp.float32)
    for i in range(3):
        for j in range(3):
            window = padded[:, i:i + row_count, j:j + col_count, :].reshape(-1, channels)
            if transpose:
                running = running + jnp.dot(window, taps[2 - i, 2 - j].T, preferred_element_type=jnp.float32)
            else:
                running = running + jnp.dot(window, taps[i, j], preferred_element_type=jnp.float32)
    return running.reshape(padded.shape[0], row_count, col_count, taps.shape[-1])


def reference(x_saved, cotangent, w_spatial, w_temporal):
    frame_count, row_count, col_count, channels = cotangent.shape
    section_count = x_saved.shape[0]
    max_reach = 2 ** (section_count - 1)
    incoming = cotangent
    own_grads = [None] * section_count
    space_grads = [None] * section_count
    time_grads = [None] * section_count
    for section_index in reversed(range(section_count)):
        dilation = 2 ** section_index
        taps_space = w_spatial[section_index]
        taps_time = w_temporal[section_index]
        extended = pad_image(x_saved[section_index])
        pre_act = apply_taps(extended, taps_space, row_count, col_count, False)
        active = jax.nn.silu(pre_act).astype(jnp.bfloat16)
        running = jnp.zeros((frame_count * row_count * col_count, channels), jnp.float32)
        for k in range(3):
            shifted = frame_shift(incoming, (1 - k) * dilation, max_reach).reshape(-1, channels)
            running = running + jnp.dot(shifted, taps_time[k].T, preferred_element_type=jnp.float32)
        back_act = running.astype(jnp.bfloat16).reshape(cotangent.shape)
        grad_pre = (lax.optimization_barrier(back_act).astype(jnp.float32) * slope_of(pre_act)).astype(jnp.bfloat16)
        branch = apply_taps(pad_image(grad_pre), taps_space, row_count, col_count, True).astype(jnp.bfloat16)
        outgoing = (incoming.astype(jnp.float32) + lax.optimization_barrier(branch).astype(jnp.float32)).astype(jnp.bfloat16)
        flat_pre = grad_pre.reshape(-1, channels)
        space_grads[section_index] = jnp.stack([jnp.stack([inner_sum(extended[:, i:i + row_count, j:j + col_count, :].reshape(-1, channels), flat_pre) for j in range(3)]) for i in range(3)])
        flat_in = incoming.reshape(-1, channels)
        time_grads[section_index] = jnp.stack([inner_sum(frame_shift(active, (k - 1) * dilation, max_reach).reshape(-1, channels), flat_in) for k in range(3)])
        own_grads[section_index] = outgoing
        incoming = outgoing
    return jnp.stack(own_grads), jnp.stack(space_grads), jnp.stack(time_grads)
```

```python
import jax
import jax.numpy as jnp
from jax import lax
from jax.sharding import PartitionSpec as P


def slope_of(pre_act):
    sigma = jax.nn.sigmoid(pre_act)
    return sigma * (1.0 + pre_act * (1.0 - sigma))


def inner_sum(first_arg, second_arg):
    return lax.dot_general(
        first_arg, second_arg, (((0,), (0,)), ((), ())), preferred_element_type=jnp.float32
    )


def row_halo(cells):
    count = lax.axis_size("row")
    index = lax.axis_index("row")
    head = cells[:, :1]
    tail = cells[:, -1:]
    nothing = jnp.zeros_like(head)
    if count == 1:
        above, below = nothing, nothing
    elif count == 2:
        got = lax.ppermute(jnp.where(index == 0, tail, head), "row", [(0, 1), (1, 0)])
        above = jnp.where(index == 0, nothing, got)
        below = jnp.where(index == 0, got, nothing)
    else:
        above = lax.ppermute(tail, "row", [(i, i + 1) for i in range(count - 1)])
        below = lax.ppermute(head, "row", [(i + 1, i) for i in range(count - 1)])
    return jnp.concatenate([above, cells, below], axis=1)


def pad_cols(values):
    return jnp.pad(values, ((0, 0), (0, 0), (1, 1), (0, 0)))


def apply_taps(padded, taps, row_count, col_count, transpose):
    channels = padded.shape[-1]
    running = jnp.zeros((padded.shape[0] * row_count * col_count, taps.shape[-1]), jnp.float32)
    for i in range(3):
        for j in range(3):
            window = padded[:, i : i + row_count, j : j + col_count, :].reshape(-1, channels)
            if transpose:
                tap = taps[2 - i, 2 - j].T
            else:
                tap = taps[i, j]
            running = running + jnp.dot(window, tap, preferred_element_type=jnp.float32)
    return running.reshape(padded.shape[0], row_count, col_count, taps.shape[-1])


def fetch(block, source, target, frame_step):
    frame_parts = lax.axis_size("frame")
    route = [
        (source * frame_parts + z + frame_step, target * frame_parts + z)
        for z in range(frame_parts)
        if 0 <= z + frame_step < frame_parts
    ]
    if not route or (source == target and frame_step == 0):
        return block if route else jnp.zeros_like(block)
    return lax.ppermute(block, ("section", "frame"), route)


def shifted_from(block, source, target, offset):
    own_frames = block.shape[0]
    step, rest = divmod(offset, own_frames)
    if rest == 0:
        return fetch(block, source, target, step)
    return jnp.concatenate(
        [fetch(block[rest:], source, target, step), fetch(block[:rest], source, target, step + 1)]
    )


def pair_from(block, source, target, dilation):
    own_frames = block.shape[0]
    frame_parts = lax.axis_size("frame")
    step, rest = divmod(dilation, own_frames)
    nothing = jnp.zeros_like(block)
    if step >= frame_parts:
        return nothing, nothing
    if rest == 0 and 2 * step >= frame_parts:
        route = [
            (source * frame_parts + z + move, target * frame_parts + z)
            for z in range(frame_parts)
            for move in (step, -step)
            if 0 <= z + move < frame_parts
        ]
        got = lax.ppermute(block, ("section", "frame"), route)
        early = lax.axis_index("frame") < frame_parts - step
        return jnp.where(early, got, nothing), jnp.where(early, nothing, got)
    return (
        shifted_from(block, source, target, dilation),
        shifted_from(block, source, target, -dilation),
    )


def gather_parts(part, axis):
    count = lax.axis_size(axis)
    if count == 1:
        return part
    if count & (count - 1) or count > 4:
        return lax.all_gather(part, axis, axis=0, tiled=True)
    index = lax.axis_index(axis)
    size = part.shape[0]
    whole = jnp.zeros((count * size,) + part.shape[1:], part.dtype)
    whole = lax.dynamic_update_slice_in_dim(whole, part, index * size, 0)
    for mask in range(1, count):
        got = lax.ppermute(part, axis, [(i, i ^ mask) for i in range(count)])
        whole = lax.dynamic_update_slice_in_dim(whole, got, (index ^ mask) * size, 0)
    return whole


def sum_over(values, axis):
    count = lax.axis_size(axis)
    if count == 1:
        return values
    size = values.shape[0] // count
    if count == 2:
        index = lax.axis_index(axis)
        own = lax.dynamic_slice_in_dim(values, index * size, size, 0)
        other = lax.dynamic_slice_in_dim(values, (1 - index) * size, size, 0)
        got = lax.ppermute(other.astype(jnp.bfloat16), axis, [(0, 1), (1, 0)])
        return own + got.astype(jnp.float32)
    parts = values.astype(jnp.bfloat16).reshape((count, size) + values.shape[1:])
    parts = lax.all_to_all(parts, axis, split_axis=0, concat_axis=0, tiled=True)
    return jnp.sum(parts.astype(jnp.float32), axis=0)


def section_run(x_saved, cotangent, w_spatial, w_temporal):
    block_input = x_saved[0]
    taps_space = w_spatial[0]
    taps_time = w_temporal[0]
    local_shape = block_input.shape
    row_count = local_shape[1]
    col_count = local_shape[2]
    channels = local_shape[3]
    section_count = lax.axis_size("section")
    section_index = lax.axis_index("section")
    extended = pad_cols(row_halo(block_input))
    pre_act = apply_taps(extended, taps_space, row_count, col_count, False)
    pre_slope = slope_of(pre_act)
    active = jax.nn.silu(pre_act).astype(jnp.bfloat16)

    top = section_count - 1
    here = cotangent
    later, earlier = pair_from(cotangent, top, top, 2**top)
    for position in range(section_count):
        owner = top - position
        running = jnp.dot(
            here.reshape(-1, channels), taps_time[1].T, preferred_element_type=jnp.float32
        )
        running += jnp.dot(
            later.reshape(-1, channels), taps_time[0].T, preferred_element_type=jnp.float32
        )
        running += jnp.dot(
            earlier.reshape(-1, channels), taps_time[2].T, preferred_element_type=jnp.float32
        )
        back_act = running.astype(jnp.bfloat16).reshape(local_shape)
        grad_pre = (back_act.astype(jnp.float32) * pre_slope).astype(jnp.bfloat16)
        padded = pad_cols(row_halo(grad_pre))
        branch = apply_taps(padded, taps_space, row_count, col_count, True).astype(jnp.bfloat16)
        outgoing = (here.astype(jnp.float32) + branch.astype(jnp.float32)).astype(jnp.bfloat16)
        if position + 1 < section_count:
            arrives = section_index == owner - 1
            new_later, new_earlier = pair_from(outgoing, owner, owner - 1, 2 ** (owner - 1))
            new_here = fetch(outgoing, owner, owner - 1, 0)
            here = jnp.where(arrives, new_here, here)
            later = jnp.where(arrives, new_later, later)
            earlier = jnp.where(arrives, new_earlier, earlier)

    flat_pre = grad_pre.reshape(-1, channels)
    flat_active = active.reshape(-1, channels)
    grads = [
        inner_sum(
            extended[:, i : i + row_count, j : j + col_count, :].reshape(-1, channels), flat_pre
        )
        for i in range(3)
        for j in range(3)
    ]
    grads += [inner_sum(flat_active, g.reshape(-1, channels)) for g in (later, here, earlier)]
    total = sum_over(jnp.concatenate(grads), "row")
    total = sum_over(total, "frame").astype(jnp.bfloat16)
    total = gather_parts(gather_parts(total, "frame"), "row").astype(jnp.float32)
    total = total.reshape((12, channels, channels))
    return (
        outgoing[None],
        total[:9].reshape((1, 3, 3, channels, channels)),
        total[9:][None],
    )


def solution(mesh):
    return jax.shard_map(
        section_run,
        mesh=mesh,
        in_specs=(
            P("section", "frame", "row", None, None),
            P("frame", "row", None, None),
            P("section", None, None, None, None),
            P("section", None, None, None),
        ),
        out_specs=(
            P("section", "frame", "row", None, None),
            P("section", None, None, None, None),
            P("section", None, None, None),
        ),
        check_vma=False,
    )
```

```python
import jax
import jax.numpy as jnp
from jax import lax
from jax.sharding import PartitionSpec as P


def slope_of(pre_act):
    sigma = jax.nn.sigmoid(pre_act)
    return sigma * (1.0 + pre_act * (1.0 - sigma))


def inner_sum(first_arg, second_arg):
    return lax.dot_general(
        first_arg, second_arg, (((0,), (0,)), ((), ())), preferred_element_type=jnp.float32
    )


def row_halo(cells):
    count = lax.axis_size("row")
    index = lax.axis_index("row")
    head = cells[:, :1]
    tail = cells[:, -1:]
    nothing = jnp.zeros_like(head)
    if count == 1:
        above, below = nothing, nothing
    elif count == 2:
        got = lax.ppermute(jnp.where(index == 0, tail, head), "row", [(0, 1), (1, 0)])
        above = jnp.where(index == 0, nothing, got)
        below = jnp.where(index == 0, got, nothing)
    else:
        above = lax.ppermute(tail, "row", [(i, i + 1) for i in range(count - 1)])
        below = lax.ppermute(head, "row", [(i + 1, i) for i in range(count - 1)])
    return jnp.concatenate([above, cells, below], axis=1)


def pad_cols(values):
    return jnp.pad(values, ((0, 0), (0, 0), (1, 1), (0, 0)))


def apply_taps(padded, taps, row_count, col_count, transpose):
    channels = padded.shape[-1]
    running = jnp.zeros((padded.shape[0] * row_count * col_count, taps.shape[-1]), jnp.float32)
    for i in range(3):
        for j in range(3):
            window = padded[:, i : i + row_count, j : j + col_count, :].reshape(-1, channels)
            if transpose:
                tap = taps[2 - i, 2 - j].T
            else:
                tap = taps[i, j]
            running = running + jnp.dot(window, tap, preferred_element_type=jnp.float32)
    return running.reshape(padded.shape[0], row_count, col_count, taps.shape[-1])


def fetch(block, source, target, frame_step):
    frame_parts = lax.axis_size("frame")
    route = [
        (source * frame_parts + z + frame_step, target * frame_parts + z)
        for z in range(frame_parts)
        if 0 <= z + frame_step < frame_parts
    ]
    if not route:
        return jnp.zeros_like(block)
    if source == target and frame_step == 0:
        return block
    return lax.ppermute(block, ("section", "frame"), route)


def shifted_from(block, source, target, offset, unmoved=None):
    own_frames = block.shape[0]
    step, rest = divmod(offset, own_frames)
    pieces = []
    for frames, move in ((slice(rest, None), step), (slice(0, rest), step + 1)):
        piece = block[frames]
        if piece.shape[0] == 0:
            continue
        if move == 0 and unmoved is not None:
            pieces.append(unmoved[frames])
        else:
            pieces.append(fetch(piece, source, target, move))
    return pieces[0] if len(pieces) == 1 else jnp.concatenate(pieces)


def triple_from(block, source, target, distance, staged):
    own_frames = block.shape[0]
    frame_parts = lax.axis_size("frame")
    step, rest = divmod(distance, own_frames)
    nothing = jnp.zeros_like(block)
    own = fetch(block, source, target, 0)
    if step >= frame_parts:
        return own, nothing, nothing
    if rest == 0 and 2 * step >= frame_parts:
        route = [
            (source * frame_parts + z + move, target * frame_parts + z)
            for z in range(frame_parts)
            for move in (step, -step)
            if 0 <= z + move < frame_parts
        ]
        got = lax.ppermute(block, ("section", "frame"), route)
        early = lax.axis_index("frame") < frame_parts - step
        return own, jnp.where(early, got, nothing), jnp.where(early, nothing, got)
    if staged:
        block, source = own, target
    return (
        own,
        shifted_from(block, source, target, distance, own),
        shifted_from(block, source, target, -distance, own),
    )


def exchange_parts(parts, axis):
    count = lax.axis_size(axis)
    index = lax.axis_index(axis)
    size = parts.shape[0] // count

    def part(at):
        return lax.dynamic_slice_in_dim(parts, at * size, size, 0)

    return [part(index)] + [
        lax.ppermute(part(index ^ mask).astype(jnp.bfloat16), axis, [(i, i ^ mask) for i in range(count)])
        for mask in range(1, count)
    ]


def by_pairs(axis):
    count = lax.axis_size(axis)
    return count <= 4 and count & (count - 1) == 0


def sum_over(values, axis):
    count = lax.axis_size(axis)
    if by_pairs(axis):
        return sum(part.astype(jnp.float32) for part in exchange_parts(values, axis))
    parts = values.astype(jnp.bfloat16).reshape((count, -1) + values.shape[1:])
    parts = lax.all_to_all(parts, axis, split_axis=0, concat_axis=0, tiled=True)
    return jnp.sum(parts.astype(jnp.float32), axis=0)


def gather_parts(part, axis):
    if not by_pairs(axis):
        return lax.all_gather(part, axis, axis=0, tiled=True)
    count = lax.axis_size(axis)
    index = lax.axis_index(axis)
    size = part.shape[0]
    whole = jnp.zeros((count * size,) + part.shape[1:], part.dtype)
    whole = lax.dynamic_update_slice_in_dim(whole, part, index * size, 0)
    for mask in range(1, count):
        got = lax.ppermute(part, axis, [(i, i ^ mask) for i in range(count)])
        whole = lax.dynamic_update_slice_in_dim(whole, got, (index ^ mask) * size, 0)
    return whole


def after(value, other):
    return lax.optimization_barrier((value, other))[0]


def section_run(x_saved, cotangent, w_spatial, w_temporal):
    block_input = x_saved[0]
    taps_space = w_spatial[0]
    taps_time = w_temporal[0]
    local_shape = block_input.shape
    own_frames, row_count, col_count, channels = local_shape
    section_count = lax.axis_size("section")
    section_index = lax.axis_index("section")
    extended = pad_cols(row_halo(block_input))
    pre_act = apply_taps(extended, taps_space, row_count, col_count, False)
    pre_slope = slope_of(pre_act)
    active = jax.nn.silu(pre_act).astype(jnp.bfloat16)

    top = section_count - 1
    chains = 2 if own_frames % 2 == 0 else 1

    def chain_of(values):
        if chains == 1:
            return [values]
        return [
            values.reshape((own_frames // 2, 2) + values.shape[1:])[:, odd] for odd in range(2)
        ]

    def both(parts):
        return parts[0] if chains == 1 else jnp.stack(parts, 1).reshape(local_shape)

    def back_pre(here, later, earlier, slope):
        running = sum(
            jnp.dot(block.reshape(-1, channels), taps_time[k].T, preferred_element_type=jnp.float32)
            for block, k in ((here, 1), (later, 0), (earlier, 2))
        )
        back_act = running.astype(jnp.bfloat16).reshape(here.shape)
        return (back_act.astype(jnp.float32) * slope).astype(jnp.bfloat16)

    def branch_out(grad_pre, here):
        padded = pad_cols(row_halo(grad_pre))
        branch = apply_taps(padded, taps_space, row_count, col_count, True).astype(jnp.bfloat16)
        return (here.astype(jnp.float32) + branch.astype(jnp.float32)).astype(jnp.bfloat16)

    def triples(blocks, source, target):
        dilation = 2**target
        if chains == 1:
            return [triple_from(blocks[0], source, target, dilation, False)]
        if dilation % 2 == 0:
            return [
                triple_from(block, source, target, dilation // 2, True) for block in blocks
            ]
        even, odd = blocks
        own_even = fetch(even, source, target, 0)
        next_even = shifted_from(even, source, target, (dilation + 1) // 2, own_even)
        own_odd = fetch(odd, source, target, 0)
        last_odd = shifted_from(odd, source, target, -((dilation + 1) // 2), own_odd)
        same_odd = shifted_from(odd, source, target, (dilation - 1) // 2, own_odd)
        same_even = shifted_from(even, source, target, -((dilation - 1) // 2), own_even)
        return [(own_even, same_odd, last_odd), (own_odd, next_even, same_even)]

    slopes = chain_of(pre_slope)
    held = triples(chain_of(cotangent), top, top)
    for position in range(top):
        owner = top - position
        outgoing = []
        for chain in range(chains):
            here, later, earlier = held[chain]
            if chain or position:
                last = outgoing[-1] if chain else sent[-1]
                here, later, earlier, _ = lax.optimization_barrier((here, later, earlier, last))
            grad_pre = back_pre(here, later, earlier, slopes[chain])
            outgoing.append(branch_out(grad_pre, here))
        sent = outgoing
        arrives = section_index == owner - 1
        held = [
            tuple(jnp.where(arrives, new, old) for new, old in zip(fresh, kept))
            for fresh, kept in zip(triples(outgoing, owner, owner - 1), held)
        ]

    here, later, earlier = (both([blocks[k] for blocks in held]) for k in range(3))
    grad_pre = back_pre(here, later, earlier, pre_slope)
    flat_pre = grad_pre.reshape(-1, channels)
    flat_active = active.reshape(-1, channels)
    grads = [
        inner_sum(
            extended[:, i : i + row_count, j : j + col_count, :].reshape(-1, channels), flat_pre
        )
        for i in range(3)
        for j in range(3)
    ]
    grads += [inner_sum(flat_active, g.reshape(-1, channels)) for g in (later, here, earlier)]
    total = sum_over(jnp.concatenate(grads), "row")
    outgoing = branch_out(after(grad_pre, total), here)
    total = sum_over(total, "frame").astype(jnp.bfloat16)
    total = gather_parts(total, "frame")
    split = 9 * channels
    if lax.axis_size("row") == 2:
        first = lax.axis_index("row") == 0
        other = lax.ppermute(total, "row", [(0, 1), (1, 0)])
        rest = split - total.shape[0]
        space = jnp.where(
            first,
            jnp.concatenate([total, other[:rest]]),
            jnp.concatenate([other, total[:rest]]),
        )
        time = jnp.where(first, other[rest:], total[rest:])
    else:
        total = gather_parts(total, "row")
        space, time = total[:split], total[split:]
    return (
        outgoing[None],
        space.astype(jnp.float32).reshape((1, 3, 3, channels, channels)),
        time.astype(jnp.float32).reshape((1, 3, channels, channels)),
    )


def solution(mesh):
    return jax.shard_map(
        section_run,
        mesh=mesh,
        in_specs=(
            P("section", "frame", "row", None, None),
            P("frame", "row", None, None),
            P("section", None, None, None, None),
            P("section", None, None, None),
        ),
        out_specs=(
            P("section", "frame", "row", None, None),
            P("section", None, None, None, None),
            P("section", None, None, None),
        ),
        check_vma=False,
    )
```

```python
import functools

import jax
import jax.numpy as jnp
from jax import lax
from jax.experimental import pallas as pl
from jax.experimental.pallas import tpu as pltpu
from jax.sharding import PartitionSpec as P

VMEM_LIMIT = 40 * 1024 * 1024
NT = (((1,), (1,)), ((), ()))
NN = (((1,), (0,)), ((), ()))
TN = (((0,), (0,)), ((), ()))


def mul(a, b, how):
    return lax.dot_general(a, b, how, preferred_element_type=jnp.float32)


def call(body, outs, args, flops):
    moved = sum(a.size * a.dtype.itemsize for a in (*args, *outs))
    return pl.pallas_call(
        body,
        out_shape=outs,
        in_specs=[pl.BlockSpec(memory_space=pltpu.VMEM) for _ in args],
        out_specs=[pl.BlockSpec(memory_space=pltpu.VMEM) for _ in outs],
        compiler_params=pltpu.CompilerParams(vmem_limit_bytes=VMEM_LIMIT),
        cost_estimate=pl.CostEstimate(flops=flops, bytes_accessed=moved, transcendentals=0),
    )(*args)


def flat(values):
    return values.reshape(-1, values.shape[-1])


def row_sides(got, row_count):
    if len(got) == 1:
        first = (lax.axis_index("row") == 0).astype(jnp.float32)
        rows = got[0].astype(jnp.float32)
        return (rows * (1.0 - first)).astype(jnp.bfloat16), (rows * first).astype(jnp.bfloat16)
    return got


def moved_rows(cells, above, below):
    return (
        flat(jnp.concatenate([above, cells[:, :-1]], axis=1)),
        flat(cells),
        flat(jnp.concatenate([cells[:, 1:], below], axis=1)),
    )


def moved_cols(values, step, col_count):
    count = values.shape[0]
    col = lax.broadcasted_iota(jnp.int32, values.shape, 0) % col_count
    if step == 1:
        return jnp.where(col == col_count - 1, 0.0, pltpu.roll(values, count - 1, 0))
    return jnp.where(col == 0, 0.0, pltpu.roll(values, 1, 0))


def edges_of(cells, row_parts):
    head, tail = cells[:, :1], cells[:, -1:]
    if row_parts == 2:
        first = (lax.axis_index("row") == 0).astype(jnp.float32)
        return [(tail.astype(jnp.float32) * first + head.astype(jnp.float32) * (1.0 - first)).astype(jnp.bfloat16)]
    return [head, tail]


def swap_edges(edges):
    count = lax.axis_size("row")
    if count == 2:
        return [lax.ppermute(edges[0], "row", [(0, 1), (1, 0)])]
    head, tail = edges
    if count == 1:
        return [jnp.zeros_like(head), jnp.zeros_like(head)]
    return [
        lax.ppermute(tail, "row", [(i, i + 1) for i in range(count - 1)]),
        lax.ppermute(head, "row", [(i + 1, i) for i in range(count - 1)]),
    ]


def split_frames(values, chains):
    if chains == 1:
        return [values]
    pairs = values.reshape((values.shape[0] // chains, chains) + values.shape[1:])
    return [pairs[:, at] for at in range(chains)]


def forward(block_input, got, taps_space, chains):
    frames, rows, cols, channels = block_input.shape
    part = (frames // chains, rows, cols, channels)

    def body(*refs):
        x_ref, got_refs, w_ref = refs[0], refs[1 : 1 + len(got)], refs[1 + len(got)]
        slope_refs = refs[2 + len(got) : 2 + len(got) + chains]
        active_refs = refs[2 + len(got) + chains :]
        above, below = row_sides([ref[...] for ref in got_refs], rows)
        sides = jnp.concatenate(moved_rows(x_ref[...], above, below), axis=1)
        taps = jnp.concatenate(
            [jnp.concatenate([w_ref[i, j] for j in range(3)], axis=1) for i in range(3)], axis=0
        )
        sums = mul(sides, taps, NN)
        pre_act = (
            moved_cols(sums[:, :channels], -1, cols)
            + sums[:, channels : 2 * channels]
            + moved_cols(sums[:, 2 * channels :], 1, cols)
        )
        sigma = jax.nn.sigmoid(pre_act)
        slope = (sigma * (1.0 + pre_act * (1.0 - sigma))).reshape(x_ref.shape)
        active = (pre_act * sigma).astype(jnp.bfloat16).reshape(x_ref.shape)
        for ref, values in zip(slope_refs, split_frames(slope, chains)):
            ref[...] = values
        for ref, values in zip(active_refs, split_frames(active, chains)):
            ref[...] = values

    outs = [jax.ShapeDtypeStruct(part, jnp.float32)] * chains
    outs += [jax.ShapeDtypeStruct(part, jnp.bfloat16)] * chains
    outs = call(body, outs, [block_input, *got, taps_space], 18 * block_input.size * channels)
    return outs[:chains], outs[chains:]


def early_half(distance_step):
    frame_parts = lax.axis_size("frame")
    return (lax.axis_index("frame") < frame_parts - distance_step).astype(jnp.float32)


def temporal(owner, triples, pair_step, slopes, taps_time):
    row_parts = lax.axis_size("row")
    part = slopes[0].shape
    channels = part[-1]
    edges = 1 if row_parts == 2 else 2
    sizes = [len(triple) for triple in triples]

    def body(*refs):
        @pl.when(lax.axis_index("section") == owner)
        def _():
            at = 0
            w_ref = refs[sum(sizes) + len(slopes)]
            outs = refs[sum(sizes) + len(slopes) + 1 :]
            for chain, size in enumerate(sizes):
                blocks = [flat(ref[...]) for ref in refs[at : at + size]]
                at += size
                taps = [w_ref[1]]
                if size == 2:
                    early = early_half(pair_step)
                    other = early * w_ref[0].astype(jnp.float32)
                    other += (1.0 - early) * w_ref[2].astype(jnp.float32)
                    taps.append(other.astype(jnp.bfloat16))
                elif size == 3:
                    taps += [w_ref[0], w_ref[2]]
                sums = mul(jnp.concatenate(blocks, axis=1), jnp.concatenate(taps, axis=1), NT)
                back_act = sums.astype(jnp.bfloat16).astype(jnp.float32)
                slope = flat(refs[sum(sizes) + chain][...])
                grad_pre = (back_act * slope).astype(jnp.bfloat16).reshape(part)
                outs[chain][...] = grad_pre
                for ref, edge in zip(outs[len(slopes) :], edges_of(grad_pre, row_parts)):
                    ref[chain * part[0] : (chain + 1) * part[0]] = edge

    outs = [jax.ShapeDtypeStruct(part, jnp.bfloat16)] * len(slopes)
    outs += [
        jax.ShapeDtypeStruct((part[0] * len(slopes), 1) + part[2:], jnp.bfloat16)
    ] * edges
    args = [block for triple in triples for block in triple] + list(slopes) + [taps_time]
    outs = call(body, outs, args, 6 * sum(s.size for s in slopes) * channels)
    return outs[: len(slopes)], outs[len(slopes) :]


def branches(owner, grads_pre, got, heres, taps_space):
    part = heres[0].shape
    _, rows, cols, channels = part
    count = len(heres)

    def body(*refs):
        @pl.when(lax.axis_index("section") == owner)
        def _():
            got_refs = refs[count : count + len(got)]
            here_refs = refs[count + len(got) : 2 * count + len(got)]
            w_ref = refs[2 * count + len(got)]
            out_refs = refs[2 * count + len(got) + 1 :]
            taps = jnp.concatenate(
                [jnp.concatenate([w_ref[2 - i, j] for i in range(3)], axis=1) for j in range(3)],
                axis=0,
            )
            for chain in range(count):
                frames = slice(chain * part[0], (chain + 1) * part[0])
                above, below = row_sides([ref[frames] for ref in got_refs], rows)
                sides = jnp.concatenate(moved_rows(refs[chain][...], above, below), axis=1)
                sums = mul(sides, taps, NT)
                branch = (
                    moved_cols(sums[:, :channels], 1, cols)
                    + sums[:, channels : 2 * channels]
                    + moved_cols(sums[:, 2 * channels :], -1, cols)
                )
                branch = branch.astype(jnp.bfloat16).astype(jnp.float32)
                here = flat(here_refs[chain][...]).astype(jnp.float32)
                out_refs[chain][...] = (here + branch).astype(jnp.bfloat16).reshape(part)

    outs = [jax.ShapeDtypeStruct(part, jnp.bfloat16)] * count
    args = [*grads_pre, *got, *heres, taps_space]
    return call(body, outs, args, 18 * sum(h.size for h in heres) * channels)


def kernel_grads(owner, block_input, got, grads_pre, actives, triples, pair_step, before):
    frames, rows, cols, channels = block_input.shape
    chains = len(actives)
    size = len(triples[0])
    fixed = 1 + len(got)

    def body(*refs):
        section = lax.axis_index("section")
        out_ref = refs[-1]

        if before is not None:

            @pl.when(section != owner)
            def _():
                out_ref[...] = refs[-2][...]

        @pl.when(section == owner)
        def _():
            above, below = row_sides([ref[...] for ref in refs[1:fixed]], rows)
            sides = []
            for cells, up, down in zip(
                *(split_frames(v, chains) for v in (refs[0][...], above, below))
            ):
                sides.append(jnp.concatenate(moved_rows(cells, up, down), axis=1))
            pre, blocks = [], []
            at = fixed + 2 * chains
            for chain in range(chains):
                mid = flat(refs[fixed + chain][...])
                wide = mid.astype(jnp.float32)
                left = moved_cols(wide, 1, cols).astype(jnp.bfloat16)
                right = moved_cols(wide, -1, cols).astype(jnp.bfloat16)
                pre.append(jnp.concatenate([left, mid, right], axis=1))
                blocks.append(
                    jnp.concatenate([flat(ref[...]) for ref in refs[at : at + size]], axis=1)
                )
                at += size
            space = mul(jnp.concatenate(sides), jnp.concatenate(pre), TN)
            for i in range(3):
                for j in range(3):
                    out_ref[3 * i + j] = space[
                        i * channels : (i + 1) * channels, j * channels : (j + 1) * channels
                    ]
            active = jnp.concatenate(
                [flat(refs[fixed + chains + chain][...]) for chain in range(chains)]
            )
            time = mul(active, jnp.concatenate(blocks), TN)
            out_ref[10] = time[:, :channels]
            if size == 1:
                out_ref[9] = jnp.zeros((channels, channels), jnp.float32)
                out_ref[11] = jnp.zeros((channels, channels), jnp.float32)
            elif size == 2:
                early = early_half(pair_step)
                out_ref[9] = early * time[:, channels:]
                out_ref[11] = (1.0 - early) * time[:, channels:]
            else:
                out_ref[9] = time[:, channels : 2 * channels]
                out_ref[11] = time[:, 2 * channels :]

    args = [block_input, *got, *grads_pre, *actives]
    args += [block for triple in triples for block in triple]
    if before is not None:
        args.append(before)
    outs = [jax.ShapeDtypeStruct((12, channels, channels), jnp.float32)]
    return call(body, outs, args, 24 * block_input.size * channels)[0]


def fetch(block, source, target, frame_step):
    frame_parts = lax.axis_size("frame")
    route = [
        (source * frame_parts + z + frame_step, target * frame_parts + z)
        for z in range(frame_parts)
        if 0 <= z + frame_step < frame_parts
    ]
    if not route:
        return jnp.zeros_like(block)
    if source == target and frame_step == 0:
        return block
    return lax.ppermute(block, ("section", "frame"), route)


def shifted_from(block, source, target, offset, unmoved=None):
    own_frames = block.shape[0]
    step, rest = divmod(offset, own_frames)
    pieces = []
    for frames, move in ((slice(rest, None), step), (slice(0, rest), step + 1)):
        piece = block[frames]
        if piece.shape[0] == 0:
            continue
        if move == 0 and unmoved is not None:
            pieces.append(unmoved[frames])
        else:
            pieces.append(fetch(piece, source, target, move))
    return pieces[0] if len(pieces) == 1 else jnp.concatenate(pieces)


def pair_step_of(own_frames, distance):
    step, rest = divmod(distance, own_frames)
    frame_parts = lax.axis_size("frame")
    return step if rest == 0 and frame_parts <= 2 * step < 2 * frame_parts else 0


def triple_from(block, source, target, distance, staged):
    own_frames = block.shape[0]
    frame_parts = lax.axis_size("frame")
    own = fetch(block, source, target, 0)
    if distance >= frame_parts * own_frames:
        return [own]
    step = pair_step_of(own_frames, distance)
    if step:
        route = [
            (source * frame_parts + z + move, target * frame_parts + z)
            for z in range(frame_parts)
            for move in (step, -step)
            if 0 <= z + move < frame_parts
        ]
        return [own, lax.ppermute(block, ("section", "frame"), route)]
    if staged:
        block, source = own, target
    return [
        own,
        shifted_from(block, source, target, distance, own),
        shifted_from(block, source, target, -distance, own),
    ]


def by_pairs(axis):
    count = lax.axis_size(axis)
    return count <= 4 and count & (count - 1) == 0


def sum_over(values, axis):
    count = lax.axis_size(axis)
    if by_pairs(axis):
        index = lax.axis_index(axis)
        size = values.shape[0] // count
        total = lax.dynamic_slice_in_dim(values, index * size, size, 0)
        for mask in range(1, count):
            part = lax.dynamic_slice_in_dim(values, (index ^ mask) * size, size, 0)
            got = lax.ppermute(
                part.astype(jnp.bfloat16), axis, [(i, i ^ mask) for i in range(count)]
            )
            total += got.astype(jnp.float32)
        return total
    parts = values.astype(jnp.bfloat16).reshape((count, -1) + values.shape[1:])
    parts = lax.all_to_all(parts, axis, split_axis=0, concat_axis=0, tiled=True)
    return jnp.sum(parts.astype(jnp.float32), axis=0)


def gather_parts(part, axis):
    if not by_pairs(axis):
        return lax.all_gather(part, axis, axis=0, tiled=True)
    count = lax.axis_size(axis)
    index = lax.axis_index(axis)
    size = part.shape[0]
    whole = jnp.zeros((count * size,) + part.shape[1:], part.dtype)
    whole = lax.dynamic_update_slice_in_dim(whole, part, index * size, 0)
    for mask in range(1, count):
        got = lax.ppermute(part, axis, [(i, i ^ mask) for i in range(count)])
        whole = lax.dynamic_update_slice_in_dim(whole, got, (index ^ mask) * size, 0)
    return whole


def after(values, *others):
    return list(lax.optimization_barrier((tuple(values), others))[0])


def section_run(chains, x_saved, cotangent, w_spatial, w_temporal):
    block_input = x_saved[0]
    taps_space = w_spatial[0]
    taps_time = w_temporal[0]
    own_frames, row_count, col_count, channels = block_input.shape
    section_count = lax.axis_size("section")
    section_index = lax.axis_index("section")
    row_parts = lax.axis_size("row")
    if own_frames % 2:
        chains = 1
    top = section_count - 1

    def triples(blocks, source, target):
        dilation = 2**target
        if chains == 1:
            return [triple_from(blocks[0], source, target, dilation, False)]
        if dilation % 2 == 0:
            return [triple_from(block, source, target, dilation // 2, STAGED) for block in blocks]
        even, odd = blocks
        own_even = fetch(even, source, target, 0)
        next_even = shifted_from(even, source, target, (dilation + 1) // 2, own_even)
        own_odd = fetch(odd, source, target, 0)
        last_odd = shifted_from(odd, source, target, -((dilation + 1) // 2), own_odd)
        same_odd = shifted_from(odd, source, target, (dilation - 1) // 2, own_odd)
        same_even = shifted_from(even, source, target, -((dilation - 1) // 2), own_even)
        return [[own_even, same_odd, last_odd], [own_odd, next_even, same_even]]

    def pair_step(target):
        dilation = 2**target
        if dilation % chains:
            return 0
        return pair_step_of(own_frames // chains, dilation // chains)

    x_got = swap_edges(edges_of(block_input, row_parts))
    slopes, actives = forward(block_input, x_got, taps_space, chains)
    ready = triples(split_frames(cotangent, chains), top, top)
    grads = None
    results = []
    for position in range(section_count):
        owner = top - position
        last = owner == 0
        groups = [list(range(chains))] if last else [[chain] for chain in range(chains)]
        pre, outgoing = [], []
        for group in groups:
            mine = [ready[chain] for chain in group]
            if outgoing:
                mine = [after(triple, *outgoing) for triple in mine]
            elif results:
                mine = [after(triple, *results[-1]) for triple in mine]
            group_pre, edges = temporal(
                owner, mine, pair_step(owner), [slopes[chain] for chain in group], taps_time
            )
            pre += group_pre
            if last:
                break
            got = swap_edges(edges)
            outgoing += branches(owner, group_pre, got, [t[0] for t in mine], taps_space)
        inputs = pre if last else after(pre, *outgoing)
        grads = kernel_grads(
            owner, block_input, x_got, inputs, actives, ready, pair_step(owner), grads
        )
        if not last:
            results.append(outgoing)
            ready = triples(outgoing, owner, owner - 1)

    total = sum_over(grads.reshape(-1, channels), "row")
    edges = after(edges, total)
    got = swap_edges(edges)
    outgoing = branches(0, pre, got, [t[0] for t in ready], taps_space)
    results.append(outgoing)
    total = sum_over(total, "frame").astype(jnp.bfloat16)
    total = gather_parts(total, "frame")
    split = 9 * channels
    if row_parts == 2:
        first = lax.axis_index("row") == 0
        other = lax.ppermute(total, "row", [(0, 1), (1, 0)])
        rest = split - total.shape[0]
        space = jnp.where(
            first,
            jnp.concatenate([total, other[:rest]]),
            jnp.concatenate([other, total[:rest]]),
        )
        time = jnp.where(first, other[rest:], total[rest:])
    else:
        total = gather_parts(total, "row")
        space, time = total[:split], total[split:]
    own = results[0]
    for position in range(1, section_count):
        own = [
            jnp.where(section_index == top - position, new, old)
            for new, old in zip(results[position], own)
        ]
    own = jnp.stack(own, 1).reshape(block_input.shape)
    return (
        own[None],
        space.astype(jnp.float32).reshape((1, 3, 3, channels, channels)),
        time.astype(jnp.float32).reshape((1, 3, channels, channels)),
    )


CHAINS = 2
STAGED = False


def solution(mesh):
    return jax.shard_map(
        functools.partial(section_run, CHAINS),
        mesh=mesh,
        in_specs=(
            P("section", "frame", "row", None, None),
            P("frame", "row", None, None),
            P("section", None, None, None, None),
            P("section", None, None, None),
        ),
        out_specs=(
            P("section", "frame", "row", None, None),
            P("section", None, None, None, None),
            P("section", None, None, None),
        ),
        check_vma=False,
    )
```

```python
import jax
import jax.numpy as jnp
from jax import lax
from jax.experimental import pallas as pl
from jax.experimental.pallas import tpu as pltpu
from jax.sharding import PartitionSpec as P

VMEM_LIMIT = 40 * 1024 * 1024
NT = (((1,), (1,)), ((), ()))
NN = (((1,), (0,)), ((), ()))
TN = (((0,), (0,)), ((), ()))


def mul(a, b, how):
    return lax.dot_general(a, b, how, preferred_element_type=jnp.float32)


def call(body, outs, args, flops):
    moved = sum(a.size * a.dtype.itemsize for a in (*args, *outs))
    return pl.pallas_call(
        body,
        out_shape=outs,
        in_specs=[pl.BlockSpec(memory_space=pltpu.VMEM) for _ in args],
        out_specs=[pl.BlockSpec(memory_space=pltpu.VMEM) for _ in outs],
        compiler_params=pltpu.CompilerParams(vmem_limit_bytes=VMEM_LIMIT),
        cost_estimate=pl.CostEstimate(flops=flops, bytes_accessed=moved, transcendentals=0),
    )(*args)


def flat(values):
    return values.reshape(-1, values.shape[-1])


def row_sides(got, row_count):
    if len(got) == 1:
        first = (lax.axis_index("row") == 0).astype(jnp.float32)
        rows = got[0].astype(jnp.float32)
        return (rows * (1.0 - first)).astype(jnp.bfloat16), (rows * first).astype(jnp.bfloat16)
    return got


def moved_rows(cells, above, below):
    return (
        flat(jnp.concatenate([above, cells[:, :-1]], axis=1)),
        flat(cells),
        flat(jnp.concatenate([cells[:, 1:], below], axis=1)),
    )


def moved_cols(values, step, col_count):
    count, lanes = values.shape
    shape = (count // col_count, col_count, lanes)
    col = lax.broadcasted_iota(jnp.int32, shape, 1).reshape(count, lanes)
    if step == 1:
        return jnp.where(col == col_count - 1, 0.0, pltpu.roll(values, count - 1, 0))
    return jnp.where(col == 0, 0.0, pltpu.roll(values, 1, 0))


def edges_of(cells, row_parts):
    head, tail = cells[:, :1], cells[:, -1:]
    if row_parts == 2:
        first = (lax.axis_index("row") == 0).astype(jnp.float32)
        return [(tail.astype(jnp.float32) * first + head.astype(jnp.float32) * (1.0 - first)).astype(jnp.bfloat16)]
    return [head, tail]


def swap_edges(edges):
    count = lax.axis_size("row")
    if count == 2:
        return [lax.ppermute(edges[0], "row", [(0, 1), (1, 0)])]
    head, tail = edges
    if count == 1:
        return [jnp.zeros_like(head), jnp.zeros_like(head)]
    return [
        lax.ppermute(tail, "row", [(i, i + 1) for i in range(count - 1)]),
        lax.ppermute(head, "row", [(i + 1, i) for i in range(count - 1)]),
    ]


def split_frames(values, chains):
    if chains == 1:
        return [values]
    pairs = values.reshape((values.shape[0] // chains, chains) + values.shape[1:])
    return [pairs[:, at] for at in range(chains)]


def windows(cells, rows):
    return jnp.concatenate([flat(cells[:, i : i + rows]) for i in range(3)], axis=1)


def is_one_of(section, sections):
    found = section == sections[0]
    for other in sections[1:]:
        found |= section == other
    return found


def forward(block_input, got, taps_space, chains, sections, dealt=()):
    frames, rows, cols, channels = block_input.shape
    part = (frames // chains, rows, cols, channels)
    args = list(dealt) or [block_input, *got]

    def body(*refs):
        section = lax.axis_index("section")
        pl.when(is_one_of(section, sections))(lambda: work(section, *refs))

    def work(section, *refs):
        w_ref, x_ref = refs[len(args) : len(args) + 2]
        slope_refs = refs[len(args) + 2 : len(args) + 2 + chains]
        active_refs = refs[len(args) + 2 + chains :]
        if dealt:
            first = jnp.where(section == 1, lax.axis_index("frame") % 2, 0)
            x_ref[first] = refs[0][0]
            x_ref[1 - first] = refs[1][0]
        else:
            above, below = row_sides([ref[...] for ref in refs[1 : len(args)]], rows)
            x_ref[...] = jnp.concatenate([above, refs[0][...], below], axis=1)
        taps = jnp.concatenate(
            [jnp.concatenate([w_ref[i, j] for j in range(3)], axis=1) for i in range(3)], axis=0
        )
        sums = mul(windows(x_ref[...], rows), taps, NN)
        pre_act = (
            moved_cols(sums[:, :channels], -1, cols)
            + sums[:, channels : 2 * channels]
            + moved_cols(sums[:, 2 * channels :], 1, cols)
        )
        sigma = jax.nn.sigmoid(pre_act)
        slope = (sigma * (1.0 + pre_act * (1.0 - sigma))).reshape(block_input.shape)
        active = (pre_act * sigma).astype(jnp.bfloat16).reshape(block_input.shape)
        for ref, values in zip(slope_refs, split_frames(slope, chains)):
            ref[...] = values
        for ref, values in zip(active_refs, split_frames(active, chains)):
            ref[...] = values

    outs = [jax.ShapeDtypeStruct((frames, rows + 2, cols, channels), jnp.bfloat16)]
    outs += [jax.ShapeDtypeStruct(part, jnp.float32)] * chains
    outs += [jax.ShapeDtypeStruct(part, jnp.bfloat16)] * chains
    outs = call(body, outs, [*args, taps_space], 18 * block_input.size * channels)
    return outs[0], outs[1 : 1 + chains], outs[1 + chains :]


def early_half(distance_step):
    return lambda: (lax.axis_index("frame") < lax.axis_size("frame") - distance_step).astype(
        jnp.float32
    )


def mixed(early, later, earlier):
    return early * later.astype(jnp.float32) + (1.0 - early) * earlier.astype(jnp.float32)


def temporal(owner, triples, slopes, taps_time):
    row_parts = lax.axis_size("row")
    part = slopes[0].shape
    channels = part[-1]
    edges = 1 if row_parts == 2 else 2
    sizes = [len(blocks) for blocks, _ in triples]

    def body(*refs):
        @pl.when(lax.axis_index("section") == owner)
        def _():
            at = 0
            w_ref = refs[sum(sizes) + len(slopes)]
            outs = refs[sum(sizes) + len(slopes) + 1 :]
            for chain, size in enumerate(sizes):
                blocks = [flat(ref[...]) for ref in refs[at : at + size]]
                at += size
                taps = [w_ref[1]]
                early = triples[chain][1]
                if size > 1 and early is None:
                    taps += [w_ref[0], w_ref[2]]
                elif size > 1:
                    taps.append(mixed(early(), w_ref[0], w_ref[2]).astype(jnp.bfloat16))
                    taps.append(mixed(early(), w_ref[2], w_ref[0]).astype(jnp.bfloat16))
                taps = taps[:size]
                sums = mul(jnp.concatenate(blocks, axis=1), jnp.concatenate(taps, axis=1), NT)
                back_act = sums.astype(jnp.bfloat16).astype(jnp.float32)
                slope = flat(refs[sum(sizes) + chain][...])
                grad_pre = (back_act * slope).astype(jnp.bfloat16).reshape(part)
                outs[chain][...] = grad_pre
                for ref, edge in zip(outs[len(slopes) :], edges_of(grad_pre, row_parts)):
                    ref[chain * part[0] : (chain + 1) * part[0]] = edge

    outs = [jax.ShapeDtypeStruct(part, jnp.bfloat16)] * len(slopes)
    outs += [
        jax.ShapeDtypeStruct((part[0] * len(slopes), 1) + part[2:], jnp.bfloat16)
    ] * edges
    args = [block for blocks, _ in triples for block in blocks] + list(slopes) + [taps_time]
    outs = call(body, outs, args, 6 * sum(s.size for s in slopes) * channels)
    return outs[: len(slopes)], outs[len(slopes) :]


def branches(owner, grads_pre, got, heres, taps_space, picks=None, before=()):
    part = heres[0].shape
    _, rows, cols, channels = part
    count = len(heres)
    picks = picks or list(range(count))
    fixed = 2 * count + len(got) + 1

    def body(*refs):
        section = lax.axis_index("section")
        out_refs = refs[fixed + len(before) :]

        if before:

            @pl.when(section != owner)
            def _():
                for ref, out_ref in zip(refs[fixed:], out_refs[-len(before) :]):
                    out_ref[...] = ref[...]

        @pl.when(section == owner)
        def _():
            got_refs = refs[count : count + len(got)]
            here_refs = refs[count + len(got) : 2 * count + len(got)]
            w_ref = refs[2 * count + len(got)]
            taps = jnp.concatenate(
                [jnp.concatenate([w_ref[2 - i, j] for i in range(3)], axis=1) for j in range(3)],
                axis=0,
            )
            for chain in range(count):
                frames = slice(chain * part[0], (chain + 1) * part[0])
                above, below = row_sides([ref[frames] for ref in got_refs], rows)
                sides = jnp.concatenate(moved_rows(refs[chain][...], above, below), axis=1)
                sums = mul(sides, taps, NT)
                branch = (
                    moved_cols(sums[:, :channels], 1, cols)
                    + sums[:, channels : 2 * channels]
                    + moved_cols(sums[:, 2 * channels :], -1, cols)
                )
                branch = branch.astype(jnp.bfloat16).astype(jnp.float32)
                here = flat(here_refs[chain][...]).astype(jnp.float32)
                out = (here + branch).astype(jnp.bfloat16).reshape(part)
                for ref, pick in zip(out_refs, picks):
                    if callable(pick):
                        wanted = pick() if chain == 0 else jnp.logical_not(pick())
                        pl.when(wanted)(lambda ref=ref, out=out: ref.__setitem__(..., out))
                    elif pick == chain:
                        ref[...] = out

    outs = [jax.ShapeDtypeStruct(part, jnp.bfloat16)] * len(picks)
    args = [*grads_pre, *got, *heres, taps_space, *before]
    return call(body, outs, args, 18 * sum(h.size for h in heres) * channels)


def kernel_grads(owner, x_rows, grads_pre, actives, triples, before):
    _, rows, cols, channels = x_rows.shape
    rows -= 2
    chains = len(actives)

    def body(*refs):
        section = lax.axis_index("section")
        out_ref = refs[-1]

        if before is not None:

            @pl.when(section != owner)
            def _():
                out_ref[...] = refs[-2][...]

        @pl.when(section == owner)
        def _():
            sides = [windows(cells, rows) for cells in split_frames(refs[0][...], chains)]
            pre = []
            time = [jnp.zeros((channels, channels), jnp.float32)] * 3
            at = 1 + 2 * chains
            for chain, (blocks, early) in enumerate(triples):
                mid = flat(refs[1 + chain][...])
                wide = mid.astype(jnp.float32)
                left = moved_cols(wide, 1, cols).astype(jnp.bfloat16)
                right = moved_cols(wide, -1, cols).astype(jnp.bfloat16)
                pre.append(jnp.concatenate([left, mid, right], axis=1))
                size = len(blocks)
                values = jnp.concatenate([flat(ref[...]) for ref in refs[at : at + size]], axis=1)
                at += size
                product = mul(flat(refs[1 + chains + chain][...]), values, TN)
                terms = [product[:, k * channels : (k + 1) * channels] for k in range(size)]
                time[1] = time[1] + terms[0]
                if size > 1 and early is None:
                    time[0] = time[0] + terms[1]
                    time[2] = time[2] + terms[2]
                elif size > 1:
                    share = early()
                    other = terms[2] if size == 3 else jnp.zeros_like(terms[1])
                    time[0] = time[0] + mixed(share, terms[1], other)
                    time[2] = time[2] + mixed(share, other, terms[1])
            space = mul(jnp.concatenate(sides), jnp.concatenate(pre), TN)
            for i in range(3):
                for j in range(3):
                    out_ref[3 * i + j] = space[
                        i * channels : (i + 1) * channels, j * channels : (j + 1) * channels
                    ]
            for k in range(3):
                out_ref[9 + k] = time[k]

    args = [x_rows, *grads_pre, *actives]
    args += [block for blocks, _ in triples for block in blocks]
    if before is not None:
        args.append(before)
    outs = [jax.ShapeDtypeStruct((12, channels, channels), jnp.float32)]
    return call(body, outs, args, 24 * x_rows.size * channels)[0]


def place_first(section):
    place = lax.axis_index("frame")
    return jnp.where(section == 2, place // 2, jnp.where((place == 0) | (place == 3), 1, 0))


def frames_to_deal(block_input, got):
    _, rows, cols, channels = block_input.shape

    def body(*refs):
        section = lax.axis_index("section")

        @pl.when(is_one_of(section, (1, 2)))
        def _():
            above, below = row_sides([ref[...] for ref in refs[1 : 1 + len(got)]], rows)
            cells = jnp.concatenate([above, refs[0][...], below], axis=1)
            first = place_first(section)
            for frame in range(2):

                @pl.when(first == frame)
                def _():
                    refs[-2][...] = cells[frame : frame + 1]
                    refs[-1][...] = cells[1 - frame : 2 - frame]

    outs = [jax.ShapeDtypeStruct((1, rows + 2, cols, channels), jnp.bfloat16)] * 2
    return call(body, outs, [block_input, *got], 0)


def line_up(pieces):
    table = ((None, 0, 1, 2), (0, 3, 2, 4), (3, 2, 4, 0), (2, 1, 0, None))

    def body(*refs):
        for place, order in enumerate(table):

            @pl.when((lax.axis_index("section") == 0) & (lax.axis_index("frame") == place))
            def _():
                for ref, at in zip(refs[len(pieces) :], order):
                    ref[...] = jnp.zeros(ref.shape, ref.dtype) if at is None else refs[at][...]

    return call(body, [jax.ShapeDtypeStruct(pieces[0].shape, jnp.bfloat16)] * 4, pieces, 0)


def own_result(tops, returned, lasts):
    shape = (2,) + lasts[0].shape[1:]

    def body(*refs):
        section = lax.axis_index("section")
        place = lax.axis_index("frame")
        out_ref = refs[-1]

        @pl.when(section == 3)
        def _():
            out_ref[place // 2] = refs[0][0]
            out_ref[1 - place // 2] = refs[1][0]

        @pl.when(is_one_of(section, (1, 2)))
        def _():
            first = place_first(section)
            out_ref[first] = refs[2][0]
            out_ref[1 - first] = refs[3][0]

        @pl.when(section == 0)
        def _():
            out_ref[0] = refs[4][0]
            out_ref[1] = refs[5][0]

    outs = [jax.ShapeDtypeStruct(shape, jnp.bfloat16)]
    return call(body, outs, [*tops, *returned, *lasts], 0)[0]


def fetch(block, source, target, frame_step):
    frame_parts = lax.axis_size("frame")
    route = [
        (source * frame_parts + z + frame_step, target * frame_parts + z)
        for z in range(frame_parts)
        if 0 <= z + frame_step < frame_parts
    ]
    if not route:
        return jnp.zeros_like(block)
    if source == target and frame_step == 0:
        return block
    return lax.ppermute(block, ("section", "frame"), route)


def shifted_from(block, source, target, offset, unmoved=None):
    own_frames = block.shape[0]
    step, rest = divmod(offset, own_frames)
    pieces = []
    for frames, move in ((slice(rest, None), step), (slice(0, rest), step + 1)):
        piece = block[frames]
        if piece.shape[0] == 0:
            continue
        if move == 0 and unmoved is not None:
            pieces.append(unmoved[frames])
        else:
            pieces.append(fetch(piece, source, target, move))
    return pieces[0] if len(pieces) == 1 else jnp.concatenate(pieces)


def pair_step_of(own_frames, distance):
    step, rest = divmod(distance, own_frames)
    frame_parts = lax.axis_size("frame")
    return step if rest == 0 and frame_parts <= 2 * step < 2 * frame_parts else 0


def triple_from(block, source, target, distance, staged):
    own_frames = block.shape[0]
    frame_parts = lax.axis_size("frame")
    own = fetch(block, source, target, 0)
    if distance >= frame_parts * own_frames:
        return [own]
    step = pair_step_of(own_frames, distance)
    if step:
        route = [
            (source * frame_parts + z + move, target * frame_parts + z)
            for z in range(frame_parts)
            for move in (step, -step)
            if 0 <= z + move < frame_parts
        ]
        return [own, lax.ppermute(block, ("section", "frame"), route)]
    if staged:
        block, source = own, target
    return [
        own,
        shifted_from(block, source, target, distance, own),
        shifted_from(block, source, target, -distance, own),
    ]


def by_pairs(axis):
    count = lax.axis_size(axis)
    return count <= 4 and count & (count - 1) == 0


def sum_over(values, axis, beside=None):
    count = lax.axis_size(axis)
    index = lax.axis_index(axis)
    if not by_pairs(axis):
        parts = values.astype(jnp.bfloat16).reshape((count, -1) + values.shape[1:])
        parts = lax.all_to_all(parts, axis, split_axis=0, concat_axis=0, tiled=True)
        return jnp.sum(parts.astype(jnp.float32), axis=0), beside and beside(values)
    size = values.shape[0] // count
    total = lax.dynamic_slice_in_dim(values, index * size, size, 0)
    parts = [
        lax.dynamic_slice_in_dim(values, (index ^ mask) * size, size, 0).astype(jnp.bfloat16)
        for mask in range(1, count)
    ]
    other = beside and beside(parts)
    parts = [
        lax.ppermute(part, axis, [(i, i ^ mask) for i in range(count)])
        for mask, part in enumerate(parts, 1)
    ]
    if beside:
        parts = after(parts, other)
    for part in parts:
        total += part.astype(jnp.float32)
    return total, other


def gather_parts(part, axis):
    if not by_pairs(axis):
        return lax.all_gather(part, axis, axis=0, tiled=True)
    count = lax.axis_size(axis)
    index = lax.axis_index(axis)
    size = part.shape[0]
    whole = jnp.zeros((count * size,) + part.shape[1:], part.dtype)
    whole = lax.dynamic_update_slice_in_dim(whole, part, index * size, 0)
    for mask in range(1, count):
        got = lax.ppermute(part, axis, [(i, i ^ mask) for i in range(count)])
        whole = lax.dynamic_update_slice_in_dim(whole, got, (index ^ mask) * size, 0)
    return whole


def after(values, *others):
    return list(lax.optimization_barrier((tuple(values), others))[0])


def shifted_chains(x_got, block_input, cotangent, taps_space, taps_time):
    own_frames = block_input.shape[0]
    section_count = lax.axis_size("section")
    chains = 1 if own_frames % 2 else 2
    top = section_count - 1

    def triples(blocks, source, target):
        dilation = 2**target
        if dilation % chains == 0:
            step = pair_step_of(own_frames // chains, dilation // chains)
            early = early_half(step) if step else None
            return [
                (triple_from(block, source, target, dilation // chains, False), early)
                for block in blocks
            ]
        even, odd = blocks
        own_even = fetch(even, source, target, 0)
        next_even = shifted_from(even, source, target, (dilation + 1) // 2, own_even)
        own_odd = fetch(odd, source, target, 0)
        last_odd = shifted_from(odd, source, target, -((dilation + 1) // 2), own_odd)
        same_odd = shifted_from(odd, source, target, (dilation - 1) // 2, own_odd)
        same_even = shifted_from(even, source, target, -((dilation - 1) // 2), own_even)
        return [([own_even, same_odd, last_odd], None), ([own_odd, next_even, same_even], None)]

    everywhere = tuple(range(section_count))
    x_rows, slopes, actives = forward(block_input, x_got, taps_space, chains, everywhere)
    ready = triples(split_frames(cotangent, chains), top, top)
    grads = None
    results = []
    for owner in reversed(range(section_count)):
        groups = [[chain] for chain in range(chains)] if owner else [list(range(chains))]
        pre, outgoing = [], []
        for group in groups:
            mine = [ready[chain] for chain in group]
            if outgoing or results:
                earlier = outgoing or results[-1]
                mine = [(after(blocks, *earlier), early) for blocks, early in mine]
            group_pre, edges = temporal(owner, mine, [slopes[chain] for chain in group], taps_time)
            pre += group_pre
            if owner:
                heres = [blocks[0] for blocks, _ in mine]
                got = swap_edges(edges)
                outgoing += branches(owner, group_pre, got, heres, taps_space)
        inputs = after(pre, *outgoing) if owner else pre
        grads = kernel_grads(owner, x_rows, inputs, actives, ready, grads)
        if owner:
            results.append(outgoing)
            ready = triples(outgoing, owner, owner - 1)

    def finish(lasts):
        section_index = lax.axis_index("section")
        own = results[0] if results else lasts
        for position, values in enumerate((results + [lasts])[1:], 1):
            own = [
                jnp.where(section_index == top - position, new, old)
                for new, old in zip(values, own)
            ]
        return jnp.stack(own, 1).reshape(block_input.shape)

    return grads, (pre, edges, [blocks[0] for blocks, _ in ready]), finish


def dealt_chains(x_got, block_input, cotangent, taps_space, taps_time):
    def place():
        return lax.axis_index("frame")

    def even():
        return (place() % 2 == 0).astype(jnp.float32)

    def odd():
        return (place() % 2).astype(jnp.float32)

    def low():
        return (place() < 2).astype(jnp.float32)

    def outer():
        return (place() == 0) | (place() == 3)

    def send(block, *hops):
        route = [(a * 4 + i, b * 4 + j) for a, b, moves in hops for i, j in moves]
        return lax.ppermute(block, ("section", "frame"), route)

    def back(moves):
        return [(j, i) for i, j in moves]

    stay = [(i, i) for i in range(4)]
    deal = {
        2: ([(0, 0), (1, 2), (2, 1), (3, 3)], [(0, 1), (1, 3), (2, 0), (3, 2)]),
        1: ([(0, 1), (1, 0), (2, 2), (3, 3)], [(0, 0), (1, 1), (2, 3), (3, 2)]),
    }
    x_dealt = [
        send(block, *((s, s, deal[s][k]) for s in (1, 2)))
        for k, block in enumerate(frames_to_deal(block_input, x_got))
    ]

    def step(owner, triples, slopes, picks, before=()):
        pre, edges = temporal(owner, triples, slopes, taps_time)
        heres = [blocks[0] for blocks, _ in triples]
        outs = branches(owner, pre, swap_edges(edges), heres, taps_space, picks, before)
        return after(pre, *outs), outs

    x_own, slopes_own, actives_own = forward(block_input, x_got, taps_space, 2, (0, 3))
    ready = [([block], None) for block in split_frames(cotangent, 2)]
    pre, tops = step(
        3, ready, slopes_own, [lambda: place() < 2, lambda: place() >= 2]
    )
    first, second = (send(block, (3, 2, deal[2][k])) for k, block in enumerate(tops))
    grads = kernel_grads(3, x_own, pre, actives_own, ready, None)
    x_moved, slopes, actives = forward(
        block_input, x_got, taps_space, 2, (1, 2), after(x_dealt, *tops)
    )

    ready = [([first, second], even), ([second, first], odd)]
    pre, outs = step(2, ready, slopes, [outer, lambda: jnp.logical_not(outer()), 0, 1])
    ends, others, *returned = outs
    end = send(ends, (2, 1, stay))
    other = send(others, (2, 1, stay))
    cross = send(others, (2, 1, [(i, i ^ 2) for i in range(4)]))
    grads = kernel_grads(2, x_moved, pre, actives, ready, grads)

    ready = [([cross, other, end], low), ([end, cross], low)]
    pre, outs = step(
        1, ready, slopes, [0, 1, lambda: place() % 2 == 0, lambda: place() % 2 == 1], returned
    )
    middles, ends, *returned = outs
    pieces = [
        send(ends, (1, 0, stay)),
        send(ends, (1, 0, [(1, 0), (2, 3)])),
        send(middles, (1, 0, stay)),
        send(middles, (1, 0, [(0, 1), (1, 2)])),
        send(middles, (1, 0, [(2, 1), (3, 2)])),
    ]
    grads = kernel_grads(1, x_moved, pre, actives, ready, grads)
    before, one, two, later = line_up(pieces)
    ready = [([one, two, before], None), ([two, later, one], None)]
    pre, edges = temporal(0, ready, slopes_own, taps_time)
    grads = kernel_grads(0, x_own, pre, actives_own, ready, grads)
    returned = [
        send(block, *((s, s, back(deal[s][k])) for s in (1, 2)))
        for k, block in enumerate(returned)
    ]

    def finish(lasts):
        return own_result(tops, returned, lasts)

    return grads, (pre, edges, [one, two]), finish


def section_run(x_saved, cotangent, w_spatial, w_temporal):
    block_input = x_saved[0]
    taps_space = w_spatial[0]
    taps_time = w_temporal[0]
    channels = block_input.shape[-1]
    row_parts = lax.axis_size("row")
    x_got = swap_edges(edges_of(block_input, row_parts))
    shape = (lax.axis_size("section"), lax.axis_size("frame"), block_input.shape[0])
    chains = dealt_chains if shape == (4, 4, 2) else shifted_chains
    grads, (pre, edges, heres), finish = chains(
        x_got, block_input, cotangent, taps_space, taps_time
    )
    total, _ = sum_over(grads.reshape(-1, channels), "row")

    def last_branch(parts):
        return branches(0, pre, swap_edges(after(edges, parts)), heres, taps_space)

    total, lasts = sum_over(total, "frame", last_branch)
    total = gather_parts(total.astype(jnp.bfloat16), "frame")
    split = 9 * channels
    if row_parts == 2:
        first = lax.axis_index("row") == 0
        other = lax.ppermute(total, "row", [(0, 1), (1, 0)])
        rest = split - total.shape[0]
        space = jnp.where(
            first,
            jnp.concatenate([total, other[:rest]]),
            jnp.concatenate([other, total[:rest]]),
        )
        time = jnp.where(first, other[rest:], total[rest:])
    else:
        total = gather_parts(total, "row")
        space, time = total[:split], total[split:]
    return (
        finish(lasts)[None],
        space.astype(jnp.float32).reshape((1, 3, 3, channels, channels)),
        time.astype(jnp.float32).reshape((1, 3, channels, channels)),
    )


def solution(mesh):
    return jax.shard_map(
        section_run,
        mesh=mesh,
        in_specs=(
            P("section", "frame", "row", None, None),
            P("frame", "row", None, None),
            P("section", None, None, None, None),
            P("section", None, None, None),
        ),
        out_specs=(
            P("section", "frame", "row", None, None),
            P("section", None, None, None, None),
            P("section", None, None, None),
        ),
        check_vma=False,
    )
```

```python
import jax
import jax.numpy as jnp
from jax import lax
from jax.experimental import pallas as pl
from jax.experimental.pallas import tpu as pltpu
from jax.sharding import PartitionSpec as P

VMEM_LIMIT = 16 * 1024 * 1024
NT = (((1,), (1,)), ((), ()))
NN = (((1,), (0,)), ((), ()))
TN = (((0,), (0,)), ((), ()))


def mul(a, b, how):
    return lax.dot_general(a, b, how, preferred_element_type=jnp.float32)


def call(body, outs, args, flops, loose=False):
    moved = sum(a.size * a.dtype.itemsize for a in (*args, *outs))
    return pl.pallas_call(
        body,
        out_shape=outs,
        in_specs=[pl.BlockSpec() if loose else pl.BlockSpec(memory_space=pltpu.VMEM) for _ in args],
        out_specs=[pl.BlockSpec(memory_space=pltpu.VMEM) for _ in outs],
        compiler_params=pltpu.CompilerParams(vmem_limit_bytes=VMEM_LIMIT),
        cost_estimate=pl.CostEstimate(flops=flops, bytes_accessed=moved, transcendentals=0),
    )(*args)


def flat(values):
    return values.reshape(-1, values.shape[-1])


def row_sides(got, row_count):
    if len(got) == 1:
        first = (lax.axis_index("row") == 0).astype(jnp.float32)
        rows = got[0].astype(jnp.float32)
        return (rows * (1.0 - first)).astype(jnp.bfloat16), (rows * first).astype(jnp.bfloat16)
    return got


def moved_rows(cells, above, below):
    return (
        flat(jnp.concatenate([above, cells[:, :-1]], axis=1)),
        flat(cells),
        flat(jnp.concatenate([cells[:, 1:], below], axis=1)),
    )


def moved_cols(values, step, col_count):
    count, lanes = values.shape
    shape = (count // col_count, col_count, lanes)
    col = lax.broadcasted_iota(jnp.int32, shape, 1).reshape(count, lanes)
    if step == 1:
        return jnp.where(col == col_count - 1, 0.0, pltpu.roll(values, count - 1, 0))
    return jnp.where(col == 0, 0.0, pltpu.roll(values, 1, 0))


def edges_of(cells, row_parts):
    head, tail = cells[:, :1], cells[:, -1:]
    if row_parts == 2:
        first = (lax.axis_index("row") == 0).astype(jnp.float32)
        return [(tail.astype(jnp.float32) * first + head.astype(jnp.float32) * (1.0 - first)).astype(jnp.bfloat16)]
    return [head, tail]


def swap_edges(edges):
    count = lax.axis_size("row")
    if count == 2:
        return [lax.ppermute(edges[0], "row", [(0, 1), (1, 0)])]
    head, tail = edges
    if count == 1:
        return [jnp.zeros_like(head), jnp.zeros_like(head)]
    return [
        lax.ppermute(tail, "row", [(i, i + 1) for i in range(count - 1)]),
        lax.ppermute(head, "row", [(i + 1, i) for i in range(count - 1)]),
    ]


def split_frames(values, chains):
    if chains == 1:
        return [values]
    pairs = values.reshape((values.shape[0] // chains, chains) + values.shape[1:])
    return [pairs[:, at] for at in range(chains)]


def windows(cells, rows):
    return jnp.concatenate([flat(cells[:, i : i + rows]) for i in range(3)], axis=1)


def is_one_of(section, sections):
    found = section == sections[0]
    for other in sections[1:]:
        found |= section == other
    return found


def forward(block_input, got, taps_space, chains, sections, dealt=()):
    frames, rows, cols, channels = block_input.shape
    part = (frames // chains, rows, cols, channels)
    args = list(dealt) or [block_input, *got]

    def body(*refs):
        section = lax.axis_index("section")
        pl.when(is_one_of(section, sections))(lambda: work(section, *refs))

    def work(section, *refs):
        w_ref, x_ref = refs[len(args) : len(args) + 2]
        slope_refs = refs[len(args) + 2 : len(args) + 2 + chains]
        active_refs = refs[len(args) + 2 + chains :]
        if dealt:
            first = jnp.where(section == 1, lax.axis_index("frame") % 2, 0)
            x_ref[first] = refs[0][0]
            x_ref[1 - first] = refs[1][0]
        else:
            above, below = row_sides([ref[...] for ref in refs[1 : len(args)]], rows)
            x_ref[...] = jnp.concatenate([above, refs[0][...], below], axis=1)
        taps = jnp.concatenate(
            [jnp.concatenate([w_ref[i, j] for j in range(3)], axis=1) for i in range(3)], axis=0
        )
        sums = mul(windows(x_ref[...], rows), taps, NN)
        pre_act = (
            moved_cols(sums[:, :channels], -1, cols)
            + sums[:, channels : 2 * channels]
            + moved_cols(sums[:, 2 * channels :], 1, cols)
        )
        sigma = jax.nn.sigmoid(pre_act)
        slope = (sigma * (1.0 + pre_act * (1.0 - sigma))).reshape(block_input.shape)
        active = (pre_act * sigma).astype(jnp.bfloat16).reshape(block_input.shape)
        for ref, values in zip(slope_refs, split_frames(slope, chains)):
            ref[...] = values
        for ref, values in zip(active_refs, split_frames(active, chains)):
            ref[...] = values

    outs = [jax.ShapeDtypeStruct((frames, rows + 2, cols, channels), jnp.bfloat16)]
    outs += [jax.ShapeDtypeStruct(part, jnp.float32)] * chains
    outs += [jax.ShapeDtypeStruct(part, jnp.bfloat16)] * chains
    outs = call(body, outs, [*args, taps_space], 18 * block_input.size * channels)
    return outs[0], outs[1 : 1 + chains], outs[1 + chains :]


def early_half(distance_step):
    return lambda: (lax.axis_index("frame") < lax.axis_size("frame") - distance_step).astype(
        jnp.float32
    )


def mixed(early, later, earlier):
    return early * later.astype(jnp.float32) + (1.0 - early) * earlier.astype(jnp.float32)


def temporal(owner, triples, slopes, taps_time):
    row_parts = lax.axis_size("row")
    part = slopes[0].shape
    channels = part[-1]
    edges = 1 if row_parts == 2 else 2
    sizes = [len(blocks) for blocks, _ in triples]

    def body(*refs):
        @pl.when(lax.axis_index("section") == owner)
        def _():
            at = 0
            w_ref = refs[sum(sizes) + len(slopes)]
            outs = refs[sum(sizes) + len(slopes) + 1 :]
            for chain, size in enumerate(sizes):
                blocks = [flat(ref[...]) for ref in refs[at : at + size]]
                at += size
                taps = [w_ref[1]]
                early = triples[chain][1]
                if size > 1 and early is None:
                    taps += [w_ref[0], w_ref[2]]
                elif size > 1:
                    taps.append(mixed(early(), w_ref[0], w_ref[2]).astype(jnp.bfloat16))
                    taps.append(mixed(early(), w_ref[2], w_ref[0]).astype(jnp.bfloat16))
                taps = taps[:size]
                sums = mul(jnp.concatenate(blocks, axis=1), jnp.concatenate(taps, axis=1), NT)
                back_act = sums.astype(jnp.bfloat16).astype(jnp.float32)
                slope = flat(refs[sum(sizes) + chain][...])
                grad_pre = (back_act * slope).astype(jnp.bfloat16).reshape(part)
                outs[chain][...] = grad_pre
                for ref, edge in zip(outs[len(slopes) :], edges_of(grad_pre, row_parts)):
                    ref[chain * part[0] : (chain + 1) * part[0]] = edge

    outs = [jax.ShapeDtypeStruct(part, jnp.bfloat16)] * len(slopes)
    outs += [
        jax.ShapeDtypeStruct((part[0] * len(slopes), 1) + part[2:], jnp.bfloat16)
    ] * edges
    args = [block for blocks, _ in triples for block in blocks] + list(slopes) + [taps_time]
    outs = call(body, outs, args, 6 * sum(s.size for s in slopes) * channels)
    return outs[: len(slopes)], outs[len(slopes) :]


def branches(owner, grads_pre, got, heres, taps_space, picks=None):
    part = heres[0].shape
    _, rows, cols, channels = part
    count = len(heres)
    picks = picks or list(range(count))

    def body(*refs):
        @pl.when(lax.axis_index("section") == owner)
        def _():
            out_refs = refs[2 * count + len(got) + 1 :]
            got_refs = refs[count : count + len(got)]
            here_refs = refs[count + len(got) : 2 * count + len(got)]
            w_ref = refs[2 * count + len(got)]
            taps = jnp.concatenate(
                [jnp.concatenate([w_ref[2 - i, j] for i in range(3)], axis=1) for j in range(3)],
                axis=0,
            )
            for chain in range(count):
                frames = slice(chain * part[0], (chain + 1) * part[0])
                above, below = row_sides([ref[frames] for ref in got_refs], rows)
                sides = jnp.concatenate(moved_rows(refs[chain][...], above, below), axis=1)
                sums = mul(sides, taps, NT)
                branch = (
                    moved_cols(sums[:, :channels], 1, cols)
                    + sums[:, channels : 2 * channels]
                    + moved_cols(sums[:, 2 * channels :], -1, cols)
                )
                branch = branch.astype(jnp.bfloat16).astype(jnp.float32)
                here = flat(here_refs[chain][...]).astype(jnp.float32)
                out = (here + branch).astype(jnp.bfloat16).reshape(part)
                for ref, pick in zip(out_refs, picks):
                    if callable(pick):
                        wanted = pick() if chain == 0 else jnp.logical_not(pick())
                        pl.when(wanted)(lambda ref=ref, out=out: ref.__setitem__(..., out))
                    elif pick == chain:
                        ref[...] = out

    outs = [jax.ShapeDtypeStruct(part, jnp.bfloat16)] * len(picks)
    args = [*grads_pre, *got, *heres, taps_space]
    return call(body, outs, args, 18 * sum(h.size for h in heres) * channels)


def kernel_grads(owner, x_rows, grads_pre, actives, triples, before):
    _, rows, cols, channels = x_rows.shape
    rows -= 2
    chains = len(actives)

    def body(*refs):
        section = lax.axis_index("section")
        out_ref = refs[-1]

        if before is not None:

            @pl.when(section != owner)
            def _():
                out_ref[...] = refs[-2][...]

        @pl.when(section == owner)
        def _():
            sides = [windows(cells, rows) for cells in split_frames(refs[0][...], chains)]
            pre = []
            time = [jnp.zeros((channels, channels), jnp.float32)] * 3
            at = 1 + 2 * chains
            for chain, (blocks, early) in enumerate(triples):
                mid = flat(refs[1 + chain][...])
                wide = mid.astype(jnp.float32)
                left = moved_cols(wide, 1, cols).astype(jnp.bfloat16)
                right = moved_cols(wide, -1, cols).astype(jnp.bfloat16)
                pre.append(jnp.concatenate([left, mid, right], axis=1))
                size = len(blocks)
                values = jnp.concatenate([flat(ref[...]) for ref in refs[at : at + size]], axis=1)
                at += size
                product = mul(flat(refs[1 + chains + chain][...]), values, TN)
                terms = [product[:, k * channels : (k + 1) * channels] for k in range(size)]
                time[1] = time[1] + terms[0]
                if size > 1 and early is None:
                    time[0] = time[0] + terms[1]
                    time[2] = time[2] + terms[2]
                elif size > 1:
                    share = early()
                    other = terms[2] if size == 3 else jnp.zeros_like(terms[1])
                    time[0] = time[0] + mixed(share, terms[1], other)
                    time[2] = time[2] + mixed(share, other, terms[1])
            space = mul(jnp.concatenate(sides), jnp.concatenate(pre), TN)
            for i in range(3):
                for j in range(3):
                    out_ref[3 * i + j] = space[
                        i * channels : (i + 1) * channels, j * channels : (j + 1) * channels
                    ]
            for k in range(3):
                out_ref[9 + k] = time[k]

    args = [x_rows, *grads_pre, *actives]
    args += [block for blocks, _ in triples for block in blocks]
    if before is not None:
        args.append(before)
    outs = [jax.ShapeDtypeStruct((12, channels, channels), jnp.float32)]
    return call(body, outs, args, 24 * x_rows.size * channels)[0]


def place_first(section):
    place = lax.axis_index("frame")
    return jnp.where(section == 2, place // 2, jnp.where((place == 0) | (place == 3), 1, 0))


def prepare(block_input):
    row_parts = lax.axis_size("row")
    frames, rows, cols, channels = block_input.shape
    edge_count = 1 if row_parts == 2 else 2

    def body(x_ref, *out_refs):
        for ref, edge in zip(out_refs, edges_of(x_ref[...], row_parts)):
            ref[...] = edge
        out_refs[edge_count][...] = x_ref[...]

    outs = [jax.ShapeDtypeStruct((frames, 1, cols, channels), jnp.bfloat16)] * edge_count
    outs += [jax.ShapeDtypeStruct(block_input.shape, jnp.bfloat16)]
    outs = call(body, outs, [block_input], 0)
    return outs[:edge_count], outs[edge_count]


def frame_by_frame(values):
    def body(ref, *out_refs):
        for frame, out_ref in enumerate(out_refs):
            out_ref[...] = ref[frame : frame + 1]

    out = jax.ShapeDtypeStruct((1,) + values.shape[1:], values.dtype)
    return call(body, [out] * values.shape[0], [values], 0)


def frames_to_deal(block_input, got):
    _, rows, cols, channels = block_input.shape

    def body(*refs):
        section = lax.axis_index("section")

        @pl.when(is_one_of(section, (1, 2)))
        def _():
            above, below = row_sides([ref[...] for ref in refs[1 : 1 + len(got)]], rows)
            cells = jnp.concatenate([above, refs[0][...], below], axis=1)
            first = place_first(section)
            for frame in range(2):

                @pl.when(first == frame)
                def _():
                    refs[-2][...] = cells[frame : frame + 1]
                    refs[-1][...] = cells[1 - frame : 2 - frame]

    outs = [jax.ShapeDtypeStruct((1, rows + 2, cols, channels), jnp.bfloat16)] * 2
    return call(body, outs, [block_input, *got], 0)


def line_up(pieces):
    table = ((None, 0, 1, 2), (0, 3, 2, 4), (3, 2, 4, 0), (2, 1, 0, None))

    def body(*refs):
        for place, order in enumerate(table):

            @pl.when((lax.axis_index("section") == 0) & (lax.axis_index("frame") == place))
            def _():
                for ref, at in zip(refs[len(pieces) :], order):
                    ref[...] = jnp.zeros(ref.shape, ref.dtype) if at is None else refs[at][...]

    return call(body, [jax.ShapeDtypeStruct(pieces[0].shape, jnp.bfloat16)] * 4, pieces, 0)


def to_return(results):
    def body(*refs):
        section = lax.axis_index("section")
        even = lax.axis_index("frame") % 2 == 0
        cases = ((section == 2, 0, 1), ((section == 1) & even, 2, 3))
        for wanted, one, two in (*cases, ((section == 1) & jnp.logical_not(even), 3, 2)):

            @pl.when(wanted)
            def _():
                refs[4][...] = refs[one][...]
                refs[5][...] = refs[two][...]

    outs = [jax.ShapeDtypeStruct(results[0].shape, jnp.bfloat16)] * 2
    return call(body, outs, results, 0, True)


def own_result(tops, returned, lasts):
    shape = (2,) + lasts[0].shape[1:]

    def body(*refs):
        section = lax.axis_index("section")
        place = lax.axis_index("frame")
        out_ref = refs[-1]

        @pl.when(section == 3)
        def _():
            out_ref[place // 2] = refs[0][0]
            out_ref[1 - place // 2] = refs[1][0]

        @pl.when(is_one_of(section, (1, 2)))
        def _():
            first = place_first(section)
            out_ref[first] = refs[2][0]
            out_ref[1 - first] = refs[3][0]

        @pl.when(section == 0)
        def _():
            out_ref[0] = refs[4][0]
            out_ref[1] = refs[5][0]

    outs = [jax.ShapeDtypeStruct(shape, jnp.bfloat16)]
    return call(body, outs, [*tops, *returned, *lasts], 0, True)[0]


def fetch(block, source, target, frame_step):
    frame_parts = lax.axis_size("frame")
    route = [
        (source * frame_parts + z + frame_step, target * frame_parts + z)
        for z in range(frame_parts)
        if 0 <= z + frame_step < frame_parts
    ]
    if not route:
        return jnp.zeros_like(block)
    if source == target and frame_step == 0:
        return block
    return lax.ppermute(block, ("section", "frame"), route)


def shifted_from(block, source, target, offset, unmoved=None):
    own_frames = block.shape[0]
    step, rest = divmod(offset, own_frames)
    pieces = []
    for frames, move in ((slice(rest, None), step), (slice(0, rest), step + 1)):
        piece = block[frames]
        if piece.shape[0] == 0:
            continue
        if move == 0 and unmoved is not None:
            pieces.append(unmoved[frames])
        else:
            pieces.append(fetch(piece, source, target, move))
    return pieces[0] if len(pieces) == 1 else jnp.concatenate(pieces)


def pair_step_of(own_frames, distance):
    step, rest = divmod(distance, own_frames)
    frame_parts = lax.axis_size("frame")
    return step if rest == 0 and frame_parts <= 2 * step < 2 * frame_parts else 0


def triple_from(block, source, target, distance, staged):
    own_frames = block.shape[0]
    frame_parts = lax.axis_size("frame")
    own = fetch(block, source, target, 0)
    if distance >= frame_parts * own_frames:
        return [own]
    step = pair_step_of(own_frames, distance)
    if step:
        route = [
            (source * frame_parts + z + move, target * frame_parts + z)
            for z in range(frame_parts)
            for move in (step, -step)
            if 0 <= z + move < frame_parts
        ]
        return [own, lax.ppermute(block, ("section", "frame"), route)]
    if staged:
        block, source = own, target
    return [
        own,
        shifted_from(block, source, target, distance, own),
        shifted_from(block, source, target, -distance, own),
    ]


def by_pairs(axis):
    count = lax.axis_size(axis)
    return count <= 4 and count & (count - 1) == 0


def sum_over(values, axis, beside=None):
    count = lax.axis_size(axis)
    index = lax.axis_index(axis)
    if not by_pairs(axis):
        parts = values.astype(jnp.bfloat16).reshape((count, -1) + values.shape[1:])
        parts = lax.all_to_all(parts, axis, split_axis=0, concat_axis=0, tiled=True)
        return jnp.sum(parts.astype(jnp.float32), axis=0), beside and beside(values)
    size = values.shape[0] // count
    total = lax.dynamic_slice_in_dim(values, index * size, size, 0)
    parts = [
        lax.dynamic_slice_in_dim(values, (index ^ mask) * size, size, 0).astype(jnp.bfloat16)
        for mask in range(1, count)
    ]
    other = beside and beside(parts)
    parts = [
        lax.ppermute(part, axis, [(i, i ^ mask) for i in range(count)])
        for mask, part in enumerate(parts, 1)
    ]
    if beside:
        parts = after(parts, other)
    for part in parts:
        total += part.astype(jnp.float32)
    return total, other


def gather_parts(part, axis):
    if not by_pairs(axis):
        return lax.all_gather(part, axis, axis=0, tiled=True)
    count = lax.axis_size(axis)
    index = lax.axis_index(axis)
    size = part.shape[0]
    whole = jnp.zeros((count * size,) + part.shape[1:], part.dtype)
    whole = lax.dynamic_update_slice_in_dim(whole, part, index * size, 0)
    for mask in range(1, count):
        got = lax.ppermute(part, axis, [(i, i ^ mask) for i in range(count)])
        whole = lax.dynamic_update_slice_in_dim(whole, got, (index ^ mask) * size, 0)
    return whole


def after(values, *others):
    return list(lax.optimization_barrier((tuple(values), others))[0])


def shifted_chains(block_input, cotangent, taps_space, taps_time):
    own_frames = block_input.shape[0]
    section_count = lax.axis_size("section")
    chains = 1 if own_frames % 2 else 2
    x_got = swap_edges(edges_of(block_input, lax.axis_size("row")))
    top = section_count - 1

    def triples(blocks, source, target):
        dilation = 2**target
        if dilation % chains == 0:
            step = pair_step_of(own_frames // chains, dilation // chains)
            early = early_half(step) if step else None
            return [
                (triple_from(block, source, target, dilation // chains, False), early)
                for block in blocks
            ]
        even, odd = blocks
        own_even = fetch(even, source, target, 0)
        next_even = shifted_from(even, source, target, (dilation + 1) // 2, own_even)
        own_odd = fetch(odd, source, target, 0)
        last_odd = shifted_from(odd, source, target, -((dilation + 1) // 2), own_odd)
        same_odd = shifted_from(odd, source, target, (dilation - 1) // 2, own_odd)
        same_even = shifted_from(even, source, target, -((dilation - 1) // 2), own_even)
        return [([own_even, same_odd, last_odd], None), ([own_odd, next_even, same_even], None)]

    everywhere = tuple(range(section_count))
    x_rows, slopes, actives = forward(block_input, x_got, taps_space, chains, everywhere)
    ready = triples(split_frames(cotangent, chains), top, top)
    grads = None
    results = []
    for owner in reversed(range(section_count)):
        groups = [[chain] for chain in range(chains)] if owner else [list(range(chains))]
        pre, outgoing = [], []
        for group in groups:
            mine = [ready[chain] for chain in group]
            if outgoing or results:
                earlier = outgoing or results[-1]
                mine = [(after(blocks, *earlier), early) for blocks, early in mine]
            group_pre, edges = temporal(owner, mine, [slopes[chain] for chain in group], taps_time)
            pre += group_pre
            if owner:
                heres = [blocks[0] for blocks, _ in mine]
                got = swap_edges(edges)
                outgoing += branches(owner, group_pre, got, heres, taps_space)
        inputs = after(pre, *outgoing) if owner else pre
        grads = kernel_grads(owner, x_rows, inputs, actives, ready, grads)
        if owner:
            results.append(outgoing)
            ready = triples(outgoing, owner, owner - 1)

    def finish(lasts, parts):
        section_index = lax.axis_index("section")
        own = results[0] if results else lasts
        for position, values in enumerate((results + [lasts])[1:], 1):
            own = [
                jnp.where(section_index == top - position, new, old)
                for new, old in zip(values, own)
            ]
        return jnp.stack(own, 1).reshape(block_input.shape)

    return grads, (pre, edges, [blocks[0] for blocks, _ in ready]), finish


def sum_kernels(grads, first_beside, then_beside):
    channels = grads.shape[-1]
    eighth = 12 * channels // 8
    pieces = grads.reshape(8, eighth, channels)
    half = jax.ShapeDtypeStruct((4, eighth, channels), jnp.bfloat16)
    part = jax.ShapeDtypeStruct((eighth, channels), jnp.bfloat16)
    wide = jax.ShapeDtypeStruct((eighth, channels), jnp.float32)

    def other_half(pieces_ref, out_ref):
        start = (1 - lax.axis_index("row")) * 4
        out_ref[...] = pieces_ref[pl.ds(start, 4)].astype(jnp.bfloat16)

    def add_half(pieces_ref, got_ref, *out_refs):
        start = lax.axis_index("row") * 4
        for mask, ref in enumerate(out_refs):
            at = lax.axis_index("frame") ^ mask
            ref[...] = (pieces_ref[start + at] + got_ref[at].astype(jnp.float32)).astype(ref.dtype)

    def add_parts(*refs):
        refs[-1][...] = sum(ref[...].astype(jnp.float32) for ref in refs[:-1]).astype(jnp.bfloat16)

    def line_parts(*refs):
        for mask, ref in enumerate(refs[:-1]):
            refs[-1][lax.axis_index("frame") ^ mask] = ref[...]

    def widen(mine_ref, other_ref, space_ref, time_ref):
        for row, (low, high) in enumerate(((mine_ref, other_ref), (other_ref, mine_ref))):

            @pl.when(lax.axis_index("row") == row)
            def _():
                space_ref[:4] = low[...].astype(jnp.float32)
                space_ref[4:] = high[:2].astype(jnp.float32)
                time_ref[...] = high[2:].astype(jnp.float32)

    def over_frame(block, mask):
        return lax.ppermute(block, "frame", [(i, i ^ mask) for i in range(4)])

    swap = [(0, 1), (1, 0)]
    got = lax.ppermute(call(other_half, [half], [pieces], 0)[0], "row", swap)
    got = after([got], *first_beside)
    own, *parts = call(add_half, [wide] + [part] * 3, [pieces, *got], 0)
    extra = then_beside(parts)
    came = [over_frame(block, mask) for mask, block in enumerate(parts, 1)]
    own = call(add_parts, [part], [own, *after(came, extra)], 0)[0]
    came = [over_frame(own, mask) for mask in range(1, 4)]
    mine = call(line_parts, [half], [own, *came], 0)[0]
    other = lax.ppermute(mine, "row", swap)
    outs = [
        jax.ShapeDtypeStruct((6, eighth, channels), jnp.float32),
        jax.ShapeDtypeStruct((2, eighth, channels), jnp.float32),
    ]
    space, time = call(widen, outs, [mine, other], 0)
    return space, time, extra


def dealt_chains(block_input, cotangent, taps_space, taps_time):
    def place():
        return lax.axis_index("frame")

    def even():
        return (place() % 2 == 0).astype(jnp.float32)

    def odd():
        return (place() % 2).astype(jnp.float32)

    def low():
        return (place() < 2).astype(jnp.float32)

    def outer():
        return (place() == 0) | (place() == 3)

    def inner():
        return (place() == 1) | (place() == 2)

    def send(block, *hops):
        route = [(a * 4 + i, b * 4 + j) for a, b, moves in hops for i, j in moves]
        return lax.ppermute(block, ("section", "frame"), route)

    def back(moves):
        return [(j, i) for i, j in moves]

    stay = [(i, i) for i in range(4)]
    deal = {
        2: ([(0, 0), (1, 2), (2, 1), (3, 3)], [(0, 1), (1, 3), (2, 0), (3, 2)]),
        1: ([(0, 1), (1, 0), (2, 2), (3, 3)], [(0, 0), (1, 1), (2, 3), (3, 2)]),
    }
    edges, block_input = prepare(block_input)
    x_got = swap_edges(edges)

    def step(owner, triples, slopes, picks):
        pre, edges = temporal(owner, triples, slopes, taps_time)
        heres = [blocks[0] for blocks, _ in triples]
        outs = branches(owner, pre, swap_edges(edges), heres, taps_space, picks)
        return after(pre, *outs), outs

    x_own, slopes_own, actives_own = forward(block_input, x_got, taps_space, 2, (0, 3))
    ready = [([block], None) for block in frame_by_frame(cotangent)]
    pre, tops = step(
        3, ready, slopes_own, [lambda: place() < 2, lambda: place() >= 2]
    )
    first, second = (send(block, (3, 2, deal[2][k])) for k, block in enumerate(tops))
    x_dealt = [
        send(block, *((s, s, deal[s][k]) for s in (1, 2)))
        for k, block in enumerate(frames_to_deal(block_input, x_got))
    ]
    grads = kernel_grads(3, x_own, pre, actives_own, ready, None)
    x_moved, slopes, actives = forward(
        block_input, x_got, taps_space, 2, (1, 2), x_dealt
    )

    ready = [([first, second], even), ([second, first], odd)]
    pre, outs = step(2, ready, slopes, [outer, inner, 0, 1])
    ends, others, *results = outs
    end = send(ends, (2, 1, stay))
    other = send(others, (2, 1, stay))
    cross = send(others, (2, 1, [(i, i ^ 2) for i in range(4)]))
    grads = kernel_grads(2, x_moved, pre, actives, ready, grads)

    ready = [([cross, other, end], low), ([end, cross], low)]
    pre, (middles, ends) = step(1, ready, slopes, [0, 1])
    results += [middles, ends]
    pieces = [
        send(ends, (1, 0, stay)),
        send(ends, (1, 0, [(1, 0), (2, 3)])),
        send(middles, (1, 0, stay)),
        send(middles, (1, 0, [(0, 1), (1, 2)])),
        send(middles, (1, 0, [(2, 1), (3, 2)])),
    ]
    grads = kernel_grads(1, x_moved, pre, actives, ready, grads)
    returned = [
        send(block, *((s, s, back(deal[s][k])) for s in (1, 2)))
        for k, block in enumerate(after(to_return(results), *pieces[:2]))
    ]
    before, one, two, later = line_up(after(pieces, *returned))
    ready = [([one, two, before], None), ([two, later, one], None)]
    pre, edges = temporal(0, ready, slopes_own, taps_time)
    grads = kernel_grads(0, x_own, pre, actives_own, ready, grads)

    def finish(lasts, parts):
        return own_result(tops, returned, lasts)

    return grads, (pre, edges, [one, two]), finish


def section_run(x_saved, cotangent, w_spatial, w_temporal):
    block_input = x_saved[0]
    taps_space = w_spatial[0]
    taps_time = w_temporal[0]
    channels = block_input.shape[-1]
    row_parts = lax.axis_size("row")
    shape = (lax.axis_size("section"), lax.axis_size("frame"), row_parts, block_input.shape[0])
    dealt = shape == (4, 4, 2, 2) and (12 * channels) % 128 == 0
    chains = dealt_chains if dealt else shifted_chains
    grads, (pre, edges, heres), finish = chains(block_input, cotangent, taps_space, taps_time)

    def last_branch(parts):
        return finish(branches(0, pre, swap_edges(after(edges, parts)), heres, taps_space), parts)

    if dealt:
        lasts = branches(0, pre, swap_edges(edges), heres, taps_space)

        def result(parts):
            return finish(after(lasts, *parts), parts)

        space, time, own = sum_kernels(grads, lasts, result)
        return (
            own[None],
            space.reshape((1, 3, 3, channels, channels)),
            time.reshape((1, 3, channels, channels)),
        )
    total, _ = sum_over(grads.reshape(-1, channels), "row")

    total, own = sum_over(total, "frame", last_branch)
    total = gather_parts(total.astype(jnp.bfloat16), "frame")
    split = 9 * channels
    if row_parts == 2:
        first = lax.axis_index("row") == 0
        other = lax.ppermute(total, "row", [(0, 1), (1, 0)])
        rest = split - total.shape[0]
        space = jnp.where(
            first,
            jnp.concatenate([total, other[:rest]]),
            jnp.concatenate([other, total[:rest]]),
        )
        time = jnp.where(first, other[rest:], total[rest:])
    else:
        total = gather_parts(total, "row")
        space, time = total[:split], total[split:]
    return (
        own[None],
        space.astype(jnp.float32).reshape((1, 3, 3, channels, channels)),
        time.astype(jnp.float32).reshape((1, 3, channels, channels)),
    )


def solution(mesh):
    return jax.shard_map(
        section_run,
        mesh=mesh,
        in_specs=(
            P("section", "frame", "row", None, None),
            P("frame", "row", None, None),
            P("section", None, None, None, None),
            P("section", None, None, None),
        ),
        out_specs=(
            P("section", "frame", "row", None, None),
            P("section", None, None, None, None),
            P("section", None, None, None),
        ),
        check_vma=False,
    )
```

```python
import jax
import jax.numpy as jnp
from jax import lax
from jax.experimental import pallas as pl
from jax.experimental.pallas import tpu as pltpu
from jax.sharding import PartitionSpec as P

VMEM_LIMIT = 16 * 1024 * 1024
NT = (((1,), (1,)), ((), ()))
NN = (((1,), (0,)), ((), ()))
TN = (((0,), (0,)), ((), ()))


def mul(a, b, how):
    return lax.dot_general(a, b, how, preferred_element_type=jnp.float32)


def call(body, outs, args, flops, loose=False):
    moved = sum(a.size * a.dtype.itemsize for a in (*args, *outs))
    return pl.pallas_call(
        body,
        out_shape=outs,
        in_specs=[pl.BlockSpec() if loose else pl.BlockSpec(memory_space=pltpu.VMEM) for _ in args],
        out_specs=[pl.BlockSpec(memory_space=pltpu.VMEM) for _ in outs],
        compiler_params=pltpu.CompilerParams(vmem_limit_bytes=VMEM_LIMIT),
        cost_estimate=pl.CostEstimate(flops=1, bytes_accessed=1, transcendentals=0),
    )(*args)


def flat(values):
    return values.reshape(-1, values.shape[-1])


def row_sides(got, row_count):
    if len(got) == 1:
        first = (lax.axis_index("row") == 0).astype(jnp.float32)
        rows = got[0].astype(jnp.float32)
        return (rows * (1.0 - first)).astype(jnp.bfloat16), (rows * first).astype(jnp.bfloat16)
    return got


def moved_rows(cells, above, below):
    return (
        flat(jnp.concatenate([above, cells[:, :-1]], axis=1)),
        flat(cells),
        flat(jnp.concatenate([cells[:, 1:], below], axis=1)),
    )


def moved_cols(values, step, col_count):
    count, lanes = values.shape
    shape = (count // col_count, col_count, lanes)
    col = lax.broadcasted_iota(jnp.int32, shape, 1).reshape(count, lanes)
    if step == 1:
        return jnp.where(col == col_count - 1, 0.0, pltpu.roll(values, count - 1, 0))
    return jnp.where(col == 0, 0.0, pltpu.roll(values, 1, 0))


def edges_of(cells, row_parts):
    head, tail = cells[:, :1], cells[:, -1:]
    if row_parts == 2:
        first = (lax.axis_index("row") == 0).astype(jnp.float32)
        return [(tail.astype(jnp.float32) * first + head.astype(jnp.float32) * (1.0 - first)).astype(jnp.bfloat16)]
    return [head, tail]


def swap_edges(edges):
    count = lax.axis_size("row")
    if count == 2:
        return [lax.ppermute(edges[0], "row", [(0, 1), (1, 0)])]
    head, tail = edges
    if count == 1:
        return [jnp.zeros_like(head), jnp.zeros_like(head)]
    return [
        lax.ppermute(tail, "row", [(i, i + 1) for i in range(count - 1)]),
        lax.ppermute(head, "row", [(i + 1, i) for i in range(count - 1)]),
    ]


def split_frames(values, chains):
    if chains == 1:
        return [values]
    pairs = values.reshape((values.shape[0] // chains, chains) + values.shape[1:])
    return [pairs[:, at] for at in range(chains)]


def windows(cells, rows):
    return jnp.concatenate([flat(cells[:, i : i + rows]) for i in range(3)], axis=1)


def is_one_of(section, sections):
    found = section == sections[0]
    for other in sections[1:]:
        found |= section == other
    return found


def forward(block_input, got, taps_space, chains, sections, dealt=()):
    frames, rows, cols, channels = block_input.shape
    part = (frames // chains, rows, cols, channels)
    args = list(dealt) or [block_input, *got]

    def body(*refs):
        section = lax.axis_index("section")
        pl.when(is_one_of(section, sections))(lambda: work(section, *refs))

    def work(section, *refs):
        w_ref, x_ref = refs[len(args) : len(args) + 2]
        slope_refs = refs[len(args) + 2 : len(args) + 2 + chains]
        active_refs = refs[len(args) + 2 + chains :]
        if dealt:
            first = jnp.where(section == 1, lax.axis_index("frame") % 2, 0)
            x_ref[first] = refs[0][0]
            x_ref[1 - first] = refs[1][0]
        else:
            above, below = row_sides([ref[...] for ref in refs[1 : len(args)]], rows)
            x_ref[...] = jnp.concatenate([above, refs[0][...], below], axis=1)
        taps = jnp.concatenate(
            [jnp.concatenate([w_ref[i, j] for j in range(3)], axis=1) for i in range(3)], axis=0
        )
        sums = mul(windows(x_ref[...], rows), taps, NN)
        pre_act = (
            moved_cols(sums[:, :channels], -1, cols)
            + sums[:, channels : 2 * channels]
            + moved_cols(sums[:, 2 * channels :], 1, cols)
        )
        sigma = jax.nn.sigmoid(pre_act)
        slope = (sigma * (1.0 + pre_act * (1.0 - sigma))).reshape(block_input.shape)
        active = (pre_act * sigma).astype(jnp.bfloat16).reshape(block_input.shape)
        for ref, values in zip(slope_refs, split_frames(slope, chains)):
            ref[...] = values
        for ref, values in zip(active_refs, split_frames(active, chains)):
            ref[...] = values

    outs = [jax.ShapeDtypeStruct((frames, rows + 2, cols, channels), jnp.bfloat16)]
    outs += [jax.ShapeDtypeStruct(part, jnp.float32)] * chains
    outs += [jax.ShapeDtypeStruct(part, jnp.bfloat16)] * chains
    outs = call(body, outs, [*args, taps_space], 18 * block_input.size * channels)
    return outs[0], outs[1 : 1 + chains], outs[1 + chains :]


def early_half(distance_step):
    return lambda: (lax.axis_index("frame") < lax.axis_size("frame") - distance_step).astype(
        jnp.float32
    )


def mixed(early, later, earlier):
    return early * later.astype(jnp.float32) + (1.0 - early) * earlier.astype(jnp.float32)


def temporal(owner, triples, slopes, taps_time):
    row_parts = lax.axis_size("row")
    part = slopes[0].shape
    channels = part[-1]
    edges = 1 if row_parts == 2 else 2
    sizes = [len(blocks) for blocks, _ in triples]

    def body(*refs):
        @pl.when(lax.axis_index("section") == owner)
        def _():
            at = 0
            w_ref = refs[sum(sizes) + len(slopes)]
            outs = refs[sum(sizes) + len(slopes) + 1 :]
            for chain, size in enumerate(sizes):
                blocks = [flat(ref[...]) for ref in refs[at : at + size]]
                at += size
                taps = [w_ref[1]]
                early = triples[chain][1]
                if size > 1 and early is None:
                    taps += [w_ref[0], w_ref[2]]
                elif size > 1:
                    taps.append(mixed(early(), w_ref[0], w_ref[2]).astype(jnp.bfloat16))
                    taps.append(mixed(early(), w_ref[2], w_ref[0]).astype(jnp.bfloat16))
                taps = taps[:size]
                sums = mul(jnp.concatenate(blocks, axis=1), jnp.concatenate(taps, axis=1), NT)
                back_act = sums.astype(jnp.bfloat16).astype(jnp.float32)
                slope = flat(refs[sum(sizes) + chain][...])
                grad_pre = (back_act * slope).astype(jnp.bfloat16).reshape(part)
                outs[chain][...] = grad_pre
                for ref, edge in zip(outs[len(slopes) :], edges_of(grad_pre, row_parts)):
                    ref[chain * part[0] : (chain + 1) * part[0]] = edge

    outs = [jax.ShapeDtypeStruct(part, jnp.bfloat16)] * len(slopes)
    outs += [
        jax.ShapeDtypeStruct((part[0] * len(slopes), 1) + part[2:], jnp.bfloat16)
    ] * edges
    args = [block for blocks, _ in triples for block in blocks] + list(slopes) + [taps_time]
    outs = call(body, outs, args, 6 * sum(s.size for s in slopes) * channels)
    return outs[: len(slopes)], outs[len(slopes) :]


def branches(owner, grads_pre, got, heres, taps_space, picks=None):
    part = heres[0].shape
    _, rows, cols, channels = part
    count = len(heres)
    picks = picks or list(range(count))

    def body(*refs):
        @pl.when(lax.axis_index("section") == owner)
        def _():
            out_refs = refs[2 * count + len(got) + 1 :]
            got_refs = refs[count : count + len(got)]
            here_refs = refs[count + len(got) : 2 * count + len(got)]
            w_ref = refs[2 * count + len(got)]
            taps = jnp.concatenate(
                [jnp.concatenate([w_ref[2 - i, j] for i in range(3)], axis=1) for j in range(3)],
                axis=0,
            )
            for chain in range(count):
                frames = slice(chain * part[0], (chain + 1) * part[0])
                above, below = row_sides([ref[frames] for ref in got_refs], rows)
                sides = jnp.concatenate(moved_rows(refs[chain][...], above, below), axis=1)
                sums = mul(sides, taps, NT)
                branch = (
                    moved_cols(sums[:, :channels], 1, cols)
                    + sums[:, channels : 2 * channels]
                    + moved_cols(sums[:, 2 * channels :], -1, cols)
                )
                branch = branch.astype(jnp.bfloat16).astype(jnp.float32)
                here = flat(here_refs[chain][...]).astype(jnp.float32)
                out = (here + branch).astype(jnp.bfloat16).reshape(part)
                for ref, pick in zip(out_refs, picks):
                    if callable(pick):
                        wanted = pick() if chain == 0 else jnp.logical_not(pick())
                        pl.when(wanted)(lambda ref=ref, out=out: ref.__setitem__(..., out))
                    elif pick == chain:
                        ref[...] = out

    outs = [jax.ShapeDtypeStruct(part, jnp.bfloat16)] * len(picks)
    args = [*grads_pre, *got, *heres, taps_space]
    return call(body, outs, args, 18 * sum(h.size for h in heres) * channels)


def kernel_grads(owner, x_rows, grads_pre, actives, triples, before):
    _, rows, cols, channels = x_rows.shape
    rows -= 2
    chains = len(actives)

    def body(*refs):
        section = lax.axis_index("section")
        out_ref = refs[-1]

        if before is not None:

            @pl.when(section != owner)
            def _():
                out_ref[...] = refs[-2][...]

        @pl.when(section == owner)
        def _():
            sides = [windows(cells, rows) for cells in split_frames(refs[0][...], chains)]
            pre = []
            time = [jnp.zeros((channels, channels), jnp.float32)] * 3
            at = 1 + 2 * chains
            for chain, (blocks, early) in enumerate(triples):
                mid = flat(refs[1 + chain][...])
                wide = mid.astype(jnp.float32)
                left = moved_cols(wide, 1, cols).astype(jnp.bfloat16)
                right = moved_cols(wide, -1, cols).astype(jnp.bfloat16)
                pre.append(jnp.concatenate([left, mid, right], axis=1))
                size = len(blocks)
                values = jnp.concatenate([flat(ref[...]) for ref in refs[at : at + size]], axis=1)
                at += size
                product = mul(flat(refs[1 + chains + chain][...]), values, TN)
                terms = [product[:, k * channels : (k + 1) * channels] for k in range(size)]
                time[1] = time[1] + terms[0]
                if size > 1 and early is None:
                    time[0] = time[0] + terms[1]
                    time[2] = time[2] + terms[2]
                elif size > 1:
                    share = early()
                    other = terms[2] if size == 3 else jnp.zeros_like(terms[1])
                    time[0] = time[0] + mixed(share, terms[1], other)
                    time[2] = time[2] + mixed(share, other, terms[1])
            space = mul(jnp.concatenate(sides), jnp.concatenate(pre), TN)
            for i in range(3):
                for j in range(3):
                    out_ref[3 * i + j] = space[
                        i * channels : (i + 1) * channels, j * channels : (j + 1) * channels
                    ]
            for k in range(3):
                out_ref[9 + k] = time[k]

    args = [x_rows, *grads_pre, *actives]
    args += [block for blocks, _ in triples for block in blocks]
    if before is not None:
        args.append(before)
    outs = [jax.ShapeDtypeStruct((12, channels, channels), jnp.float32)]
    return call(body, outs, args, 24 * x_rows.size * channels)[0]


def place_first(section):
    place = lax.axis_index("frame")
    return jnp.where(section == 2, place // 2, jnp.where((place == 0) | (place == 3), 1, 0))


def prepare(block_input):
    row_parts = lax.axis_size("row")
    frames, rows, cols, channels = block_input.shape
    edge_count = 1 if row_parts == 2 else 2

    def body(x_ref, *out_refs):
        for ref, edge in zip(out_refs, edges_of(x_ref[...], row_parts)):
            ref[...] = edge
        out_refs[edge_count][...] = x_ref[...]

    outs = [jax.ShapeDtypeStruct((frames, 1, cols, channels), jnp.bfloat16)] * edge_count
    outs += [jax.ShapeDtypeStruct(block_input.shape, jnp.bfloat16)]
    outs = call(body, outs, [block_input], 0)
    return outs[:edge_count], outs[edge_count]


def frame_by_frame(values):
    def body(ref, *out_refs):
        for frame, out_ref in enumerate(out_refs):
            out_ref[...] = ref[frame : frame + 1]

    out = jax.ShapeDtypeStruct((1,) + values.shape[1:], values.dtype)
    return call(body, [out] * values.shape[0], [values], 0)


def frames_to_deal(block_input, got):
    _, rows, cols, channels = block_input.shape

    def body(*refs):
        section = lax.axis_index("section")

        @pl.when(is_one_of(section, (1, 2)))
        def _():
            above, below = row_sides([ref[...] for ref in refs[1 : 1 + len(got)]], rows)
            cells = jnp.concatenate([above, refs[0][...], below], axis=1)
            first = place_first(section)
            for frame in range(2):

                @pl.when(first == frame)
                def _():
                    refs[-2][...] = cells[frame : frame + 1]
                    refs[-1][...] = cells[1 - frame : 2 - frame]

    outs = [jax.ShapeDtypeStruct((1, rows + 2, cols, channels), jnp.bfloat16)] * 2
    return call(body, outs, [block_input, *got], 0)


def line_up(pieces):
    table = ((None, 0, 1, 2), (0, 3, 2, 4), (3, 2, 4, 0), (2, 1, 0, None))

    def body(*refs):
        for place, order in enumerate(table):

            @pl.when((lax.axis_index("section") == 0) & (lax.axis_index("frame") == place))
            def _():
                for ref, at in zip(refs[len(pieces) :], order):
                    ref[...] = jnp.zeros(ref.shape, ref.dtype) if at is None else refs[at][...]

    return call(body, [jax.ShapeDtypeStruct(pieces[0].shape, jnp.bfloat16)] * 4, pieces, 0)


def to_return(results):
    def body(*refs):
        section = lax.axis_index("section")
        even = lax.axis_index("frame") % 2 == 0
        cases = ((section == 2, 0, 1), ((section == 1) & even, 2, 3))
        for wanted, one, two in (*cases, ((section == 1) & jnp.logical_not(even), 3, 2)):

            @pl.when(wanted)
            def _():
                refs[4][...] = refs[one][...]
                refs[5][...] = refs[two][...]

    outs = [jax.ShapeDtypeStruct(results[0].shape, jnp.bfloat16)] * 2
    return call(body, outs, results, 0, True)


def own_result(tops, returned, lasts):
    shape = (2,) + lasts[0].shape[1:]

    def body(*refs):
        section = lax.axis_index("section")
        place = lax.axis_index("frame")
        out_ref = refs[-1]

        @pl.when(section == 3)
        def _():
            out_ref[place // 2] = refs[0][0]
            out_ref[1 - place // 2] = refs[1][0]

        @pl.when(is_one_of(section, (1, 2)))
        def _():
            first = place_first(section)
            out_ref[first] = refs[2][0]
            out_ref[1 - first] = refs[3][0]

        @pl.when(section == 0)
        def _():
            out_ref[0] = refs[4][0]
            out_ref[1] = refs[5][0]

    outs = [jax.ShapeDtypeStruct(shape, jnp.bfloat16)]
    return call(body, outs, [*tops, *returned, *lasts], 0, True)[0]


def fetch(block, source, target, frame_step):
    frame_parts = lax.axis_size("frame")
    route = [
        (source * frame_parts + z + frame_step, target * frame_parts + z)
        for z in range(frame_parts)
        if 0 <= z + frame_step < frame_parts
    ]
    if not route:
        return jnp.zeros_like(block)
    if source == target and frame_step == 0:
        return block
    return lax.ppermute(block, ("section", "frame"), route)


def shifted_from(block, source, target, offset, unmoved=None):
    own_frames = block.shape[0]
    step, rest = divmod(offset, own_frames)
    pieces = []
    for frames, move in ((slice(rest, None), step), (slice(0, rest), step + 1)):
        piece = block[frames]
        if piece.shape[0] == 0:
            continue
        if move == 0 and unmoved is not None:
            pieces.append(unmoved[frames])
        else:
            pieces.append(fetch(piece, source, target, move))
    return pieces[0] if len(pieces) == 1 else jnp.concatenate(pieces)


def pair_step_of(own_frames, distance):
    step, rest = divmod(distance, own_frames)
    frame_parts = lax.axis_size("frame")
    return step if rest == 0 and frame_parts <= 2 * step < 2 * frame_parts else 0


def triple_from(block, source, target, distance, staged):
    own_frames = block.shape[0]
    frame_parts = lax.axis_size("frame")
    own = fetch(block, source, target, 0)
    if distance >= frame_parts * own_frames:
        return [own]
    step = pair_step_of(own_frames, distance)
    if step:
        route = [
            (source * frame_parts + z + move, target * frame_parts + z)
            for z in range(frame_parts)
            for move in (step, -step)
            if 0 <= z + move < frame_parts
        ]
        return [own, lax.ppermute(block, ("section", "frame"), route)]
    if staged:
        block, source = own, target
    return [
        own,
        shifted_from(block, source, target, distance, own),
        shifted_from(block, source, target, -distance, own),
    ]


def by_pairs(axis):
    count = lax.axis_size(axis)
    return count <= 4 and count & (count - 1) == 0


def sum_over(values, axis, beside=None):
    count = lax.axis_size(axis)
    index = lax.axis_index(axis)
    if not by_pairs(axis):
        parts = values.astype(jnp.bfloat16).reshape((count, -1) + values.shape[1:])
        parts = lax.all_to_all(parts, axis, split_axis=0, concat_axis=0, tiled=True)
        return jnp.sum(parts.astype(jnp.float32), axis=0), beside and beside(values)
    size = values.shape[0] // count
    total = lax.dynamic_slice_in_dim(values, index * size, size, 0)
    parts = [
        lax.dynamic_slice_in_dim(values, (index ^ mask) * size, size, 0).astype(jnp.bfloat16)
        for mask in range(1, count)
    ]
    other = beside and beside(parts)
    parts = [
        lax.ppermute(part, axis, [(i, i ^ mask) for i in range(count)])
        for mask, part in enumerate(parts, 1)
    ]
    if beside:
        parts = after(parts, other)
    for part in parts:
        total += part.astype(jnp.float32)
    return total, other


def gather_parts(part, axis):
    if not by_pairs(axis):
        return lax.all_gather(part, axis, axis=0, tiled=True)
    count = lax.axis_size(axis)
    index = lax.axis_index(axis)
    size = part.shape[0]
    whole = jnp.zeros((count * size,) + part.shape[1:], part.dtype)
    whole = lax.dynamic_update_slice_in_dim(whole, part, index * size, 0)
    for mask in range(1, count):
        got = lax.ppermute(part, axis, [(i, i ^ mask) for i in range(count)])
        whole = lax.dynamic_update_slice_in_dim(whole, got, (index ^ mask) * size, 0)
    return whole


def after(values, *others):
    return list(lax.optimization_barrier((tuple(values), others))[0])


def shifted_chains(block_input, cotangent, taps_space, taps_time):
    own_frames = block_input.shape[0]
    section_count = lax.axis_size("section")
    chains = 1 if own_frames % 2 else 2
    x_got = swap_edges(edges_of(block_input, lax.axis_size("row")))
    top = section_count - 1

    def triples(blocks, source, target):
        dilation = 2**target
        if dilation % chains == 0:
            step = pair_step_of(own_frames // chains, dilation // chains)
            early = early_half(step) if step else None
            return [
                (triple_from(block, source, target, dilation // chains, False), early)
                for block in blocks
            ]
        even, odd = blocks
        own_even = fetch(even, source, target, 0)
        next_even = shifted_from(even, source, target, (dilation + 1) // 2, own_even)
        own_odd = fetch(odd, source, target, 0)
        last_odd = shifted_from(odd, source, target, -((dilation + 1) // 2), own_odd)
        same_odd = shifted_from(odd, source, target, (dilation - 1) // 2, own_odd)
        same_even = shifted_from(even, source, target, -((dilation - 1) // 2), own_even)
        return [([own_even, same_odd, last_odd], None), ([own_odd, next_even, same_even], None)]

    everywhere = tuple(range(section_count))
    x_rows, slopes, actives = forward(block_input, x_got, taps_space, chains, everywhere)
    ready = triples(split_frames(cotangent, chains), top, top)
    grads = None
    results = []
    for owner in reversed(range(section_count)):
        groups = [[chain] for chain in range(chains)] if owner else [list(range(chains))]
        pre, outgoing = [], []
        for group in groups:
            mine = [ready[chain] for chain in group]
            if outgoing or results:
                earlier = outgoing or results[-1]
                mine = [(after(blocks, *earlier), early) for blocks, early in mine]
            group_pre, edges = temporal(owner, mine, [slopes[chain] for chain in group], taps_time)
            pre += group_pre
            if owner:
                heres = [blocks[0] for blocks, _ in mine]
                got = swap_edges(edges)
                outgoing += branches(owner, group_pre, got, heres, taps_space)
        inputs = after(pre, *outgoing) if owner else pre
        grads = kernel_grads(owner, x_rows, inputs, actives, ready, grads)
        if owner:
            results.append(outgoing)
            ready = triples(outgoing, owner, owner - 1)

    def finish(lasts, parts):
        section_index = lax.axis_index("section")
        own = results[0] if results else lasts
        for position, values in enumerate((results + [lasts])[1:], 1):
            own = [
                jnp.where(section_index == top - position, new, old)
                for new, old in zip(values, own)
            ]
        return jnp.stack(own, 1).reshape(block_input.shape)

    return grads, (pre, edges, [blocks[0] for blocks, _ in ready]), finish


def sum_kernels(grads, first_beside, then_beside):
    channels = grads.shape[-1]
    eighth = 12 * channels // 8
    pieces = grads.reshape(8, eighth, channels)
    half = jax.ShapeDtypeStruct((4, eighth, channels), jnp.bfloat16)
    part = jax.ShapeDtypeStruct((eighth, channels), jnp.bfloat16)
    wide = jax.ShapeDtypeStruct((eighth, channels), jnp.float32)

    def other_half(pieces_ref, out_ref):
        start = (1 - lax.axis_index("row")) * 4
        out_ref[...] = pieces_ref[pl.ds(start, 4)].astype(jnp.bfloat16)

    def add_half(pieces_ref, got_ref, *out_refs):
        start = lax.axis_index("row") * 4
        for mask, ref in enumerate(out_refs):
            at = lax.axis_index("frame") ^ mask
            ref[...] = (pieces_ref[start + at] + got_ref[at].astype(jnp.float32)).astype(ref.dtype)

    def add_parts(*refs):
        refs[-1][...] = sum(ref[...].astype(jnp.float32) for ref in refs[:-1]).astype(jnp.bfloat16)

    def line_parts(*refs):
        for mask, ref in enumerate(refs[:-1]):
            refs[-1][lax.axis_index("frame") ^ mask] = ref[...]

    def widen(mine_ref, other_ref, space_ref, time_ref):
        for row, (low, high) in enumerate(((mine_ref, other_ref), (other_ref, mine_ref))):

            @pl.when(lax.axis_index("row") == row)
            def _():
                space_ref[:4] = low[...].astype(jnp.float32)
                space_ref[4:] = high[:2].astype(jnp.float32)
                time_ref[...] = high[2:].astype(jnp.float32)

    def over_frame(block, mask):
        return lax.ppermute(block, "frame", [(i, i ^ mask) for i in range(4)])

    swap = [(0, 1), (1, 0)]
    got = lax.ppermute(call(other_half, [half], [pieces], 0)[0], "row", swap)
    got = after([got], *first_beside)
    own, *parts = call(add_half, [wide] + [part] * 3, [pieces, *got], 0)
    extra = then_beside(parts)
    came = [over_frame(block, mask) for mask, block in enumerate(parts, 1)]
    own = call(add_parts, [part], [own, *after(came, extra)], 0)[0]
    came = [over_frame(own, mask) for mask in range(1, 4)]
    mine = call(line_parts, [half], [own, *came], 0)[0]
    other = lax.ppermute(mine, "row", swap)
    outs = [
        jax.ShapeDtypeStruct((6, eighth, channels), jnp.float32),
        jax.ShapeDtypeStruct((2, eighth, channels), jnp.float32),
    ]
    space, time = call(widen, outs, [mine, other], 0)
    return space, time, extra


def dealt_chains(block_input, cotangent, taps_space, taps_time):
    def place():
        return lax.axis_index("frame")

    def even():
        return (place() % 2 == 0).astype(jnp.float32)

    def odd():
        return (place() % 2).astype(jnp.float32)

    def low():
        return (place() < 2).astype(jnp.float32)

    def outer():
        return (place() == 0) | (place() == 3)

    def inner():
        return (place() == 1) | (place() == 2)

    def send(block, *hops):
        route = [(a * 4 + i, b * 4 + j) for a, b, moves in hops for i, j in moves]
        return lax.ppermute(block, ("section", "frame"), route)

    def back(moves):
        return [(j, i) for i, j in moves]

    stay = [(i, i) for i in range(4)]
    deal = {
        2: ([(0, 0), (1, 2), (2, 1), (3, 3)], [(0, 1), (1, 3), (2, 0), (3, 2)]),
        1: ([(0, 1), (1, 0), (2, 2), (3, 3)], [(0, 0), (1, 1), (2, 3), (3, 2)]),
    }
    edges, block_input = prepare(block_input)
    x_got = swap_edges(edges)

    def step(owner, triples, slopes, picks):
        pre, edges = temporal(owner, triples, slopes, taps_time)
        heres = [blocks[0] for blocks, _ in triples]
        outs = branches(owner, pre, swap_edges(edges), heres, taps_space, picks)
        return after(pre, *outs), outs

    x_own, slopes_own, actives_own = forward(block_input, x_got, taps_space, 2, (0, 3))
    ready = [([block], None) for block in frame_by_frame(cotangent)]
    pre, tops = step(
        3, ready, slopes_own, [lambda: place() < 2, lambda: place() >= 2]
    )
    first, second = (send(block, (3, 2, deal[2][k])) for k, block in enumerate(tops))
    x_dealt = [
        send(block, *((s, s, deal[s][k]) for s in (1, 2)))
        for k, block in enumerate(frames_to_deal(block_input, x_got))
    ]
    grads = kernel_grads(3, x_own, pre, actives_own, ready, None)
    x_moved, slopes, actives = forward(
        block_input, x_got, taps_space, 2, (1, 2), x_dealt
    )

    ready = [([first, second], even), ([second, first], odd)]
    pre, outs = step(2, ready, slopes, [outer, inner, 0, 1])
    ends, others, *results = outs
    end = send(ends, (2, 1, stay))
    other = send(others, (2, 1, stay))
    cross = send(others, (2, 1, [(i, i ^ 2) for i in range(4)]))
    grads = kernel_grads(2, x_moved, pre, actives, ready, grads)

    ready = [([cross, other, end], low), ([end, cross], low)]
    pre, (middles, ends) = step(1, ready, slopes, [0, 1])
    results += [middles, ends]
    pieces = [
        send(ends, (1, 0, stay)),
        send(ends, (1, 0, [(1, 0), (2, 3)])),
        send(middles, (1, 0, stay)),
        send(middles, (1, 0, [(0, 1), (1, 2)])),
        send(middles, (1, 0, [(2, 1), (3, 2)])),
    ]
    grads = kernel_grads(1, x_moved, pre, actives, ready, grads)
    returned = [
        send(block, *((s, s, back(deal[s][k])) for s in (1, 2)))
        for k, block in enumerate(after(to_return(results), *pieces[:2]))
    ]
    before, one, two, later = line_up(after(pieces, *returned))
    ready = [([one, two, before], None), ([two, later, one], None)]
    pre, edges = temporal(0, ready, slopes_own, taps_time)
    grads = kernel_grads(0, x_own, pre, actives_own, ready, grads)

    def finish(lasts, parts):
        return own_result(tops, returned, lasts)

    return grads, (pre, edges, [one, two]), finish


def section_run(x_saved, cotangent, w_spatial, w_temporal):
    block_input = x_saved[0]
    taps_space = w_spatial[0]
    taps_time = w_temporal[0]
    channels = block_input.shape[-1]
    row_parts = lax.axis_size("row")
    shape = (lax.axis_size("section"), lax.axis_size("frame"), row_parts, block_input.shape[0])
    dealt = shape == (4, 4, 2, 2) and (12 * channels) % 128 == 0
    chains = dealt_chains if dealt else shifted_chains
    grads, (pre, edges, heres), finish = chains(block_input, cotangent, taps_space, taps_time)

    def last_branch(parts):
        return finish(branches(0, pre, swap_edges(after(edges, parts)), heres, taps_space), parts)

    if dealt:
        lasts = branches(0, pre, swap_edges(edges), heres, taps_space)

        def result(parts):
            return finish(after(lasts, *parts), parts)

        space, time, own = sum_kernels(grads, lasts, result)
        return (
            own[None],
            space.reshape((1, 3, 3, channels, channels)),
            time.reshape((1, 3, channels, channels)),
        )
    total, _ = sum_over(grads.reshape(-1, channels), "row")

    total, own = sum_over(total, "frame", last_branch)
    total = gather_parts(total.astype(jnp.bfloat16), "frame")
    split = 9 * channels
    if row_parts == 2:
        first = lax.axis_index("row") == 0
        other = lax.ppermute(total, "row", [(0, 1), (1, 0)])
        rest = split - total.shape[0]
        space = jnp.where(
            first,
            jnp.concatenate([total, other[:rest]]),
            jnp.concatenate([other, total[:rest]]),
        )
        time = jnp.where(first, other[rest:], total[rest:])
    else:
        total = gather_parts(total, "row")
        space, time = total[:split], total[split:]
    return (
        own[None],
        space.astype(jnp.float32).reshape((1, 3, 3, channels, channels)),
        time.astype(jnp.float32).reshape((1, 3, channels, channels)),
    )


def solution(mesh):
    return jax.shard_map(
        section_run,
        mesh=mesh,
        in_specs=(
            P("section", "frame", "row", None, None),
            P("frame", "row", None, None),
            P("section", None, None, None, None),
            P("section", None, None, None),
        ),
        out_specs=(
            P("section", "frame", "row", None, None),
            P("section", None, None, None, None),
            P("section", None, None, None),
        ),
        check_vma=False,
    )
```

```python
import jax
import jax.numpy as jnp
from jax import lax
from jax.experimental import pallas as pl
from jax.experimental.pallas import tpu as pltpu
from jax.sharding import PartitionSpec as P

VMEM_LIMIT = 16 * 1024 * 1024
NT = (((1,), (1,)), ((), ()))
NN = (((1,), (0,)), ((), ()))
TN = (((0,), (0,)), ((), ()))


def mul(a, b, how):
    return lax.dot_general(a, b, how, preferred_element_type=jnp.float32)


def call(body, outs, args, flops, loose=False, aliases=None):
    moved = sum(a.size * a.dtype.itemsize for a in (*args, *outs))
    return pl.pallas_call(
        body,
        out_shape=outs,
        input_output_aliases=aliases or {},
        in_specs=[pl.BlockSpec() if loose else pl.BlockSpec(memory_space=pltpu.VMEM) for _ in args],
        out_specs=[pl.BlockSpec(memory_space=pltpu.VMEM) for _ in outs],
        compiler_params=pltpu.CompilerParams(vmem_limit_bytes=VMEM_LIMIT),
        cost_estimate=pl.CostEstimate(flops=1, bytes_accessed=1, transcendentals=0),
    )(*args)


def flat(values):
    return values.reshape(-1, values.shape[-1])


def row_sides(got, row_count):
    if len(got) == 1:
        first = (lax.axis_index("row") == 0).astype(jnp.float32)
        rows = got[0].astype(jnp.float32)
        return (rows * (1.0 - first)).astype(jnp.bfloat16), (rows * first).astype(jnp.bfloat16)
    return got


def moved_rows(cells, above, below):
    return (
        flat(jnp.concatenate([above, cells[:, :-1]], axis=1)),
        flat(cells),
        flat(jnp.concatenate([cells[:, 1:], below], axis=1)),
    )


def moved_cols(values, step, col_count):
    count, lanes = values.shape
    shape = (count // col_count, col_count, lanes)
    col = lax.broadcasted_iota(jnp.int32, shape, 1).reshape(count, lanes)
    if step == 1:
        return jnp.where(col == col_count - 1, 0.0, pltpu.roll(values, count - 1, 0))
    return jnp.where(col == 0, 0.0, pltpu.roll(values, 1, 0))


def edges_of(cells, row_parts):
    head, tail = cells[:, :1], cells[:, -1:]
    if row_parts == 2:
        first = (lax.axis_index("row") == 0).astype(jnp.float32)
        return [(tail.astype(jnp.float32) * first + head.astype(jnp.float32) * (1.0 - first)).astype(jnp.bfloat16)]
    return [head, tail]


def swap_edges(edges):
    count = lax.axis_size("row")
    if count == 2:
        return [lax.ppermute(edges[0], "row", [(0, 1), (1, 0)])]
    head, tail = edges
    if count == 1:
        return [jnp.zeros_like(head), jnp.zeros_like(head)]
    return [
        lax.ppermute(tail, "row", [(i, i + 1) for i in range(count - 1)]),
        lax.ppermute(head, "row", [(i + 1, i) for i in range(count - 1)]),
    ]


def split_frames(values, chains):
    if chains == 1:
        return [values]
    pairs = values.reshape((values.shape[0] // chains, chains) + values.shape[1:])
    return [pairs[:, at] for at in range(chains)]


def put_picked(out_refs, picks, chain, put):
    for ref, pick in zip(out_refs, picks):
        if callable(pick):
            wanted = pick() if chain == 0 else jnp.logical_not(pick())
            pl.when(wanted)(lambda ref=ref: put(ref))
        elif pick == chain:
            put(ref)


def split_branches(owner, grads_pre, edges, heres, taps_space, picks):
    part = heres[0].shape
    _, rows, cols, channels = part
    count = len(heres)

    def wide(sides, taps):
        sums = mul(sides, taps, NT)
        return (
            moved_cols(sums[:, :channels], 1, cols)
            + sums[:, channels : 2 * channels]
            + moved_cols(sums[:, 2 * channels :], -1, cols)
        )

    def rounded(branch, here):
        branch = branch.astype(jnp.bfloat16).astype(jnp.float32)
        return (here.astype(jnp.float32) + branch).astype(jnp.bfloat16)

    def inner(*refs):
        @pl.when(lax.axis_index("section") == owner)
        def _():
            w_ref = refs[2 * count]
            out_refs = refs[2 * count + 1 : -1]
            taps = jnp.concatenate(
                [jnp.concatenate([w_ref[2 - i, j] for i in range(3)], axis=1) for j in range(3)],
                axis=0,
            )
            nothing = jnp.zeros((1, 1, cols, channels), jnp.bfloat16)
            for chain in range(count):
                sides = jnp.concatenate(moved_rows(refs[chain][...], nothing, nothing), axis=1)
                branch = wide(sides, taps)
                refs[-1][chain] = branch[(rows - 1) * cols :]
                refs[-1][count + chain] = branch[:cols]
                out = rounded(branch, flat(refs[count + chain][...])).reshape(part)
                put_picked(
                    out_refs, picks, chain, lambda ref, out=out: ref.__setitem__(..., out)
                )

    def outer(*refs):
        @pl.when(lax.axis_index("section") == owner)
        def _():
            row = lax.axis_index("row")
            at = (1 - row) * (rows - 1)
            partial_ref, got_ref, *here_refs = refs[len(picks) : len(picks) + 2 + count]
            w_ref = refs[len(picks) + 2 + count]
            out_refs = refs[len(picks) + 3 + count :]
            taps = jnp.concatenate([w_ref[2 * row, j] for j in range(3)], axis=0)
            for chain in range(count):
                branch = partial_ref[row * count + chain] + wide(got_ref[chain, 0], taps)
                out = rounded(branch, here_refs[chain][0, at])
                put_picked(
                    out_refs, picks, chain, lambda ref, out=out: ref.__setitem__((0, at), out)
                )

    outs = [jax.ShapeDtypeStruct(part, jnp.bfloat16)] * len(picks)
    rim = jax.ShapeDtypeStruct((2 * count, cols, channels), jnp.float32)
    got = swap_edges(edges)
    *begun, partial = call(inner, outs + [rim], [*grads_pre, *heres, taps_space], 0)
    args = [*begun, partial, *got, *heres, taps_space]
    return call(outer, outs, args, 0, aliases={k: k for k in range(len(picks))})


def windows(cells, rows):
    return jnp.concatenate([flat(cells[:, i : i + rows]) for i in range(3)], axis=1)


def is_one_of(section, sections):
    found = section == sections[0]
    for other in sections[1:]:
        found |= section == other
    return found


def forward(block_input, got, taps_space, chains, sections, dealt=()):
    frames, rows, cols, channels = block_input.shape
    part = (frames // chains, rows, cols, channels)
    args = list(dealt) or [block_input, *got]

    def body(*refs):
        section = lax.axis_index("section")
        pl.when(is_one_of(section, sections))(lambda: work(section, *refs))

    def work(section, *refs):
        w_ref, x_ref = refs[len(args) : len(args) + 2]
        slope_refs = refs[len(args) + 2 : len(args) + 2 + chains]
        active_refs = refs[len(args) + 2 + chains :]
        if dealt:
            first = jnp.where(section == 1, lax.axis_index("frame") % 2, 0)
            x_ref[first] = refs[0][0]
            x_ref[1 - first] = refs[1][0]
        else:
            above, below = row_sides([ref[...] for ref in refs[1 : len(args)]], rows)
            x_ref[...] = jnp.concatenate([above, refs[0][...], below], axis=1)
        taps = jnp.concatenate(
            [jnp.concatenate([w_ref[i, j] for j in range(3)], axis=1) for i in range(3)], axis=0
        )
        sums = mul(windows(x_ref[...], rows), taps, NN)
        pre_act = (
            moved_cols(sums[:, :channels], -1, cols)
            + sums[:, channels : 2 * channels]
            + moved_cols(sums[:, 2 * channels :], 1, cols)
        )
        sigma = jax.nn.sigmoid(pre_act)
        slope = (sigma * (1.0 + pre_act * (1.0 - sigma))).reshape(block_input.shape)
        active = (pre_act * sigma).astype(jnp.bfloat16).reshape(block_input.shape)
        for ref, values in zip(slope_refs, split_frames(slope, chains)):
            ref[...] = values
        for ref, values in zip(active_refs, split_frames(active, chains)):
            ref[...] = values

    outs = [jax.ShapeDtypeStruct((frames, rows + 2, cols, channels), jnp.bfloat16)]
    outs += [jax.ShapeDtypeStruct(part, jnp.float32)] * chains
    outs += [jax.ShapeDtypeStruct(part, jnp.bfloat16)] * chains
    outs = call(body, outs, [*args, taps_space], 18 * block_input.size * channels)
    return outs[0], outs[1 : 1 + chains], outs[1 + chains :]


def early_half(distance_step):
    return lambda: (lax.axis_index("frame") < lax.axis_size("frame") - distance_step).astype(
        jnp.float32
    )


def mixed(early, later, earlier):
    return early * later.astype(jnp.float32) + (1.0 - early) * earlier.astype(jnp.float32)


def temporal(owner, triples, slopes, taps_time):
    row_parts = lax.axis_size("row")
    part = slopes[0].shape
    channels = part[-1]
    edges = 1 if row_parts == 2 else 2
    sizes = [len(blocks) for blocks, _ in triples]

    def body(*refs):
        @pl.when(lax.axis_index("section") == owner)
        def _():
            at = 0
            w_ref = refs[sum(sizes) + len(slopes)]
            outs = refs[sum(sizes) + len(slopes) + 1 :]
            for chain, size in enumerate(sizes):
                blocks = [flat(ref[...]) for ref in refs[at : at + size]]
                at += size
                taps = [w_ref[1]]
                early = triples[chain][1]
                if size > 1 and early is None:
                    taps += [w_ref[0], w_ref[2]]
                elif size > 1:
                    taps.append(mixed(early(), w_ref[0], w_ref[2]).astype(jnp.bfloat16))
                    taps.append(mixed(early(), w_ref[2], w_ref[0]).astype(jnp.bfloat16))
                taps = taps[:size]
                sums = mul(jnp.concatenate(blocks, axis=1), jnp.concatenate(taps, axis=1), NT)
                back_act = sums.astype(jnp.bfloat16).astype(jnp.float32)
                slope = flat(refs[sum(sizes) + chain][...])
                grad_pre = (back_act * slope).astype(jnp.bfloat16).reshape(part)
                outs[chain][...] = grad_pre
                for ref, edge in zip(outs[len(slopes) :], edges_of(grad_pre, row_parts)):
                    ref[chain * part[0] : (chain + 1) * part[0]] = edge

    outs = [jax.ShapeDtypeStruct(part, jnp.bfloat16)] * len(slopes)
    outs += [
        jax.ShapeDtypeStruct((part[0] * len(slopes), 1) + part[2:], jnp.bfloat16)
    ] * edges
    args = [block for blocks, _ in triples for block in blocks] + list(slopes) + [taps_time]
    outs = call(body, outs, args, 6 * sum(s.size for s in slopes) * channels)
    return outs[: len(slopes)], outs[len(slopes) :]


def branches(owner, grads_pre, got, heres, taps_space, picks=None):
    part = heres[0].shape
    _, rows, cols, channels = part
    count = len(heres)
    picks = picks or list(range(count))

    def body(*refs):
        @pl.when(lax.axis_index("section") == owner)
        def _():
            out_refs = refs[2 * count + len(got) + 1 :]
            got_refs = refs[count : count + len(got)]
            here_refs = refs[count + len(got) : 2 * count + len(got)]
            w_ref = refs[2 * count + len(got)]
            taps = jnp.concatenate(
                [jnp.concatenate([w_ref[2 - i, j] for i in range(3)], axis=1) for j in range(3)],
                axis=0,
            )
            for chain in range(count):
                frames = slice(chain * part[0], (chain + 1) * part[0])
                above, below = row_sides([ref[frames] for ref in got_refs], rows)
                sides = jnp.concatenate(moved_rows(refs[chain][...], above, below), axis=1)
                sums = mul(sides, taps, NT)
                branch = (
                    moved_cols(sums[:, :channels], 1, cols)
                    + sums[:, channels : 2 * channels]
                    + moved_cols(sums[:, 2 * channels :], -1, cols)
                )
                branch = branch.astype(jnp.bfloat16).astype(jnp.float32)
                here = flat(here_refs[chain][...]).astype(jnp.float32)
                out = (here + branch).astype(jnp.bfloat16).reshape(part)
                for ref, pick in zip(out_refs, picks):
                    if callable(pick):
                        wanted = pick() if chain == 0 else jnp.logical_not(pick())
                        pl.when(wanted)(lambda ref=ref, out=out: ref.__setitem__(..., out))
                    elif pick == chain:
                        ref[...] = out

    outs = [jax.ShapeDtypeStruct(part, jnp.bfloat16)] * len(picks)
    args = [*grads_pre, *got, *heres, taps_space]
    return call(body, outs, args, 18 * sum(h.size for h in heres) * channels)


def kernel_grads(owner, x_rows, grads_pre, actives, triples, before):
    _, rows, cols, channels = x_rows.shape
    rows -= 2
    chains = len(actives)

    def body(*refs):
        section = lax.axis_index("section")
        out_ref = refs[-1]

        if before is not None:

            @pl.when(section != owner)
            def _():
                out_ref[...] = refs[-2][...]

        @pl.when(section == owner)
        def _():
            sides = [windows(cells, rows) for cells in split_frames(refs[0][...], chains)]
            pre = []
            time = [jnp.zeros((channels, channels), jnp.float32)] * 3
            at = 1 + 2 * chains
            for chain, (blocks, early) in enumerate(triples):
                mid = flat(refs[1 + chain][...])
                wide = mid.astype(jnp.float32)
                left = moved_cols(wide, 1, cols).astype(jnp.bfloat16)
                right = moved_cols(wide, -1, cols).astype(jnp.bfloat16)
                pre.append(jnp.concatenate([left, mid, right], axis=1))
                size = len(blocks)
                values = jnp.concatenate([flat(ref[...]) for ref in refs[at : at + size]], axis=1)
                at += size
                product = mul(flat(refs[1 + chains + chain][...]), values, TN)
                terms = [product[:, k * channels : (k + 1) * channels] for k in range(size)]
                time[1] = time[1] + terms[0]
                if size > 1 and early is None:
                    time[0] = time[0] + terms[1]
                    time[2] = time[2] + terms[2]
                elif size > 1:
                    share = early()
                    other = terms[2] if size == 3 else jnp.zeros_like(terms[1])
                    time[0] = time[0] + mixed(share, terms[1], other)
                    time[2] = time[2] + mixed(share, other, terms[1])
            space = mul(jnp.concatenate(sides), jnp.concatenate(pre), TN)
            for i in range(3):
                for j in range(3):
                    out_ref[3 * i + j] = space[
                        i * channels : (i + 1) * channels, j * channels : (j + 1) * channels
                    ]
            for k in range(3):
                out_ref[9 + k] = time[k]

    args = [x_rows, *grads_pre, *actives]
    args += [block for blocks, _ in triples for block in blocks]
    if before is not None:
        args.append(before)
    outs = [jax.ShapeDtypeStruct((12, channels, channels), jnp.float32)]
    return call(body, outs, args, 24 * x_rows.size * channels)[0]


def place_first(section):
    place = lax.axis_index("frame")
    return jnp.where(section == 2, place // 2, jnp.where((place == 0) | (place == 3), 1, 0))


def prepare(block_input):
    row_parts = lax.axis_size("row")
    frames, rows, cols, channels = block_input.shape
    edge_count = 1 if row_parts == 2 else 2

    def body(x_ref, *out_refs):
        for ref, edge in zip(out_refs, edges_of(x_ref[...], row_parts)):
            ref[...] = edge
        out_refs[edge_count][...] = x_ref[...]

    outs = [jax.ShapeDtypeStruct((frames, 1, cols, channels), jnp.bfloat16)] * edge_count
    outs += [jax.ShapeDtypeStruct(block_input.shape, jnp.bfloat16)]
    outs = call(body, outs, [block_input], 0)
    return outs[:edge_count], outs[edge_count]


def frame_by_frame(values):
    def body(ref, *out_refs):
        for frame, out_ref in enumerate(out_refs):
            out_ref[...] = ref[frame : frame + 1]

    out = jax.ShapeDtypeStruct((1,) + values.shape[1:], values.dtype)
    return call(body, [out] * values.shape[0], [values], 0)


def frames_to_deal(block_input, got):
    _, rows, cols, channels = block_input.shape

    def body(*refs):
        section = lax.axis_index("section")

        @pl.when(is_one_of(section, (1, 2)))
        def _():
            above, below = row_sides([ref[...] for ref in refs[1 : 1 + len(got)]], rows)
            cells = jnp.concatenate([above, refs[0][...], below], axis=1)
            first = place_first(section)
            for frame in range(2):

                @pl.when(first == frame)
                def _():
                    refs[-2][...] = cells[frame : frame + 1]
                    refs[-1][...] = cells[1 - frame : 2 - frame]

    outs = [jax.ShapeDtypeStruct((1, rows + 2, cols, channels), jnp.bfloat16)] * 2
    return call(body, outs, [block_input, *got], 0)


def line_up(pieces):
    table = ((None, 0, 1, 2), (0, 3, 2, 4), (3, 2, 4, 0), (2, 1, 0, None))

    def body(*refs):
        for place, order in enumerate(table):

            @pl.when((lax.axis_index("section") == 0) & (lax.axis_index("frame") == place))
            def _():
                for ref, at in zip(refs[len(pieces) :], order):
                    ref[...] = jnp.zeros(ref.shape, ref.dtype) if at is None else refs[at][...]

    return call(body, [jax.ShapeDtypeStruct(pieces[0].shape, jnp.bfloat16)] * 4, pieces, 0)


def to_return(results):
    def body(*refs):
        section = lax.axis_index("section")
        even = lax.axis_index("frame") % 2 == 0
        cases = ((section == 2, 0, 1), ((section == 1) & even, 2, 3))
        for wanted, one, two in (*cases, ((section == 1) & jnp.logical_not(even), 3, 2)):

            @pl.when(wanted)
            def _():
                refs[4][...] = refs[one][...]
                refs[5][...] = refs[two][...]

    outs = [jax.ShapeDtypeStruct(results[0].shape, jnp.bfloat16)] * 2
    return call(body, outs, results, 0, True)


def own_result(tops, returned, lasts):
    shape = (2,) + lasts[0].shape[1:]

    def body(*refs):
        section = lax.axis_index("section")
        place = lax.axis_index("frame")
        out_ref = refs[-1]

        @pl.when(section == 3)
        def _():
            out_ref[place // 2] = refs[0][0]
            out_ref[1 - place // 2] = refs[1][0]

        @pl.when(is_one_of(section, (1, 2)))
        def _():
            first = place_first(section)
            out_ref[first] = refs[2][0]
            out_ref[1 - first] = refs[3][0]

        @pl.when(section == 0)
        def _():
            out_ref[0] = refs[4][0]
            out_ref[1] = refs[5][0]

    outs = [jax.ShapeDtypeStruct(shape, jnp.bfloat16)]
    return call(body, outs, [*tops, *returned, *lasts], 0, True)[0]


def fetch(block, source, target, frame_step):
    frame_parts = lax.axis_size("frame")
    route = [
        (source * frame_parts + z + frame_step, target * frame_parts + z)
        for z in range(frame_parts)
        if 0 <= z + frame_step < frame_parts
    ]
    if not route:
        return jnp.zeros_like(block)
    if source == target and frame_step == 0:
        return block
    return lax.ppermute(block, ("section", "frame"), route)


def shifted_from(block, source, target, offset, unmoved=None):
    own_frames = block.shape[0]
    step, rest = divmod(offset, own_frames)
    pieces = []
    for frames, move in ((slice(rest, None), step), (slice(0, rest), step + 1)):
        piece = block[frames]
        if piece.shape[0] == 0:
            continue
        if move == 0 and unmoved is not None:
            pieces.append(unmoved[frames])
        else:
            pieces.append(fetch(piece, source, target, move))
    return pieces[0] if len(pieces) == 1 else jnp.concatenate(pieces)


def pair_step_of(own_frames, distance):
    step, rest = divmod(distance, own_frames)
    frame_parts = lax.axis_size("frame")
    return step if rest == 0 and frame_parts <= 2 * step < 2 * frame_parts else 0


def triple_from(block, source, target, distance, staged):
    own_frames = block.shape[0]
    frame_parts = lax.axis_size("frame")
    own = fetch(block, source, target, 0)
    if distance >= frame_parts * own_frames:
        return [own]
    step = pair_step_of(own_frames, distance)
    if step:
        route = [
            (source * frame_parts + z + move, target * frame_parts + z)
            for z in range(frame_parts)
            for move in (step, -step)
            if 0 <= z + move < frame_parts
        ]
        return [own, lax.ppermute(block, ("section", "frame"), route)]
    if staged:
        block, source = own, target
    return [
        own,
        shifted_from(block, source, target, distance, own),
        shifted_from(block, source, target, -distance, own),
    ]


def by_pairs(axis):
    count = lax.axis_size(axis)
    return count <= 4 and count & (count - 1) == 0


def sum_over(values, axis, beside=None):
    count = lax.axis_size(axis)
    index = lax.axis_index(axis)
    if not by_pairs(axis):
        parts = values.astype(jnp.bfloat16).reshape((count, -1) + values.shape[1:])
        parts = lax.all_to_all(parts, axis, split_axis=0, concat_axis=0, tiled=True)
        return jnp.sum(parts.astype(jnp.float32), axis=0), beside and beside(values)
    size = values.shape[0] // count
    total = lax.dynamic_slice_in_dim(values, index * size, size, 0)
    parts = [
        lax.dynamic_slice_in_dim(values, (index ^ mask) * size, size, 0).astype(jnp.bfloat16)
        for mask in range(1, count)
    ]
    other = beside and beside(parts)
    parts = [
        lax.ppermute(part, axis, [(i, i ^ mask) for i in range(count)])
        for mask, part in enumerate(parts, 1)
    ]
    if beside:
        parts = after(parts, other)
    for part in parts:
        total += part.astype(jnp.float32)
    return total, other


def gather_parts(part, axis):
    if not by_pairs(axis):
        return lax.all_gather(part, axis, axis=0, tiled=True)
    count = lax.axis_size(axis)
    index = lax.axis_index(axis)
    size = part.shape[0]
    whole = jnp.zeros((count * size,) + part.shape[1:], part.dtype)
    whole = lax.dynamic_update_slice_in_dim(whole, part, index * size, 0)
    for mask in range(1, count):
        got = lax.ppermute(part, axis, [(i, i ^ mask) for i in range(count)])
        whole = lax.dynamic_update_slice_in_dim(whole, got, (index ^ mask) * size, 0)
    return whole


def after(values, *others):
    return list(lax.optimization_barrier((tuple(values), others))[0])


def shifted_chains(block_input, cotangent, taps_space, taps_time):
    own_frames = block_input.shape[0]
    section_count = lax.axis_size("section")
    chains = 1 if own_frames % 2 else 2
    x_got = swap_edges(edges_of(block_input, lax.axis_size("row")))
    top = section_count - 1

    def triples(blocks, source, target):
        dilation = 2**target
        if dilation % chains == 0:
            step = pair_step_of(own_frames // chains, dilation // chains)
            early = early_half(step) if step else None
            return [
                (triple_from(block, source, target, dilation // chains, False), early)
                for block in blocks
            ]
        even, odd = blocks
        own_even = fetch(even, source, target, 0)
        next_even = shifted_from(even, source, target, (dilation + 1) // 2, own_even)
        own_odd = fetch(odd, source, target, 0)
        last_odd = shifted_from(odd, source, target, -((dilation + 1) // 2), own_odd)
        same_odd = shifted_from(odd, source, target, (dilation - 1) // 2, own_odd)
        same_even = shifted_from(even, source, target, -((dilation - 1) // 2), own_even)
        return [([own_even, same_odd, last_odd], None), ([own_odd, next_even, same_even], None)]

    everywhere = tuple(range(section_count))
    x_rows, slopes, actives = forward(block_input, x_got, taps_space, chains, everywhere)
    ready = triples(split_frames(cotangent, chains), top, top)
    grads = None
    results = []
    for owner in reversed(range(section_count)):
        groups = [[chain] for chain in range(chains)] if owner else [list(range(chains))]
        pre, outgoing = [], []
        for group in groups:
            mine = [ready[chain] for chain in group]
            if outgoing or results:
                earlier = outgoing or results[-1]
                mine = [(after(blocks, *earlier), early) for blocks, early in mine]
            group_pre, edges = temporal(owner, mine, [slopes[chain] for chain in group], taps_time)
            pre += group_pre
            if owner:
                heres = [blocks[0] for blocks, _ in mine]
                got = swap_edges(edges)
                outgoing += branches(owner, group_pre, got, heres, taps_space)
        inputs = after(pre, *outgoing) if owner else pre
        grads = kernel_grads(owner, x_rows, inputs, actives, ready, grads)
        if owner:
            results.append(outgoing)
            ready = triples(outgoing, owner, owner - 1)

    def finish(lasts, parts):
        section_index = lax.axis_index("section")
        own = results[0] if results else lasts
        for position, values in enumerate((results + [lasts])[1:], 1):
            own = [
                jnp.where(section_index == top - position, new, old)
                for new, old in zip(values, own)
            ]
        return jnp.stack(own, 1).reshape(block_input.shape)

    return grads, (pre, edges, [blocks[0] for blocks, _ in ready]), finish


def sum_kernels(grads, first_beside, then_beside):
    channels = grads.shape[-1]
    eighth = 12 * channels // 8
    pieces = grads.reshape(8, eighth, channels)
    half = jax.ShapeDtypeStruct((4, eighth, channels), jnp.bfloat16)
    part = jax.ShapeDtypeStruct((eighth, channels), jnp.bfloat16)
    wide = jax.ShapeDtypeStruct((eighth, channels), jnp.float32)

    def other_half(pieces_ref, out_ref):
        start = (1 - lax.axis_index("row")) * 4
        out_ref[...] = pieces_ref[pl.ds(start, 4)].astype(jnp.bfloat16)

    def add_half(pieces_ref, got_ref, *out_refs):
        start = lax.axis_index("row") * 4
        for mask, ref in enumerate(out_refs):
            at = lax.axis_index("frame") ^ mask
            ref[...] = (pieces_ref[start + at] + got_ref[at].astype(jnp.float32)).astype(ref.dtype)

    def add_parts(*refs):
        refs[-1][...] = sum(ref[...].astype(jnp.float32) for ref in refs[:-1]).astype(jnp.bfloat16)

    def line_parts(*refs):
        for mask, ref in enumerate(refs[:-1]):
            refs[-1][lax.axis_index("frame") ^ mask] = ref[...]

    def widen(mine_ref, other_ref, space_ref, time_ref):
        for row, (low, high) in enumerate(((mine_ref, other_ref), (other_ref, mine_ref))):

            @pl.when(lax.axis_index("row") == row)
            def _():
                space_ref[:4] = low[...].astype(jnp.float32)
                space_ref[4:] = high[:2].astype(jnp.float32)
                time_ref[...] = high[2:].astype(jnp.float32)

    def over_frame(block, mask):
        return lax.ppermute(block, "frame", [(i, i ^ mask) for i in range(4)])

    swap = [(0, 1), (1, 0)]
    got = lax.ppermute(call(other_half, [half], [pieces], 0)[0], "row", swap)
    got = after([got], *first_beside)
    own, *parts = call(add_half, [wide] + [part] * 3, [pieces, *got], 0)
    extra = then_beside(parts)
    came = [over_frame(block, mask) for mask, block in enumerate(parts, 1)]
    own = call(add_parts, [part], [own, *after(came, extra)], 0)[0]
    came = [over_frame(own, mask) for mask in range(1, 4)]
    mine = call(line_parts, [half], [own, *came], 0)[0]
    other = lax.ppermute(mine, "row", swap)
    outs = [
        jax.ShapeDtypeStruct((6, eighth, channels), jnp.float32),
        jax.ShapeDtypeStruct((2, eighth, channels), jnp.float32),
    ]
    space, time = call(widen, outs, [mine, other], 0)
    return space, time, extra


def dealt_chains(block_input, cotangent, taps_space, taps_time):
    def place():
        return lax.axis_index("frame")

    def even():
        return (place() % 2 == 0).astype(jnp.float32)

    def odd():
        return (place() % 2).astype(jnp.float32)

    def low():
        return (place() < 2).astype(jnp.float32)

    def outer():
        return (place() == 0) | (place() == 3)

    def inner():
        return (place() == 1) | (place() == 2)

    def send(block, *hops):
        route = [(a * 4 + i, b * 4 + j) for a, b, moves in hops for i, j in moves]
        return lax.ppermute(block, ("section", "frame"), route)

    def back(moves):
        return [(j, i) for i, j in moves]

    stay = [(i, i) for i in range(4)]
    deal = {
        2: ([(0, 0), (1, 2), (2, 1), (3, 3)], [(0, 1), (1, 3), (2, 0), (3, 2)]),
        1: ([(0, 1), (1, 0), (2, 2), (3, 3)], [(0, 0), (1, 1), (2, 3), (3, 2)]),
    }
    edges, block_input = prepare(block_input)
    x_got = swap_edges(edges)

    def step(owner, triples, slopes, picks):
        pre, edges = temporal(owner, triples, slopes, taps_time)
        heres = [blocks[0] for blocks, _ in triples]
        outs = split_branches(owner, pre, edges, heres, taps_space, picks)
        return after(pre, *outs), outs

    x_own, slopes_own, actives_own = forward(block_input, x_got, taps_space, 2, (0, 3))
    ready = [([block], None) for block in frame_by_frame(cotangent)]
    pre, tops = step(
        3, ready, slopes_own, [lambda: place() < 2, lambda: place() >= 2]
    )
    first, second = (send(block, (3, 2, deal[2][k])) for k, block in enumerate(tops))
    x_dealt = [
        send(block, *((s, s, deal[s][k]) for s in (1, 2)))
        for k, block in enumerate(frames_to_deal(block_input, x_got))
    ]
    grads = kernel_grads(3, x_own, pre, actives_own, ready, None)
    x_moved, slopes, actives = forward(
        block_input, x_got, taps_space, 2, (1, 2), x_dealt
    )

    ready = [([first, second], even), ([second, first], odd)]
    pre, outs = step(2, ready, slopes, [outer, inner, 0, 1])
    ends, others, *results = outs
    end = send(ends, (2, 1, stay))
    other = send(others, (2, 1, stay))
    cross = send(others, (2, 1, [(i, i ^ 2) for i in range(4)]))
    grads = kernel_grads(2, x_moved, pre, actives, ready, grads)

    ready = [([cross, other, end], low), ([end, cross], low)]
    pre, (middles, ends) = step(1, ready, slopes, [0, 1])
    results += [middles, ends]
    pieces = [
        send(ends, (1, 0, stay)),
        send(ends, (1, 0, [(1, 0), (2, 3)])),
        send(middles, (1, 0, stay)),
        send(middles, (1, 0, [(0, 1), (1, 2)])),
        send(middles, (1, 0, [(2, 1), (3, 2)])),
    ]
    grads = kernel_grads(1, x_moved, pre, actives, ready, grads)
    returned = [
        send(block, *((s, s, back(deal[s][k])) for s in (1, 2)))
        for k, block in enumerate(after(to_return(results), *pieces[:2]))
    ]
    before, one, two, later = line_up(after(pieces, *returned))
    ready = [([one, two, before], None), ([two, later, one], None)]
    pre, edges = temporal(0, ready, slopes_own, taps_time)
    grads = kernel_grads(0, x_own, pre, actives_own, ready, grads)

    def finish(lasts, parts):
        return own_result(tops, returned, lasts)

    return grads, (pre, edges, [one, two]), finish


def section_run(x_saved, cotangent, w_spatial, w_temporal):
    block_input = x_saved[0]
    taps_space = w_spatial[0]
    taps_time = w_temporal[0]
    channels = block_input.shape[-1]
    row_parts = lax.axis_size("row")
    shape = (lax.axis_size("section"), lax.axis_size("frame"), row_parts, block_input.shape[0])
    dealt = shape == (4, 4, 2, 2) and (12 * channels) % 128 == 0
    chains = dealt_chains if dealt else shifted_chains
    grads, (pre, edges, heres), finish = chains(block_input, cotangent, taps_space, taps_time)

    def last_branch(parts):
        return finish(branches(0, pre, swap_edges(after(edges, parts)), heres, taps_space), parts)

    if dealt:
        lasts = branches(0, pre, swap_edges(edges), heres, taps_space)

        def result(parts):
            return finish(after(lasts, *parts), parts)

        space, time, own = sum_kernels(grads, lasts, result)
        return (
            own[None],
            space.reshape((1, 3, 3, channels, channels)),
            time.reshape((1, 3, channels, channels)),
        )
    total, _ = sum_over(grads.reshape(-1, channels), "row")

    total, own = sum_over(total, "frame", last_branch)
    total = gather_parts(total.astype(jnp.bfloat16), "frame")
    split = 9 * channels
    if row_parts == 2:
        first = lax.axis_index("row") == 0
        other = lax.ppermute(total, "row", [(0, 1), (1, 0)])
        rest = split - total.shape[0]
        space = jnp.where(
            first,
            jnp.concatenate([total, other[:rest]]),
            jnp.concatenate([other, total[:rest]]),
        )
        time = jnp.where(first, other[rest:], total[rest:])
    else:
        total = gather_parts(total, "row")
        space, time = total[:split], total[split:]
    return (
        own[None],
        space.astype(jnp.float32).reshape((1, 3, 3, channels, channels)),
        time.astype(jnp.float32).reshape((1, 3, channels, channels)),
    )


def solution(mesh):
    return jax.shard_map(
        section_run,
        mesh=mesh,
        in_specs=(
            P("section", "frame", "row", None, None),
            P("frame", "row", None, None),
            P("section", None, None, None, None),
            P("section", None, None, None),
        ),
        out_specs=(
            P("section", "frame", "row", None, None),
            P("section", None, None, None, None),
            P("section", None, None, None),
        ),
        check_vma=False,
    )
```

```python
import jax
import jax.numpy as jnp
from jax import lax
from jax.experimental import pallas as pl
from jax.experimental.pallas import tpu as pltpu
from jax.sharding import PartitionSpec as P

VMEM_LIMIT = 16 * 1024 * 1024
NT = (((1,), (1,)), ((), ()))
NN = (((1,), (0,)), ((), ()))
TN = (((0,), (0,)), ((), ()))


def mul(a, b, how):
    return lax.dot_general(a, b, how, preferred_element_type=jnp.float32)


def call(body, outs, args, flops, loose=False, aliases=None):
    moved = sum(a.size * a.dtype.itemsize for a in (*args, *outs))
    return pl.pallas_call(
        body,
        out_shape=outs,
        input_output_aliases=aliases or {},
        in_specs=[pl.BlockSpec() if loose else pl.BlockSpec(memory_space=pltpu.VMEM) for _ in args],
        out_specs=[pl.BlockSpec(memory_space=pltpu.VMEM) for _ in outs],
        compiler_params=pltpu.CompilerParams(vmem_limit_bytes=VMEM_LIMIT),
        cost_estimate=pl.CostEstimate(flops=1, bytes_accessed=1, transcendentals=0),
    )(*args)


def flat(values):
    return values.reshape(-1, values.shape[-1])


def row_sides(got, row_count):
    if len(got) == 1:
        first = (lax.axis_index("row") == 0).astype(jnp.float32)
        rows = got[0].astype(jnp.float32)
        return (rows * (1.0 - first)).astype(jnp.bfloat16), (rows * first).astype(jnp.bfloat16)
    return got


def moved_rows(cells, above, below):
    return (
        flat(jnp.concatenate([above, cells[:, :-1]], axis=1)),
        flat(cells),
        flat(jnp.concatenate([cells[:, 1:], below], axis=1)),
    )


def moved_cols(values, step, col_count):
    count, lanes = values.shape
    shape = (count // col_count, col_count, lanes)
    col = lax.broadcasted_iota(jnp.int32, shape, 1).reshape(count, lanes)
    if step == 1:
        return jnp.where(col == col_count - 1, 0.0, pltpu.roll(values, count - 1, 0))
    return jnp.where(col == 0, 0.0, pltpu.roll(values, 1, 0))


def edges_of(cells, row_parts):
    head, tail = cells[:, :1], cells[:, -1:]
    if row_parts == 2:
        first = (lax.axis_index("row") == 0).astype(jnp.float32)
        return [(tail.astype(jnp.float32) * first + head.astype(jnp.float32) * (1.0 - first)).astype(jnp.bfloat16)]
    return [head, tail]


def swap_edges(edges):
    count = lax.axis_size("row")
    if count == 2:
        return [lax.ppermute(edges[0], "row", [(0, 1), (1, 0)])]
    head, tail = edges
    if count == 1:
        return [jnp.zeros_like(head), jnp.zeros_like(head)]
    return [
        lax.ppermute(tail, "row", [(i, i + 1) for i in range(count - 1)]),
        lax.ppermute(head, "row", [(i + 1, i) for i in range(count - 1)]),
    ]


def split_frames(values, chains):
    if chains == 1:
        return [values]
    pairs = values.reshape((values.shape[0] // chains, chains) + values.shape[1:])
    return [pairs[:, at] for at in range(chains)]


def put_picked(out_refs, picks, chain, put):
    for ref, pick in zip(out_refs, picks):
        if callable(pick):
            wanted = pick() if chain == 0 else jnp.logical_not(pick())
            pl.when(wanted)(lambda ref=ref: put(ref))
        elif pick == chain:
            put(ref)


def split_branches(owner, grads_pre, edges, heres, taps_space, picks):
    part = heres[0].shape
    _, rows, cols, channels = part
    count = len(heres)

    def wide(sides, taps):
        sums = mul(sides, taps, NT)
        return (
            moved_cols(sums[:, :channels], 1, cols)
            + sums[:, channels : 2 * channels]
            + moved_cols(sums[:, 2 * channels :], -1, cols)
        )

    def rounded(branch, here):
        branch = branch.astype(jnp.bfloat16).astype(jnp.float32)
        return (here.astype(jnp.float32) + branch).astype(jnp.bfloat16)

    def inner(*refs):
        @pl.when(lax.axis_index("section") == owner)
        def _():
            w_ref = refs[2 * count]
            out_refs = refs[2 * count + 1 : -1]
            taps = jnp.concatenate(
                [jnp.concatenate([w_ref[2 - i, j] for i in range(3)], axis=1) for j in range(3)],
                axis=0,
            )
            nothing = jnp.zeros((1, 1, cols, channels), jnp.bfloat16)
            for chain in range(count):
                sides = jnp.concatenate(moved_rows(refs[chain][...], nothing, nothing), axis=1)
                branch = wide(sides, taps)
                refs[-1][chain] = branch[(rows - 1) * cols :]
                refs[-1][count + chain] = branch[:cols]
                out = rounded(branch, flat(refs[count + chain][...])).reshape(part)
                put_picked(
                    out_refs, picks, chain, lambda ref, out=out: ref.__setitem__(..., out)
                )

    def outer(*refs):
        @pl.when(lax.axis_index("section") == owner)
        def _():
            row = lax.axis_index("row")
            at = (1 - row) * (rows - 1)
            partial_ref, got_ref, *here_refs = refs[len(picks) : len(picks) + 2 + count]
            w_ref = refs[len(picks) + 2 + count]
            out_refs = refs[len(picks) + 3 + count :]
            taps = jnp.concatenate([w_ref[2 * row, j] for j in range(3)], axis=0)
            for chain in range(count):
                branch = partial_ref[row * count + chain] + wide(got_ref[chain, 0], taps)
                out = rounded(branch, here_refs[chain][0, at])
                put_picked(
                    out_refs, picks, chain, lambda ref, out=out: ref.__setitem__((0, at), out)
                )

    outs = [jax.ShapeDtypeStruct(part, jnp.bfloat16)] * len(picks)
    rim = jax.ShapeDtypeStruct((2 * count, cols, channels), jnp.float32)
    got = swap_edges(edges)
    *begun, partial = call(inner, outs + [rim], [*grads_pre, *heres, taps_space], 0)
    args = [*begun, partial, *got, *heres, taps_space]
    return call(outer, outs, args, 0, aliases={k: k for k in range(len(picks))})


def windows(cells, rows):
    return jnp.concatenate([flat(cells[:, i : i + rows]) for i in range(3)], axis=1)


def is_one_of(section, sections):
    found = section == sections[0]
    for other in sections[1:]:
        found |= section == other
    return found


def forward(block_input, got, taps_space, chains, sections, dealt=()):
    frames, rows, cols, channels = block_input.shape
    part = (frames // chains, rows, cols, channels)
    args = list(dealt) or [block_input, *got]

    def body(*refs):
        section = lax.axis_index("section")
        pl.when(is_one_of(section, sections))(lambda: work(section, *refs))

    def work(section, *refs):
        w_ref, x_ref = refs[len(args) : len(args) + 2]
        slope_refs = refs[len(args) + 2 : len(args) + 2 + chains]
        active_refs = refs[len(args) + 2 + chains :]
        if dealt:
            first = jnp.where(section == 1, lax.axis_index("frame") % 2, 0)
            x_ref[first] = refs[0][0]
            x_ref[1 - first] = refs[1][0]
        else:
            above, below = row_sides([ref[...] for ref in refs[1 : len(args)]], rows)
            x_ref[...] = jnp.concatenate([above, refs[0][...], below], axis=1)
        taps = jnp.concatenate(
            [jnp.concatenate([w_ref[i, j] for j in range(3)], axis=1) for i in range(3)], axis=0
        )
        sums = mul(windows(x_ref[...], rows), taps, NN)
        pre_act = (
            moved_cols(sums[:, :channels], -1, cols)
            + sums[:, channels : 2 * channels]
            + moved_cols(sums[:, 2 * channels :], 1, cols)
        )
        sigma = jax.nn.sigmoid(pre_act)
        slope = (sigma * (1.0 + pre_act * (1.0 - sigma))).reshape(block_input.shape)
        active = (pre_act * sigma).astype(jnp.bfloat16).reshape(block_input.shape)
        for ref, values in zip(slope_refs, split_frames(slope, chains)):
            ref[...] = values
        for ref, values in zip(active_refs, split_frames(active, chains)):
            ref[...] = values

    outs = [jax.ShapeDtypeStruct((frames, rows + 2, cols, channels), jnp.bfloat16)]
    outs += [jax.ShapeDtypeStruct(part, jnp.float32)] * chains
    outs += [jax.ShapeDtypeStruct(part, jnp.bfloat16)] * chains
    outs = call(body, outs, [*args, taps_space], 18 * block_input.size * channels)
    return outs[0], outs[1 : 1 + chains], outs[1 + chains :]


def early_half(distance_step):
    return lambda: (lax.axis_index("frame") < lax.axis_size("frame") - distance_step).astype(
        jnp.float32
    )


def mixed(early, later, earlier):
    return early * later.astype(jnp.float32) + (1.0 - early) * earlier.astype(jnp.float32)


def temporal(owner, triples, slopes, taps_time):
    row_parts = lax.axis_size("row")
    part = slopes[0].shape
    channels = part[-1]
    edges = 1 if row_parts == 2 else 2
    sizes = [len(blocks) for blocks, _ in triples]

    def body(*refs):
        @pl.when(lax.axis_index("section") == owner)
        def _():
            at = 0
            w_ref = refs[sum(sizes) + len(slopes)]
            outs = refs[sum(sizes) + len(slopes) + 1 :]
            for chain, size in enumerate(sizes):
                blocks = [flat(ref[...]) for ref in refs[at : at + size]]
                at += size
                taps = [w_ref[1]]
                early = triples[chain][1]
                if size > 1 and early is None:
                    taps += [w_ref[0], w_ref[2]]
                elif size > 1:
                    taps.append(mixed(early(), w_ref[0], w_ref[2]).astype(jnp.bfloat16))
                    taps.append(mixed(early(), w_ref[2], w_ref[0]).astype(jnp.bfloat16))
                taps = taps[:size]
                sums = mul(jnp.concatenate(blocks, axis=1), jnp.concatenate(taps, axis=1), NT)
                back_act = sums.astype(jnp.bfloat16).astype(jnp.float32)
                slope = flat(refs[sum(sizes) + chain][...])
                grad_pre = (back_act * slope).astype(jnp.bfloat16).reshape(part)
                outs[chain][...] = grad_pre
                for ref, edge in zip(outs[len(slopes) :], edges_of(grad_pre, row_parts)):
                    ref[chain * part[0] : (chain + 1) * part[0]] = edge

    outs = [jax.ShapeDtypeStruct(part, jnp.bfloat16)] * len(slopes)
    outs += [
        jax.ShapeDtypeStruct((part[0] * len(slopes), 1) + part[2:], jnp.bfloat16)
    ] * edges
    args = [block for blocks, _ in triples for block in blocks] + list(slopes) + [taps_time]
    outs = call(body, outs, args, 6 * sum(s.size for s in slopes) * channels)
    return outs[: len(slopes)], outs[len(slopes) :]


def branches(owner, grads_pre, got, heres, taps_space, picks=None):
    part = heres[0].shape
    _, rows, cols, channels = part
    count = len(heres)
    picks = picks or list(range(count))

    def body(*refs):
        @pl.when(lax.axis_index("section") == owner)
        def _():
            out_refs = refs[2 * count + len(got) + 1 :]
            got_refs = refs[count : count + len(got)]
            here_refs = refs[count + len(got) : 2 * count + len(got)]
            w_ref = refs[2 * count + len(got)]
            taps = jnp.concatenate(
                [jnp.concatenate([w_ref[2 - i, j] for i in range(3)], axis=1) for j in range(3)],
                axis=0,
            )
            for chain in range(count):
                frames = slice(chain * part[0], (chain + 1) * part[0])
                above, below = row_sides([ref[frames] for ref in got_refs], rows)
                sides = jnp.concatenate(moved_rows(refs[chain][...], above, below), axis=1)
                sums = mul(sides, taps, NT)
                branch = (
                    moved_cols(sums[:, :channels], 1, cols)
                    + sums[:, channels : 2 * channels]
                    + moved_cols(sums[:, 2 * channels :], -1, cols)
                )
                branch = branch.astype(jnp.bfloat16).astype(jnp.float32)
                here = flat(here_refs[chain][...]).astype(jnp.float32)
                out = (here + branch).astype(jnp.bfloat16).reshape(part)
                for ref, pick in zip(out_refs, picks):
                    if callable(pick):
                        wanted = pick() if chain == 0 else jnp.logical_not(pick())
                        pl.when(wanted)(lambda ref=ref, out=out: ref.__setitem__(..., out))
                    elif pick == chain:
                        ref[...] = out

    outs = [jax.ShapeDtypeStruct(part, jnp.bfloat16)] * len(picks)
    args = [*grads_pre, *got, *heres, taps_space]
    return call(body, outs, args, 18 * sum(h.size for h in heres) * channels)


def kernel_grads(owner, x_rows, grads_pre, actives, triples, before):
    _, rows, cols, channels = x_rows.shape
    rows -= 2
    chains = len(actives)

    def body(*refs):
        section = lax.axis_index("section")
        out_ref = refs[-1]

        if before is not None:

            @pl.when(section != owner)
            def _():
                out_ref[...] = refs[-2][...]

        @pl.when(section == owner)
        def _():
            sides = [windows(cells, rows) for cells in split_frames(refs[0][...], chains)]
            pre = []
            time = [jnp.zeros((channels, channels), jnp.float32)] * 3
            at = 1 + 2 * chains
            for chain, (blocks, early) in enumerate(triples):
                mid = flat(refs[1 + chain][...])
                wide = mid.astype(jnp.float32)
                left = moved_cols(wide, 1, cols).astype(jnp.bfloat16)
                right = moved_cols(wide, -1, cols).astype(jnp.bfloat16)
                pre.append(jnp.concatenate([left, mid, right], axis=1))
                size = len(blocks)
                values = jnp.concatenate([flat(ref[...]) for ref in refs[at : at + size]], axis=1)
                at += size
                product = mul(flat(refs[1 + chains + chain][...]), values, TN)
                terms = [product[:, k * channels : (k + 1) * channels] for k in range(size)]
                time[1] = time[1] + terms[0]
                if size > 1 and early is None:
                    time[0] = time[0] + terms[1]
                    time[2] = time[2] + terms[2]
                elif size > 1:
                    share = early()
                    other = terms[2] if size == 3 else jnp.zeros_like(terms[1])
                    time[0] = time[0] + mixed(share, terms[1], other)
                    time[2] = time[2] + mixed(share, other, terms[1])
            space = mul(jnp.concatenate(sides), jnp.concatenate(pre), TN)
            for i in range(3):
                for j in range(3):
                    out_ref[3 * i + j] = space[
                        i * channels : (i + 1) * channels, j * channels : (j + 1) * channels
                    ]
            for k in range(3):
                out_ref[9 + k] = time[k]

    args = [x_rows, *grads_pre, *actives]
    args += [block for blocks, _ in triples for block in blocks]
    if before is not None:
        args.append(before)
    outs = [jax.ShapeDtypeStruct((12, channels, channels), jnp.float32)]
    return call(body, outs, args, 24 * x_rows.size * channels)[0]


def place_first(section):
    place = lax.axis_index("frame")
    return jnp.where(section == 2, place // 2, jnp.where((place == 0) | (place == 3), 1, 0))


def prepare(block_input):
    row_parts = lax.axis_size("row")
    frames, rows, cols, channels = block_input.shape
    edge_count = 1 if row_parts == 2 else 2

    def body(x_ref, *out_refs):
        for ref, edge in zip(out_refs, edges_of(x_ref[...], row_parts)):
            ref[...] = edge
        out_refs[edge_count][...] = x_ref[...]

    outs = [jax.ShapeDtypeStruct((frames, 1, cols, channels), jnp.bfloat16)] * edge_count
    outs += [jax.ShapeDtypeStruct(block_input.shape, jnp.bfloat16)]
    outs = call(body, outs, [block_input], 0)
    return outs[:edge_count], outs[edge_count]


def frame_by_frame(values):
    def body(ref, *out_refs):
        for frame, out_ref in enumerate(out_refs):
            out_ref[...] = ref[frame : frame + 1]

    out = jax.ShapeDtypeStruct((1,) + values.shape[1:], values.dtype)
    return call(body, [out] * values.shape[0], [values], 0)


def frames_to_deal(block_input, got):
    _, rows, cols, channels = block_input.shape

    def body(*refs):
        section = lax.axis_index("section")

        @pl.when(is_one_of(section, (1, 2)))
        def _():
            above, below = row_sides([ref[...] for ref in refs[1 : 1 + len(got)]], rows)
            cells = jnp.concatenate([above, refs[0][...], below], axis=1)
            first = place_first(section)
            for frame in range(2):

                @pl.when(first == frame)
                def _():
                    refs[-2][...] = cells[frame : frame + 1]
                    refs[-1][...] = cells[1 - frame : 2 - frame]

    outs = [jax.ShapeDtypeStruct((1, rows + 2, cols, channels), jnp.bfloat16)] * 2
    return call(body, outs, [block_input, *got], 0)


def line_up(pieces):
    table = ((None, 0, 1, 2), (0, 3, 2, 4), (3, 2, 4, 0), (2, 1, 0, None))

    def body(*refs):
        for place, order in enumerate(table):

            @pl.when((lax.axis_index("section") == 0) & (lax.axis_index("frame") == place))
            def _():
                for ref, at in zip(refs[len(pieces) :], order):
                    ref[...] = jnp.zeros(ref.shape, ref.dtype) if at is None else refs[at][...]

    return call(body, [jax.ShapeDtypeStruct(pieces[0].shape, jnp.bfloat16)] * 4, pieces, 0)


def to_return(results):
    def body(*refs):
        section = lax.axis_index("section")
        even = lax.axis_index("frame") % 2 == 0
        cases = ((section == 2, 0, 1), ((section == 1) & even, 2, 3))
        for wanted, one, two in (*cases, ((section == 1) & jnp.logical_not(even), 3, 2)):

            @pl.when(wanted)
            def _():
                refs[4][...] = refs[one][...]
                refs[5][...] = refs[two][...]

    outs = [jax.ShapeDtypeStruct(results[0].shape, jnp.bfloat16)] * 2
    return call(body, outs, results, 0, True)


def own_result(tops, returned, lasts):
    shape = (2,) + lasts[0].shape[1:]

    def body(*refs):
        section = lax.axis_index("section")
        place = lax.axis_index("frame")
        out_ref = refs[-1]

        @pl.when(section == 3)
        def _():
            out_ref[place // 2] = refs[0][0]
            out_ref[1 - place // 2] = refs[1][0]

        @pl.when(is_one_of(section, (1, 2)))
        def _():
            first = place_first(section)
            out_ref[first] = refs[2][0]
            out_ref[1 - first] = refs[3][0]

        @pl.when(section == 0)
        def _():
            out_ref[0] = refs[4][0]
            out_ref[1] = refs[5][0]

    outs = [jax.ShapeDtypeStruct(shape, jnp.bfloat16)]
    return call(body, outs, [*tops, *returned, *lasts], 0, True)[0]


def fetch(block, source, target, frame_step):
    frame_parts = lax.axis_size("frame")
    route = [
        (source * frame_parts + z + frame_step, target * frame_parts + z)
        for z in range(frame_parts)
        if 0 <= z + frame_step < frame_parts
    ]
    if not route:
        return jnp.zeros_like(block)
    if source == target and frame_step == 0:
        return block
    return lax.ppermute(block, ("section", "frame"), route)


def shifted_from(block, source, target, offset, unmoved=None):
    own_frames = block.shape[0]
    step, rest = divmod(offset, own_frames)
    pieces = []
    for frames, move in ((slice(rest, None), step), (slice(0, rest), step + 1)):
        piece = block[frames]
        if piece.shape[0] == 0:
            continue
        if move == 0 and unmoved is not None:
            pieces.append(unmoved[frames])
        else:
            pieces.append(fetch(piece, source, target, move))
    return pieces[0] if len(pieces) == 1 else jnp.concatenate(pieces)


def pair_step_of(own_frames, distance):
    step, rest = divmod(distance, own_frames)
    frame_parts = lax.axis_size("frame")
    return step if rest == 0 and frame_parts <= 2 * step < 2 * frame_parts else 0


def triple_from(block, source, target, distance, staged):
    own_frames = block.shape[0]
    frame_parts = lax.axis_size("frame")
    own = fetch(block, source, target, 0)
    if distance >= frame_parts * own_frames:
        return [own]
    step = pair_step_of(own_frames, distance)
    if step:
        route = [
            (source * frame_parts + z + move, target * frame_parts + z)
            for z in range(frame_parts)
            for move in (step, -step)
            if 0 <= z + move < frame_parts
        ]
        return [own, lax.ppermute(block, ("section", "frame"), route)]
    if staged:
        block, source = own, target
    return [
        own,
        shifted_from(block, source, target, distance, own),
        shifted_from(block, source, target, -distance, own),
    ]


def by_pairs(axis):
    count = lax.axis_size(axis)
    return count <= 4 and count & (count - 1) == 0


def sum_over(values, axis, beside=None):
    count = lax.axis_size(axis)
    index = lax.axis_index(axis)
    if not by_pairs(axis):
        parts = values.astype(jnp.bfloat16).reshape((count, -1) + values.shape[1:])
        parts = lax.all_to_all(parts, axis, split_axis=0, concat_axis=0, tiled=True)
        return jnp.sum(parts.astype(jnp.float32), axis=0), beside and beside(values)
    size = values.shape[0] // count
    total = lax.dynamic_slice_in_dim(values, index * size, size, 0)
    parts = [
        lax.dynamic_slice_in_dim(values, (index ^ mask) * size, size, 0).astype(jnp.bfloat16)
        for mask in range(1, count)
    ]
    other = beside and beside(parts)
    parts = [
        lax.ppermute(part, axis, [(i, i ^ mask) for i in range(count)])
        for mask, part in enumerate(parts, 1)
    ]
    if beside:
        parts = after(parts, other)
    for part in parts:
        total += part.astype(jnp.float32)
    return total, other


def gather_parts(part, axis):
    if not by_pairs(axis):
        return lax.all_gather(part, axis, axis=0, tiled=True)
    count = lax.axis_size(axis)
    index = lax.axis_index(axis)
    size = part.shape[0]
    whole = jnp.zeros((count * size,) + part.shape[1:], part.dtype)
    whole = lax.dynamic_update_slice_in_dim(whole, part, index * size, 0)
    for mask in range(1, count):
        got = lax.ppermute(part, axis, [(i, i ^ mask) for i in range(count)])
        whole = lax.dynamic_update_slice_in_dim(whole, got, (index ^ mask) * size, 0)
    return whole


def after(values, *others):
    return list(lax.optimization_barrier((tuple(values), others))[0])


def shifted_chains(block_input, cotangent, taps_space, taps_time):
    own_frames = block_input.shape[0]
    section_count = lax.axis_size("section")
    chains = 1 if own_frames % 2 else 2
    x_got = swap_edges(edges_of(block_input, lax.axis_size("row")))
    top = section_count - 1

    def triples(blocks, source, target):
        dilation = 2**target
        if dilation % chains == 0:
            step = pair_step_of(own_frames // chains, dilation // chains)
            early = early_half(step) if step else None
            return [
                (triple_from(block, source, target, dilation // chains, False), early)
                for block in blocks
            ]
        even, odd = blocks
        own_even = fetch(even, source, target, 0)
        next_even = shifted_from(even, source, target, (dilation + 1) // 2, own_even)
        own_odd = fetch(odd, source, target, 0)
        last_odd = shifted_from(odd, source, target, -((dilation + 1) // 2), own_odd)
        same_odd = shifted_from(odd, source, target, (dilation - 1) // 2, own_odd)
        same_even = shifted_from(even, source, target, -((dilation - 1) // 2), own_even)
        return [([own_even, same_odd, last_odd], None), ([own_odd, next_even, same_even], None)]

    everywhere = tuple(range(section_count))
    x_rows, slopes, actives = forward(block_input, x_got, taps_space, chains, everywhere)
    ready = triples(split_frames(cotangent, chains), top, top)
    grads = None
    results = []
    for owner in reversed(range(section_count)):
        groups = [[chain] for chain in range(chains)] if owner else [list(range(chains))]
        pre, outgoing = [], []
        for group in groups:
            mine = [ready[chain] for chain in group]
            if outgoing or results:
                earlier = outgoing or results[-1]
                mine = [(after(blocks, *earlier), early) for blocks, early in mine]
            group_pre, edges = temporal(owner, mine, [slopes[chain] for chain in group], taps_time)
            pre += group_pre
            if owner:
                heres = [blocks[0] for blocks, _ in mine]
                got = swap_edges(edges)
                outgoing += branches(owner, group_pre, got, heres, taps_space)
        inputs = after(pre, *outgoing) if owner else pre
        grads = kernel_grads(owner, x_rows, inputs, actives, ready, grads)
        if owner:
            results.append(outgoing)
            ready = triples(outgoing, owner, owner - 1)

    def finish(lasts, parts):
        section_index = lax.axis_index("section")
        own = results[0] if results else lasts
        for position, values in enumerate((results + [lasts])[1:], 1):
            own = [
                jnp.where(section_index == top - position, new, old)
                for new, old in zip(values, own)
            ]
        return jnp.stack(own, 1).reshape(block_input.shape)

    return grads, (pre, edges, [blocks[0] for blocks, _ in ready]), finish


def sum_kernels(grads, first_beside, then_beside):
    channels = grads.shape[-1]
    eighth = 12 * channels // 8
    pieces = grads.reshape(8, eighth, channels)
    half = jax.ShapeDtypeStruct((4, eighth, channels), jnp.bfloat16)
    part = jax.ShapeDtypeStruct((eighth, channels), jnp.bfloat16)
    wide = jax.ShapeDtypeStruct((eighth, channels), jnp.float32)

    def other_half(pieces_ref, out_ref):
        start = (1 - lax.axis_index("row")) * 4
        out_ref[...] = pieces_ref[pl.ds(start, 4)].astype(jnp.bfloat16)

    def add_half(pieces_ref, got_ref, *out_refs):
        start = lax.axis_index("row") * 4
        for mask, ref in enumerate(out_refs):
            at = lax.axis_index("frame") ^ mask
            ref[...] = (pieces_ref[start + at] + got_ref[at].astype(jnp.float32)).astype(ref.dtype)

    def add_parts(*refs):
        refs[-1][...] = sum(ref[...].astype(jnp.float32) for ref in refs[:-1]).astype(jnp.bfloat16)

    def line_parts(*refs):
        for mask, ref in enumerate(refs[:-1]):
            refs[-1][lax.axis_index("frame") ^ mask] = ref[...]

    def widen(mine_ref, other_ref, space_ref, time_ref):
        for row, (low, high) in enumerate(((mine_ref, other_ref), (other_ref, mine_ref))):

            @pl.when(lax.axis_index("row") == row)
            def _():
                space_ref[:4] = low[...].astype(jnp.float32)
                space_ref[4:] = high[:2].astype(jnp.float32)
                time_ref[...] = high[2:].astype(jnp.float32)

    def over_frame(block, mask):
        return lax.ppermute(block, "frame", [(i, i ^ mask) for i in range(4)])

    swap = [(0, 1), (1, 0)]
    got = lax.ppermute(call(other_half, [half], [pieces], 0)[0], "row", swap)
    own, *parts = call(add_half, [wide] + [part] * 3, [pieces, got], 0)
    extra = then_beside(parts)
    came = [over_frame(block, mask) for mask, block in enumerate(parts, 1)]
    own = call(add_parts, [part], [own, *after(came, extra)], 0)[0]
    came = [over_frame(own, mask) for mask in range(1, 4)]
    mine = call(line_parts, [half], [own, *came], 0)[0]
    other = lax.ppermute(mine, "row", swap)
    outs = [
        jax.ShapeDtypeStruct((6, eighth, channels), jnp.float32),
        jax.ShapeDtypeStruct((2, eighth, channels), jnp.float32),
    ]
    space, time = call(widen, outs, [mine, other], 0)
    return space, time, extra


def dealt_chains(block_input, cotangent, taps_space, taps_time):
    def place():
        return lax.axis_index("frame")

    def even():
        return (place() % 2 == 0).astype(jnp.float32)

    def odd():
        return (place() % 2).astype(jnp.float32)

    def low():
        return (place() < 2).astype(jnp.float32)

    def outer():
        return (place() == 0) | (place() == 3)

    def inner():
        return (place() == 1) | (place() == 2)

    def send(block, *hops):
        route = [(a * 4 + i, b * 4 + j) for a, b, moves in hops for i, j in moves]
        return lax.ppermute(block, ("section", "frame"), route)

    def back(moves):
        return [(j, i) for i, j in moves]

    stay = [(i, i) for i in range(4)]
    deal = {
        2: ([(0, 0), (1, 2), (2, 1), (3, 3)], [(0, 1), (1, 3), (2, 0), (3, 2)]),
        1: ([(0, 1), (1, 0), (2, 2), (3, 3)], [(0, 0), (1, 1), (2, 3), (3, 2)]),
    }
    edges, block_input = prepare(block_input)
    x_got = swap_edges(edges)

    def step(owner, triples, slopes, picks):
        pre, edges = temporal(owner, triples, slopes, taps_time)
        heres = [blocks[0] for blocks, _ in triples]
        outs = split_branches(owner, pre, edges, heres, taps_space, picks)
        return after(pre, *outs), outs

    x_own, slopes_own, actives_own = forward(block_input, x_got, taps_space, 2, (0, 3))
    ready = [([block], None) for block in frame_by_frame(cotangent)]
    pre, tops = step(
        3, ready, slopes_own, [lambda: place() < 2, lambda: place() >= 2]
    )
    first, second = (send(block, (3, 2, deal[2][k])) for k, block in enumerate(tops))
    x_dealt = [
        send(block, *((s, s, deal[s][k]) for s in (1, 2)))
        for k, block in enumerate(frames_to_deal(block_input, x_got))
    ]
    grads = kernel_grads(3, x_own, pre, actives_own, ready, None)
    x_moved, slopes, actives = forward(
        block_input, x_got, taps_space, 2, (1, 2), x_dealt
    )

    ready = [([first, second], even), ([second, first], odd)]
    pre, outs = step(2, ready, slopes, [outer, inner, 0, 1])
    ends, others, *results = outs
    end = send(ends, (2, 1, stay))
    other = send(others, (2, 1, stay))
    cross = send(others, (2, 1, [(i, i ^ 2) for i in range(4)]))
    grads = kernel_grads(2, x_moved, pre, actives, ready, grads)

    ready = [([cross, other, end], low), ([end, cross], low)]
    pre, (middles, ends) = step(1, ready, slopes, [0, 1])
    results += [middles, ends]
    pieces = [
        send(ends, (1, 0, stay)),
        send(ends, (1, 0, [(1, 0), (2, 3)])),
        send(middles, (1, 0, stay)),
        send(middles, (1, 0, [(0, 1), (1, 2)])),
        send(middles, (1, 0, [(2, 1), (3, 2)])),
    ]
    grads = kernel_grads(1, x_moved, pre, actives, ready, grads)
    returned = [
        send(block, *((s, s, back(deal[s][k])) for s in (1, 2)))
        for k, block in enumerate(after(to_return(results), *pieces[:2]))
    ]
    before, one, two, later = line_up(after(pieces, *returned))
    ready = [([one, two, before], None), ([two, later, one], None)]
    pre, edges = temporal(0, ready, slopes_own, taps_time)
    grads = kernel_grads(0, x_own, pre, actives_own, ready, grads)

    def finish(lasts, parts):
        return own_result(tops, returned, lasts)

    return grads, (pre, edges, [one, two]), finish


def section_run(x_saved, cotangent, w_spatial, w_temporal):
    block_input = x_saved[0]
    taps_space = w_spatial[0]
    taps_time = w_temporal[0]
    channels = block_input.shape[-1]
    row_parts = lax.axis_size("row")
    shape = (lax.axis_size("section"), lax.axis_size("frame"), row_parts, block_input.shape[0])
    dealt = shape == (4, 4, 2, 2) and (12 * channels) % 128 == 0
    chains = dealt_chains if dealt else shifted_chains
    grads, (pre, edges, heres), finish = chains(block_input, cotangent, taps_space, taps_time)

    def last_branch(parts):
        return finish(branches(0, pre, swap_edges(after(edges, parts)), heres, taps_space), parts)

    if dealt:
        lasts = split_branches(0, pre, edges, heres, taps_space, [0, 1])

        def result(parts):
            return finish(after(lasts, *parts), parts)

        space, time, own = sum_kernels(grads, lasts, result)
        return (
            own[None],
            space.reshape((1, 3, 3, channels, channels)),
            time.reshape((1, 3, channels, channels)),
        )
    total, _ = sum_over(grads.reshape(-1, channels), "row")

    total, own = sum_over(total, "frame", last_branch)
    total = gather_parts(total.astype(jnp.bfloat16), "frame")
    split = 9 * channels
    if row_parts == 2:
        first = lax.axis_index("row") == 0
        other = lax.ppermute(total, "row", [(0, 1), (1, 0)])
        rest = split - total.shape[0]
        space = jnp.where(
            first,
            jnp.concatenate([total, other[:rest]]),
            jnp.concatenate([other, total[:rest]]),
        )
        time = jnp.where(first, other[rest:], total[rest:])
    else:
        total = gather_parts(total, "row")
        space, time = total[:split], total[split:]
    return (
        own[None],
        space.astype(jnp.float32).reshape((1, 3, 3, channels, channels)),
        time.astype(jnp.float32).reshape((1, 3, channels, channels)),
    )


def solution(mesh):
    return jax.shard_map(
        section_run,
        mesh=mesh,
        in_specs=(
            P("section", "frame", "row", None, None),
            P("frame", "row", None, None),
            P("section", None, None, None, None),
            P("section", None, None, None),
        ),
        out_specs=(
            P("section", "frame", "row", None, None),
            P("section", None, None, None, None),
            P("section", None, None, None),
        ),
        check_vma=False,
    )
```

```python
import jax
import jax.numpy as jnp
from jax import lax
from jax.experimental import pallas as pl
from jax.experimental.pallas import tpu as pltpu
from jax.sharding import PartitionSpec as P

VMEM_LIMIT = 16 * 1024 * 1024
NT = (((1,), (1,)), ((), ()))
NN = (((1,), (0,)), ((), ()))
TN = (((0,), (0,)), ((), ()))


def mul(a, b, how):
    return lax.dot_general(a, b, how, preferred_element_type=jnp.float32)


def call(body, outs, args, flops, loose=False, aliases=None):
    moved = sum(a.size * a.dtype.itemsize for a in (*args, *outs))
    return pl.pallas_call(
        body,
        out_shape=outs,
        input_output_aliases=aliases or {},
        in_specs=[pl.BlockSpec() if loose else pl.BlockSpec(memory_space=pltpu.VMEM) for _ in args],
        out_specs=[pl.BlockSpec(memory_space=pltpu.VMEM) for _ in outs],
        compiler_params=pltpu.CompilerParams(vmem_limit_bytes=VMEM_LIMIT),
        cost_estimate=pl.CostEstimate(flops=1, bytes_accessed=1, transcendentals=0),
    )(*args)


def flat(values):
    return values.reshape(-1, values.shape[-1])


def row_sides(got, row_count):
    if len(got) == 1:
        first = (lax.axis_index("row") == 0).astype(jnp.float32)
        rows = got[0].astype(jnp.float32)
        return (rows * (1.0 - first)).astype(jnp.bfloat16), (rows * first).astype(jnp.bfloat16)
    return got


def moved_rows(cells, above, below):
    return (
        flat(jnp.concatenate([above, cells[:, :-1]], axis=1)),
        flat(cells),
        flat(jnp.concatenate([cells[:, 1:], below], axis=1)),
    )


def moved_cols(values, step, col_count):
    count, lanes = values.shape
    shape = (count // col_count, col_count, lanes)
    col = lax.broadcasted_iota(jnp.int32, shape, 1).reshape(count, lanes)
    if step == 1:
        return jnp.where(col == col_count - 1, 0.0, pltpu.roll(values, count - 1, 0))
    return jnp.where(col == 0, 0.0, pltpu.roll(values, 1, 0))


def edges_of(cells, row_parts):
    head, tail = cells[:, :1], cells[:, -1:]
    if row_parts == 2:
        first = (lax.axis_index("row") == 0).astype(jnp.float32)
        return [(tail.astype(jnp.float32) * first + head.astype(jnp.float32) * (1.0 - first)).astype(jnp.bfloat16)]
    return [head, tail]


def swap_edges(edges):
    count = lax.axis_size("row")
    if count == 2:
        return [lax.ppermute(edges[0], "row", [(0, 1), (1, 0)])]
    head, tail = edges
    if count == 1:
        return [jnp.zeros_like(head), jnp.zeros_like(head)]
    return [
        lax.ppermute(tail, "row", [(i, i + 1) for i in range(count - 1)]),
        lax.ppermute(head, "row", [(i + 1, i) for i in range(count - 1)]),
    ]


def split_frames(values, chains):
    if chains == 1:
        return [values]
    pairs = values.reshape((values.shape[0] // chains, chains) + values.shape[1:])
    return [pairs[:, at] for at in range(chains)]


def put_picked(out_refs, picks, chain, put):
    for ref, pick in zip(out_refs, picks):
        if callable(pick):
            wanted = pick() if chain == 0 else jnp.logical_not(pick())
            pl.when(wanted)(lambda ref=ref: put(ref))
        elif pick == chain:
            put(ref)


def split_branches(owner, grads_pre, edges, heres, taps_space, picks):
    part = heres[0].shape
    _, rows, cols, channels = part
    count = len(heres)

    def wide(sides, taps):
        sums = mul(sides, taps, NT)
        return (
            moved_cols(sums[:, :channels], 1, cols)
            + sums[:, channels : 2 * channels]
            + moved_cols(sums[:, 2 * channels :], -1, cols)
        )

    def rounded(branch, here):
        branch = branch.astype(jnp.bfloat16).astype(jnp.float32)
        return (here.astype(jnp.float32) + branch).astype(jnp.bfloat16)

    def inner(*refs):
        @pl.when(lax.axis_index("section") == owner)
        def _():
            w_ref = refs[2 * count]
            out_refs = refs[2 * count + 1 : -1]
            taps = jnp.concatenate(
                [jnp.concatenate([w_ref[2 - i, j] for i in range(3)], axis=1) for j in range(3)],
                axis=0,
            )
            nothing = jnp.zeros((1, 1, cols, channels), jnp.bfloat16)
            for chain in range(count):
                sides = jnp.concatenate(moved_rows(refs[chain][...], nothing, nothing), axis=1)
                branch = wide(sides, taps)
                refs[-1][chain] = branch[(rows - 1) * cols :]
                refs[-1][count + chain] = branch[:cols]
                out = rounded(branch, flat(refs[count + chain][...])).reshape(part)
                put_picked(
                    out_refs, picks, chain, lambda ref, out=out: ref.__setitem__(..., out)
                )

    def outer(*refs):
        @pl.when(lax.axis_index("section") == owner)
        def _():
            row = lax.axis_index("row")
            at = (1 - row) * (rows - 1)
            partial_ref, got_ref, *here_refs = refs[len(picks) : len(picks) + 2 + count]
            w_ref = refs[len(picks) + 2 + count]
            out_refs = refs[len(picks) + 3 + count :]
            taps = jnp.concatenate([w_ref[2 * row, j] for j in range(3)], axis=0)
            for chain in range(count):
                branch = partial_ref[row * count + chain] + wide(got_ref[chain, 0], taps)
                out = rounded(branch, here_refs[chain][0, at])
                put_picked(
                    out_refs, picks, chain, lambda ref, out=out: ref.__setitem__((0, at), out)
                )

    outs = [jax.ShapeDtypeStruct(part, jnp.bfloat16)] * len(picks)
    rim = jax.ShapeDtypeStruct((2 * count, cols, channels), jnp.float32)
    got = swap_edges(edges)
    *begun, partial = call(inner, outs + [rim], [*grads_pre, *heres, taps_space], 0)
    args = [*begun, partial, *got, *heres, taps_space]
    return call(outer, outs, args, 0, aliases={k: k for k in range(len(picks))})


def windows(cells, rows):
    return jnp.concatenate([flat(cells[:, i : i + rows]) for i in range(3)], axis=1)


def is_one_of(section, sections):
    found = section == sections[0]
    for other in sections[1:]:
        found |= section == other
    return found


def forward(block_input, got, taps_space, chains, sections, dealt=()):
    frames, rows, cols, channels = block_input.shape
    part = (frames // chains, rows, cols, channels)
    args = list(dealt) or [block_input, *got]

    def body(*refs):
        section = lax.axis_index("section")
        pl.when(is_one_of(section, sections))(lambda: work(section, *refs))

    def work(section, *refs):
        w_ref, x_ref = refs[len(args) : len(args) + 2]
        slope_refs = refs[len(args) + 2 : len(args) + 2 + chains]
        active_refs = refs[len(args) + 2 + chains :]
        if dealt:
            first = jnp.where(section == 1, lax.axis_index("frame") % 2, 0)
            x_ref[first] = refs[0][0]
            x_ref[1 - first] = refs[1][0]
        else:
            above, below = row_sides([ref[...] for ref in refs[1 : len(args)]], rows)
            x_ref[...] = jnp.concatenate([above, refs[0][...], below], axis=1)
        taps = jnp.concatenate(
            [jnp.concatenate([w_ref[i, j] for j in range(3)], axis=1) for i in range(3)], axis=0
        )
        sums = mul(windows(x_ref[...], rows), taps, NN)
        pre_act = (
            moved_cols(sums[:, :channels], -1, cols)
            + sums[:, channels : 2 * channels]
            + moved_cols(sums[:, 2 * channels :], 1, cols)
        )
        sigma = jax.nn.sigmoid(pre_act)
        slope = (sigma * (1.0 + pre_act * (1.0 - sigma))).reshape(block_input.shape)
        active = (pre_act * sigma).astype(jnp.bfloat16).reshape(block_input.shape)
        for ref, values in zip(slope_refs, split_frames(slope, chains)):
            ref[...] = values
        for ref, values in zip(active_refs, split_frames(active, chains)):
            ref[...] = values

    outs = [jax.ShapeDtypeStruct((frames, rows + 2, cols, channels), jnp.bfloat16)]
    outs += [jax.ShapeDtypeStruct(part, jnp.float32)] * chains
    outs += [jax.ShapeDtypeStruct(part, jnp.bfloat16)] * chains
    outs = call(body, outs, [*args, taps_space], 18 * block_input.size * channels)
    return outs[0], outs[1 : 1 + chains], outs[1 + chains :]


def early_half(distance_step):
    return lambda: (lax.axis_index("frame") < lax.axis_size("frame") - distance_step).astype(
        jnp.float32
    )


def mixed(early, later, earlier):
    return early * later.astype(jnp.float32) + (1.0 - early) * earlier.astype(jnp.float32)


def temporal(owner, triples, slopes, taps_time):
    row_parts = lax.axis_size("row")
    part = slopes[0].shape
    channels = part[-1]
    edges = 1 if row_parts == 2 else 2
    sizes = [len(blocks) for blocks, _ in triples]

    def body(*refs):
        @pl.when(lax.axis_index("section") == owner)
        def _():
            at = 0
            w_ref = refs[sum(sizes) + len(slopes)]
            outs = refs[sum(sizes) + len(slopes) + 1 :]
            for chain, size in enumerate(sizes):
                blocks = [flat(ref[...]) for ref in refs[at : at + size]]
                at += size
                taps = [w_ref[1]]
                early = triples[chain][1]
                if size > 1 and early is None:
                    taps += [w_ref[0], w_ref[2]]
                elif size > 1:
                    taps.append(mixed(early(), w_ref[0], w_ref[2]).astype(jnp.bfloat16))
                    taps.append(mixed(early(), w_ref[2], w_ref[0]).astype(jnp.bfloat16))
                taps = taps[:size]
                sums = mul(jnp.concatenate(blocks, axis=1), jnp.concatenate(taps, axis=1), NT)
                back_act = sums.astype(jnp.bfloat16).astype(jnp.float32)
                slope = flat(refs[sum(sizes) + chain][...])
                grad_pre = (back_act * slope).astype(jnp.bfloat16).reshape(part)
                outs[chain][...] = grad_pre
                for ref, edge in zip(outs[len(slopes) :], edges_of(grad_pre, row_parts)):
                    ref[chain * part[0] : (chain + 1) * part[0]] = edge

    outs = [jax.ShapeDtypeStruct(part, jnp.bfloat16)] * len(slopes)
    outs += [
        jax.ShapeDtypeStruct((part[0] * len(slopes), 1) + part[2:], jnp.bfloat16)
    ] * edges
    args = [block for blocks, _ in triples for block in blocks] + list(slopes) + [taps_time]
    outs = call(body, outs, args, 6 * sum(s.size for s in slopes) * channels)
    return outs[: len(slopes)], outs[len(slopes) :]


def branches(owner, grads_pre, got, heres, taps_space, picks=None):
    part = heres[0].shape
    _, rows, cols, channels = part
    count = len(heres)
    picks = picks or list(range(count))

    def body(*refs):
        @pl.when(lax.axis_index("section") == owner)
        def _():
            out_refs = refs[2 * count + len(got) + 1 :]
            got_refs = refs[count : count + len(got)]
            here_refs = refs[count + len(got) : 2 * count + len(got)]
            w_ref = refs[2 * count + len(got)]
            taps = jnp.concatenate(
                [jnp.concatenate([w_ref[2 - i, j] for i in range(3)], axis=1) for j in range(3)],
                axis=0,
            )
            for chain in range(count):
                frames = slice(chain * part[0], (chain + 1) * part[0])
                above, below = row_sides([ref[frames] for ref in got_refs], rows)
                sides = jnp.concatenate(moved_rows(refs[chain][...], above, below), axis=1)
                sums = mul(sides, taps, NT)
                branch = (
                    moved_cols(sums[:, :channels], 1, cols)
                    + sums[:, channels : 2 * channels]
                    + moved_cols(sums[:, 2 * channels :], -1, cols)
                )
                branch = branch.astype(jnp.bfloat16).astype(jnp.float32)
                here = flat(here_refs[chain][...]).astype(jnp.float32)
                out = (here + branch).astype(jnp.bfloat16).reshape(part)
                for ref, pick in zip(out_refs, picks):
                    if callable(pick):
                        wanted = pick() if chain == 0 else jnp.logical_not(pick())
                        pl.when(wanted)(lambda ref=ref, out=out: ref.__setitem__(..., out))
                    elif pick == chain:
                        ref[...] = out

    outs = [jax.ShapeDtypeStruct(part, jnp.bfloat16)] * len(picks)
    args = [*grads_pre, *got, *heres, taps_space]
    return call(body, outs, args, 18 * sum(h.size for h in heres) * channels)


def kernel_grads(owner, x_rows, grads_pre, actives, triples, before):
    _, rows, cols, channels = x_rows.shape
    rows -= 2
    chains = len(actives)

    def body(*refs):
        section = lax.axis_index("section")
        out_ref = refs[-1]

        if before is not None:

            @pl.when(section != owner)
            def _():
                out_ref[...] = refs[-2][...]

        @pl.when(section == owner)
        def _():
            sides = [windows(cells, rows) for cells in split_frames(refs[0][...], chains)]
            pre = []
            time = [jnp.zeros((channels, channels), jnp.float32)] * 3
            at = 1 + 2 * chains
            for chain, (blocks, early) in enumerate(triples):
                mid = flat(refs[1 + chain][...])
                wide = mid.astype(jnp.float32)
                left = moved_cols(wide, 1, cols).astype(jnp.bfloat16)
                right = moved_cols(wide, -1, cols).astype(jnp.bfloat16)
                pre.append(jnp.concatenate([left, mid, right], axis=1))
                size = len(blocks)
                values = jnp.concatenate([flat(ref[...]) for ref in refs[at : at + size]], axis=1)
                at += size
                product = mul(flat(refs[1 + chains + chain][...]), values, TN)
                terms = [product[:, k * channels : (k + 1) * channels] for k in range(size)]
                time[1] = time[1] + terms[0]
                if size > 1 and early is None:
                    time[0] = time[0] + terms[1]
                    time[2] = time[2] + terms[2]
                elif size > 1:
                    share = early()
                    other = terms[2] if size == 3 else jnp.zeros_like(terms[1])
                    time[0] = time[0] + mixed(share, terms[1], other)
                    time[2] = time[2] + mixed(share, other, terms[1])
            space = mul(jnp.concatenate(sides), jnp.concatenate(pre), TN)
            for i in range(3):
                for j in range(3):
                    out_ref[3 * i + j] = space[
                        i * channels : (i + 1) * channels, j * channels : (j + 1) * channels
                    ]
            for k in range(3):
                out_ref[9 + k] = time[k]

    args = [x_rows, *grads_pre, *actives]
    args += [block for blocks, _ in triples for block in blocks]
    if before is not None:
        args.append(before)
    outs = [jax.ShapeDtypeStruct((12, channels, channels), jnp.float32)]
    return call(body, outs, args, 24 * x_rows.size * channels)[0]


def place_first(section):
    place = lax.axis_index("frame")
    return jnp.where(section == 2, place // 2, jnp.where((place == 0) | (place == 3), 1, 0))


def prepare(block_input):
    row_parts = lax.axis_size("row")
    frames, rows, cols, channels = block_input.shape
    edge_count = 1 if row_parts == 2 else 2

    def body(x_ref, *out_refs):
        for ref, edge in zip(out_refs, edges_of(x_ref[...], row_parts)):
            ref[...] = edge
        out_refs[edge_count][...] = x_ref[...]

    outs = [jax.ShapeDtypeStruct((frames, 1, cols, channels), jnp.bfloat16)] * edge_count
    outs += [jax.ShapeDtypeStruct(block_input.shape, jnp.bfloat16)]
    outs = call(body, outs, [block_input], 0)
    return outs[:edge_count], outs[edge_count]


def frame_by_frame(values):
    def body(ref, *out_refs):
        for frame, out_ref in enumerate(out_refs):
            out_ref[...] = ref[frame : frame + 1]

    out = jax.ShapeDtypeStruct((1,) + values.shape[1:], values.dtype)
    return call(body, [out] * values.shape[0], [values], 0)


def frames_to_deal(block_input, got):
    _, rows, cols, channels = block_input.shape

    def body(*refs):
        section = lax.axis_index("section")

        @pl.when(is_one_of(section, (1, 2)))
        def _():
            above, below = row_sides([ref[...] for ref in refs[1 : 1 + len(got)]], rows)
            cells = jnp.concatenate([above, refs[0][...], below], axis=1)
            first = place_first(section)
            for frame in range(2):

                @pl.when(first == frame)
                def _():
                    refs[-2][...] = cells[frame : frame + 1]
                    refs[-1][...] = cells[1 - frame : 2 - frame]

    outs = [jax.ShapeDtypeStruct((1, rows + 2, cols, channels), jnp.bfloat16)] * 2
    return call(body, outs, [block_input, *got], 0)


def line_up(pieces):
    table = ((None, 0, 3, 2), (0, 1, 2, 3), (1, 2, 3, 0), (2, 1, 0, None))

    def body(*refs):
        for place, order in enumerate(table):

            @pl.when((lax.axis_index("section") == 0) & (lax.axis_index("frame") == place))
            def _():
                for ref, at in zip(refs[len(pieces) :], order):
                    ref[...] = jnp.zeros(ref.shape, ref.dtype) if at is None else refs[at][...]

    return call(body, [jax.ShapeDtypeStruct(pieces[0].shape, jnp.bfloat16)] * 4, pieces, 0)


def to_return(results):
    def body(*refs):
        section = lax.axis_index("section")
        even = lax.axis_index("frame") % 2 == 0
        cases = ((section == 2, 0, 1), ((section == 1) & even, 2, 3))
        for wanted, one, two in (*cases, ((section == 1) & jnp.logical_not(even), 3, 2)):

            @pl.when(wanted)
            def _():
                refs[4][...] = refs[one][...]
                refs[5][...] = refs[two][...]

    outs = [jax.ShapeDtypeStruct(results[0].shape, jnp.bfloat16)] * 2
    return call(body, outs, results, 0, True)


def own_result(tops, returned, lasts):
    shape = (2,) + lasts[0].shape[1:]

    def body(*refs):
        section = lax.axis_index("section")
        place = lax.axis_index("frame")
        out_ref = refs[-1]

        @pl.when(section == 3)
        def _():
            out_ref[place // 2] = refs[0][0]
            out_ref[1 - place // 2] = refs[1][0]

        @pl.when(is_one_of(section, (1, 2)))
        def _():
            first = place_first(section)
            out_ref[first] = refs[2][0]
            out_ref[1 - first] = refs[3][0]

        @pl.when(section == 0)
        def _():
            out_ref[0] = refs[4][0]
            out_ref[1] = refs[5][0]

    outs = [jax.ShapeDtypeStruct(shape, jnp.bfloat16)]
    return call(body, outs, [*tops, *returned, *lasts], 0, True)[0]


def fetch(block, source, target, frame_step):
    frame_parts = lax.axis_size("frame")
    route = [
        (source * frame_parts + z + frame_step, target * frame_parts + z)
        for z in range(frame_parts)
        if 0 <= z + frame_step < frame_parts
    ]
    if not route:
        return jnp.zeros_like(block)
    if source == target and frame_step == 0:
        return block
    return lax.ppermute(block, ("section", "frame"), route)


def shifted_from(block, source, target, offset, unmoved=None):
    own_frames = block.shape[0]
    step, rest = divmod(offset, own_frames)
    pieces = []
    for frames, move in ((slice(rest, None), step), (slice(0, rest), step + 1)):
        piece = block[frames]
        if piece.shape[0] == 0:
            continue
        if move == 0 and unmoved is not None:
            pieces.append(unmoved[frames])
        else:
            pieces.append(fetch(piece, source, target, move))
    return pieces[0] if len(pieces) == 1 else jnp.concatenate(pieces)


def pair_step_of(own_frames, distance):
    step, rest = divmod(distance, own_frames)
    frame_parts = lax.axis_size("frame")
    return step if rest == 0 and frame_parts <= 2 * step < 2 * frame_parts else 0


def triple_from(block, source, target, distance, staged):
    own_frames = block.shape[0]
    frame_parts = lax.axis_size("frame")
    own = fetch(block, source, target, 0)
    if distance >= frame_parts * own_frames:
        return [own]
    step = pair_step_of(own_frames, distance)
    if step:
        route = [
            (source * frame_parts + z + move, target * frame_parts + z)
            for z in range(frame_parts)
            for move in (step, -step)
            if 0 <= z + move < frame_parts
        ]
        return [own, lax.ppermute(block, ("section", "frame"), route)]
    if staged:
        block, source = own, target
    return [
        own,
        shifted_from(block, source, target, distance, own),
        shifted_from(block, source, target, -distance, own),
    ]


def by_pairs(axis):
    count = lax.axis_size(axis)
    return count <= 4 and count & (count - 1) == 0


def sum_over(values, axis, beside=None):
    count = lax.axis_size(axis)
    index = lax.axis_index(axis)
    if not by_pairs(axis):
        parts = values.astype(jnp.bfloat16).reshape((count, -1) + values.shape[1:])
        parts = lax.all_to_all(parts, axis, split_axis=0, concat_axis=0, tiled=True)
        return jnp.sum(parts.astype(jnp.float32), axis=0), beside and beside(values)
    size = values.shape[0] // count
    total = lax.dynamic_slice_in_dim(values, index * size, size, 0)
    parts = [
        lax.dynamic_slice_in_dim(values, (index ^ mask) * size, size, 0).astype(jnp.bfloat16)
        for mask in range(1, count)
    ]
    other = beside and beside(parts)
    parts = [
        lax.ppermute(part, axis, [(i, i ^ mask) for i in range(count)])
        for mask, part in enumerate(parts, 1)
    ]
    if beside:
        parts = after(parts, other)
    for part in parts:
        total += part.astype(jnp.float32)
    return total, other


def gather_parts(part, axis):
    if not by_pairs(axis):
        return lax.all_gather(part, axis, axis=0, tiled=True)
    count = lax.axis_size(axis)
    index = lax.axis_index(axis)
    size = part.shape[0]
    whole = jnp.zeros((count * size,) + part.shape[1:], part.dtype)
    whole = lax.dynamic_update_slice_in_dim(whole, part, index * size, 0)
    for mask in range(1, count):
        got = lax.ppermute(part, axis, [(i, i ^ mask) for i in range(count)])
        whole = lax.dynamic_update_slice_in_dim(whole, got, (index ^ mask) * size, 0)
    return whole


def after(values, *others):
    return list(lax.optimization_barrier((tuple(values), others))[0])


def shifted_chains(block_input, cotangent, taps_space, taps_time):
    own_frames = block_input.shape[0]
    section_count = lax.axis_size("section")
    chains = 1 if own_frames % 2 else 2
    x_got = swap_edges(edges_of(block_input, lax.axis_size("row")))
    top = section_count - 1

    def triples(blocks, source, target):
        dilation = 2**target
        if dilation % chains == 0:
            step = pair_step_of(own_frames // chains, dilation // chains)
            early = early_half(step) if step else None
            return [
                (triple_from(block, source, target, dilation // chains, False), early)
                for block in blocks
            ]
        even, odd = blocks
        own_even = fetch(even, source, target, 0)
        next_even = shifted_from(even, source, target, (dilation + 1) // 2, own_even)
        own_odd = fetch(odd, source, target, 0)
        last_odd = shifted_from(odd, source, target, -((dilation + 1) // 2), own_odd)
        same_odd = shifted_from(odd, source, target, (dilation - 1) // 2, own_odd)
        same_even = shifted_from(even, source, target, -((dilation - 1) // 2), own_even)
        return [([own_even, same_odd, last_odd], None), ([own_odd, next_even, same_even], None)]

    everywhere = tuple(range(section_count))
    x_rows, slopes, actives = forward(block_input, x_got, taps_space, chains, everywhere)
    ready = triples(split_frames(cotangent, chains), top, top)
    grads = None
    results = []
    for owner in reversed(range(section_count)):
        groups = [[chain] for chain in range(chains)] if owner else [list(range(chains))]
        pre, outgoing = [], []
        for group in groups:
            mine = [ready[chain] for chain in group]
            if outgoing or results:
                earlier = outgoing or results[-1]
                mine = [(after(blocks, *earlier), early) for blocks, early in mine]
            group_pre, edges = temporal(owner, mine, [slopes[chain] for chain in group], taps_time)
            pre += group_pre
            if owner:
                heres = [blocks[0] for blocks, _ in mine]
                got = swap_edges(edges)
                outgoing += branches(owner, group_pre, got, heres, taps_space)
        inputs = after(pre, *outgoing) if owner else pre
        grads = kernel_grads(owner, x_rows, inputs, actives, ready, grads)
        if owner:
            results.append(outgoing)
            ready = triples(outgoing, owner, owner - 1)

    def finish(lasts, parts):
        section_index = lax.axis_index("section")
        own = results[0] if results else lasts
        for position, values in enumerate((results + [lasts])[1:], 1):
            own = [
                jnp.where(section_index == top - position, new, old)
                for new, old in zip(values, own)
            ]
        return jnp.stack(own, 1).reshape(block_input.shape)

    return grads, (pre, edges, [blocks[0] for blocks, _ in ready]), finish


def sum_kernels(grads, first_beside, then_beside):
    channels = grads.shape[-1]
    eighth = 12 * channels // 8
    pieces = grads.reshape(8, eighth, channels)
    half = jax.ShapeDtypeStruct((4, eighth, channels), jnp.bfloat16)
    part = jax.ShapeDtypeStruct((eighth, channels), jnp.bfloat16)
    wide = jax.ShapeDtypeStruct((eighth, channels), jnp.float32)

    def other_half(pieces_ref, out_ref):
        start = (1 - lax.axis_index("row")) * 4
        out_ref[...] = pieces_ref[pl.ds(start, 4)].astype(jnp.bfloat16)

    def add_half(pieces_ref, got_ref, *out_refs):
        start = lax.axis_index("row") * 4
        for mask, ref in enumerate(out_refs):
            at = lax.axis_index("frame") ^ mask
            ref[...] = (pieces_ref[start + at] + got_ref[at].astype(jnp.float32)).astype(ref.dtype)

    def add_parts(*refs):
        refs[-1][...] = sum(ref[...].astype(jnp.float32) for ref in refs[:-1]).astype(jnp.bfloat16)

    def line_parts(*refs):
        for mask, ref in enumerate(refs[:-1]):
            refs[-1][lax.axis_index("frame") ^ mask] = ref[...]

    def widen(mine_ref, other_ref, space_ref, time_ref):
        for row, (low, high) in enumerate(((mine_ref, other_ref), (other_ref, mine_ref))):

            @pl.when(lax.axis_index("row") == row)
            def _():
                space_ref[:4] = low[...].astype(jnp.float32)
                space_ref[4:] = high[:2].astype(jnp.float32)
                time_ref[...] = high[2:].astype(jnp.float32)

    def over_frame(block, mask):
        return lax.ppermute(block, "frame", [(i, i ^ mask) for i in range(4)])

    swap = [(0, 1), (1, 0)]
    got = lax.ppermute(call(other_half, [half], [pieces], 0)[0], "row", swap)
    own, *parts = call(add_half, [wide] + [part] * 3, [pieces, got], 0)
    extra = then_beside(parts)
    came = [over_frame(block, mask) for mask, block in enumerate(parts, 1)]
    own = call(add_parts, [part], [own, *after(came, extra)], 0)[0]
    came = [over_frame(own, mask) for mask in range(1, 4)]
    mine = call(line_parts, [half], [own, *came], 0)[0]
    other = lax.ppermute(mine, "row", swap)
    outs = [
        jax.ShapeDtypeStruct((6, eighth, channels), jnp.float32),
        jax.ShapeDtypeStruct((2, eighth, channels), jnp.float32),
    ]
    space, time = call(widen, outs, [mine, other], 0)
    return space, time, extra


def dealt_chains(block_input, cotangent, taps_space, taps_time):
    def place():
        return lax.axis_index("frame")

    def even():
        return (place() % 2 == 0).astype(jnp.float32)

    def odd():
        return (place() % 2).astype(jnp.float32)

    def low():
        return (place() < 2).astype(jnp.float32)

    def outer():
        return (place() == 0) | (place() == 3)

    def inner():
        return (place() == 1) | (place() == 2)

    def send(block, *hops):
        route = [(a * 4 + i, b * 4 + j) for a, b, moves in hops for i, j in moves]
        return lax.ppermute(block, ("section", "frame"), route)

    def back(moves):
        return [(j, i) for i, j in moves]

    stay = [(i, i) for i in range(4)]
    deal = {
        2: ([(0, 0), (1, 2), (2, 1), (3, 3)], [(0, 1), (1, 3), (2, 0), (3, 2)]),
        1: ([(0, 1), (1, 0), (2, 2), (3, 3)], [(0, 0), (1, 1), (2, 3), (3, 2)]),
    }
    edges, block_input = prepare(block_input)
    x_got = swap_edges(edges)

    def step(owner, triples, slopes, picks):
        pre, edges = temporal(owner, triples, slopes, taps_time)
        heres = [blocks[0] for blocks, _ in triples]
        outs = split_branches(owner, pre, edges, heres, taps_space, picks)
        return after(pre, *outs), outs

    x_own, slopes_own, actives_own = forward(block_input, x_got, taps_space, 2, (0, 3))
    ready = [([block], None) for block in frame_by_frame(cotangent)]
    pre, tops = step(
        3, ready, slopes_own, [lambda: place() < 2, lambda: place() >= 2]
    )
    first, second = (send(block, (3, 2, deal[2][k])) for k, block in enumerate(tops))
    x_dealt = [
        send(block, *((s, s, deal[s][k]) for s in (1, 2)))
        for k, block in enumerate(frames_to_deal(block_input, x_got))
    ]
    grads = kernel_grads(3, x_own, pre, actives_own, ready, None)
    x_moved, slopes, actives = forward(
        block_input, x_got, taps_space, 2, (1, 2), x_dealt
    )

    ready = [([first, second], even), ([second, first], odd)]
    pre, outs = step(2, ready, slopes, [outer, inner, 0, 1])
    ends, others, *results = outs
    end = send(ends, (2, 1, stay))
    other = send(others, (2, 1, stay))
    cross = send(others, (2, 1, [(i, i ^ 2) for i in range(4)]))
    grads = kernel_grads(2, x_moved, pre, actives, ready, grads)

    ready = [([cross, other, end], low), ([end, cross], low)]
    pre, outs = step(1, ready, slopes, [0, 1, lambda: place() < 2, lambda: place() >= 2])
    middles, ends, ups, downs = outs
    results += [middles, ends]
    pieces = [
        send(ends, (1, 0, stay)),
        send(ups, (1, 0, [(0, 1), (1, 2), (2, 3)])),
        send(middles, (1, 0, stay)),
        send(downs, (1, 0, [(1, 0), (2, 1), (3, 2)])),
    ]
    grads = kernel_grads(1, x_moved, pre, actives, ready, grads)
    returned = [
        send(block, *((s, s, back(deal[s][k])) for s in (1, 2)))
        for k, block in enumerate(after(to_return(results), pieces[1], pieces[3]))
    ]
    before, one, two, later = line_up(after(pieces, *returned))
    ready = [([one, two, before], None), ([two, later, one], None)]
    pre, edges = temporal(0, ready, slopes_own, taps_time)
    grads = kernel_grads(0, x_own, pre, actives_own, ready, grads)

    def finish(lasts, parts):
        return own_result(tops, returned, lasts)

    return grads, (pre, edges, [one, two]), finish


def section_run(x_saved, cotangent, w_spatial, w_temporal):
    block_input = x_saved[0]
    taps_space = w_spatial[0]
    taps_time = w_temporal[0]
    channels = block_input.shape[-1]
    row_parts = lax.axis_size("row")
    shape = (lax.axis_size("section"), lax.axis_size("frame"), row_parts, block_input.shape[0])
    dealt = shape == (4, 4, 2, 2) and (12 * channels) % 128 == 0
    chains = dealt_chains if dealt else shifted_chains
    grads, (pre, edges, heres), finish = chains(block_input, cotangent, taps_space, taps_time)

    def last_branch(parts):
        return finish(branches(0, pre, swap_edges(after(edges, parts)), heres, taps_space), parts)

    if dealt:
        lasts = split_branches(0, pre, edges, heres, taps_space, [0, 1])

        def result(parts):
            return finish(after(lasts, *parts), parts)

        space, time, own = sum_kernels(grads, lasts, result)
        return (
            own[None],
            space.reshape((1, 3, 3, channels, channels)),
            time.reshape((1, 3, channels, channels)),
        )
    total, _ = sum_over(grads.reshape(-1, channels), "row")

    total, own = sum_over(total, "frame", last_branch)
    total = gather_parts(total.astype(jnp.bfloat16), "frame")
    split = 9 * channels
    if row_parts == 2:
        first = lax.axis_index("row") == 0
        other = lax.ppermute(total, "row", [(0, 1), (1, 0)])
        rest = split - total.shape[0]
        space = jnp.where(
            first,
            jnp.concatenate([total, other[:rest]]),
            jnp.concatenate([other, total[:rest]]),
        )
        time = jnp.where(first, other[rest:], total[rest:])
    else:
        total = gather_parts(total, "row")
        space, time = total[:split], total[split:]
    return (
        own[None],
        space.astype(jnp.float32).reshape((1, 3, 3, channels, channels)),
        time.astype(jnp.float32).reshape((1, 3, channels, channels)),
    )


def solution(mesh):
    return jax.shard_map(
        section_run,
        mesh=mesh,
        in_specs=(
            P("section", "frame", "row", None, None),
            P("frame", "row", None, None),
            P("section", None, None, None, None),
            P("section", None, None, None),
        ),
        out_specs=(
            P("section", "frame", "row", None, None),
            P("section", None, None, None, None),
            P("section", None, None, None),
        ),
        check_vma=False,
    )
```

```python
import jax
import jax.numpy as jnp
from jax import lax
from jax.experimental import pallas as pl
from jax.experimental.pallas import tpu as pltpu
from jax.sharding import PartitionSpec as P

VMEM_LIMIT = 16 * 1024 * 1024
NT = (((1,), (1,)), ((), ()))
NN = (((1,), (0,)), ((), ()))
TN = (((0,), (0,)), ((), ()))


def mul(a, b, how):
    return lax.dot_general(a, b, how, preferred_element_type=jnp.float32)


def call(body, outs, args, flops, loose=False, aliases=None):
    moved = sum(a.size * a.dtype.itemsize for a in (*args, *outs))
    return pl.pallas_call(
        body,
        out_shape=outs,
        input_output_aliases=aliases or {},
        in_specs=[pl.BlockSpec() if loose else pl.BlockSpec(memory_space=pltpu.VMEM) for _ in args],
        out_specs=[pl.BlockSpec(memory_space=pltpu.VMEM) for _ in outs],
        compiler_params=pltpu.CompilerParams(vmem_limit_bytes=VMEM_LIMIT),
        cost_estimate=pl.CostEstimate(flops=1, bytes_accessed=1, transcendentals=0),
    )(*args)


def flat(values):
    return values.reshape(-1, values.shape[-1])


def row_sides(got, row_count):
    if len(got) == 1:
        first = (lax.axis_index("row") == 0).astype(jnp.float32)
        rows = got[0].astype(jnp.float32)
        return (rows * (1.0 - first)).astype(jnp.bfloat16), (rows * first).astype(jnp.bfloat16)
    return got


def moved_rows(cells, above, below):
    return (
        flat(jnp.concatenate([above, cells[:, :-1]], axis=1)),
        flat(cells),
        flat(jnp.concatenate([cells[:, 1:], below], axis=1)),
    )


def moved_cols(values, step, col_count):
    count, lanes = values.shape
    shape = (count // col_count, col_count, lanes)
    col = lax.broadcasted_iota(jnp.int32, shape, 1).reshape(count, lanes)
    if step == 1:
        return jnp.where(col == col_count - 1, 0.0, pltpu.roll(values, count - 1, 0))
    return jnp.where(col == 0, 0.0, pltpu.roll(values, 1, 0))


def edges_of(cells, row_parts):
    head, tail = cells[:, :1], cells[:, -1:]
    if row_parts == 2:
        first = (lax.axis_index("row") == 0).astype(jnp.float32)
        return [(tail.astype(jnp.float32) * first + head.astype(jnp.float32) * (1.0 - first)).astype(jnp.bfloat16)]
    return [head, tail]


def swap_edges(edges):
    count = lax.axis_size("row")
    if count == 2:
        return [lax.ppermute(edges[0], "row", [(0, 1), (1, 0)])]
    head, tail = edges
    if count == 1:
        return [jnp.zeros_like(head), jnp.zeros_like(head)]
    return [
        lax.ppermute(tail, "row", [(i, i + 1) for i in range(count - 1)]),
        lax.ppermute(head, "row", [(i + 1, i) for i in range(count - 1)]),
    ]


def split_frames(values, chains):
    if chains == 1:
        return [values]
    pairs = values.reshape((values.shape[0] // chains, chains) + values.shape[1:])
    return [pairs[:, at] for at in range(chains)]


def put_picked(out_refs, picks, chain, put):
    for ref, pick in zip(out_refs, picks):
        if callable(pick):
            wanted = pick() if chain == 0 else jnp.logical_not(pick())
            pl.when(wanted)(lambda ref=ref: put(ref))
        elif pick == chain:
            put(ref)


def split_branches(owner, grads_pre, edges, heres, taps_space, picks):
    part = heres[0].shape
    _, rows, cols, channels = part
    count = len(heres)

    def wide(sides, taps):
        sums = mul(sides, taps, NT)
        return (
            moved_cols(sums[:, :channels], 1, cols)
            + sums[:, channels : 2 * channels]
            + moved_cols(sums[:, 2 * channels :], -1, cols)
        )

    def rounded(branch, here):
        branch = branch.astype(jnp.bfloat16).astype(jnp.float32)
        return (here.astype(jnp.float32) + branch).astype(jnp.bfloat16)

    def inner(*refs):
        @pl.when(lax.axis_index("section") == owner)
        def _():
            w_ref = refs[2 * count]
            out_refs = refs[2 * count + 1 : -1]
            taps = jnp.concatenate(
                [jnp.concatenate([w_ref[2 - i, j] for i in range(3)], axis=1) for j in range(3)],
                axis=0,
            )
            nothing = jnp.zeros((1, 1, cols, channels), jnp.bfloat16)
            for chain in range(count):
                sides = jnp.concatenate(moved_rows(refs[chain][...], nothing, nothing), axis=1)
                branch = wide(sides, taps)
                refs[-1][chain] = branch[(rows - 1) * cols :]
                refs[-1][count + chain] = branch[:cols]
                out = rounded(branch, flat(refs[count + chain][...])).reshape(part)
                put_picked(
                    out_refs, picks, chain, lambda ref, out=out: ref.__setitem__(..., out)
                )

    def outer(*refs):
        @pl.when(lax.axis_index("section") == owner)
        def _():
            row = lax.axis_index("row")
            at = (1 - row) * (rows - 1)
            partial_ref, got_ref, *here_refs = refs[len(picks) : len(picks) + 2 + count]
            w_ref = refs[len(picks) + 2 + count]
            out_refs = refs[len(picks) + 3 + count :]
            taps = jnp.concatenate([w_ref[2 * row, j] for j in range(3)], axis=0)
            for chain in range(count):
                branch = partial_ref[row * count + chain] + wide(got_ref[chain, 0], taps)
                out = rounded(branch, here_refs[chain][0, at])
                put_picked(
                    out_refs, picks, chain, lambda ref, out=out: ref.__setitem__((0, at), out)
                )

    outs = [jax.ShapeDtypeStruct(part, jnp.bfloat16)] * len(picks)
    rim = jax.ShapeDtypeStruct((2 * count, cols, channels), jnp.float32)
    got = swap_edges(edges)
    *begun, partial = call(inner, outs + [rim], [*grads_pre, *heres, taps_space], 0)
    args = [*begun, partial, *got, *heres, taps_space]
    return call(outer, outs, args, 0, aliases={k: k for k in range(len(picks))})


def windows(cells, rows):
    return jnp.concatenate([flat(cells[:, i : i + rows]) for i in range(3)], axis=1)


def is_one_of(section, sections):
    found = section == sections[0]
    for other in sections[1:]:
        found |= section == other
    return found


def forward(block_input, got, taps_space, chains, sections, dealt=()):
    frames, rows, cols, channels = block_input.shape
    part = (frames // chains, rows, cols, channels)
    args = list(dealt) or [block_input, *got]

    def body(*refs):
        section = lax.axis_index("section")
        pl.when(is_one_of(section, sections))(lambda: work(section, *refs))

    def work(section, *refs):
        w_ref, x_ref = refs[len(args) : len(args) + 2]
        slope_refs = refs[len(args) + 2 : len(args) + 2 + chains]
        active_refs = refs[len(args) + 2 + chains :]
        if dealt:
            first = jnp.where(section == 1, lax.axis_index("frame") % 2, 0)
            x_ref[first] = refs[0][0]
            x_ref[1 - first] = refs[1][0]
        else:
            above, below = row_sides([ref[...] for ref in refs[1 : len(args)]], rows)
            x_ref[...] = jnp.concatenate([above, refs[0][...], below], axis=1)
        taps = jnp.concatenate(
            [jnp.concatenate([w_ref[i, j] for j in range(3)], axis=1) for i in range(3)], axis=0
        )
        sums = mul(windows(x_ref[...], rows), taps, NN)
        pre_act = (
            moved_cols(sums[:, :channels], -1, cols)
            + sums[:, channels : 2 * channels]
            + moved_cols(sums[:, 2 * channels :], 1, cols)
        )
        sigma = jax.nn.sigmoid(pre_act)
        slope = (sigma * (1.0 + pre_act * (1.0 - sigma))).reshape(block_input.shape)
        active = (pre_act * sigma).astype(jnp.bfloat16).reshape(block_input.shape)
        for ref, values in zip(slope_refs, split_frames(slope, chains)):
            ref[...] = values
        for ref, values in zip(active_refs, split_frames(active, chains)):
            ref[...] = values

    outs = [jax.ShapeDtypeStruct((frames, rows + 2, cols, channels), jnp.bfloat16)]
    outs += [jax.ShapeDtypeStruct(part, jnp.float32)] * chains
    outs += [jax.ShapeDtypeStruct(part, jnp.bfloat16)] * chains
    outs = call(body, outs, [*args, taps_space], 18 * block_input.size * channels)
    return outs[0], outs[1 : 1 + chains], outs[1 + chains :]


def early_half(distance_step):
    return lambda: (lax.axis_index("frame") < lax.axis_size("frame") - distance_step).astype(
        jnp.float32
    )


def mixed(early, later, earlier):
    return early * later.astype(jnp.float32) + (1.0 - early) * earlier.astype(jnp.float32)


def temporal(owner, triples, slopes, taps_time):
    row_parts = lax.axis_size("row")
    part = slopes[0].shape
    channels = part[-1]
    edges = 1 if row_parts == 2 else 2
    sizes = [len(blocks) for blocks, _ in triples]

    def body(*refs):
        @pl.when(lax.axis_index("section") == owner)
        def _():
            at = 0
            w_ref = refs[sum(sizes) + len(slopes)]
            outs = refs[sum(sizes) + len(slopes) + 1 :]
            for chain, size in enumerate(sizes):
                blocks = [flat(ref[...]) for ref in refs[at : at + size]]
                at += size
                taps = [w_ref[1]]
                early = triples[chain][1]
                if size > 1 and early is None:
                    taps += [w_ref[0], w_ref[2]]
                elif size > 1:
                    taps.append(mixed(early(), w_ref[0], w_ref[2]).astype(jnp.bfloat16))
                    taps.append(mixed(early(), w_ref[2], w_ref[0]).astype(jnp.bfloat16))
                taps = taps[:size]
                sums = mul(jnp.concatenate(blocks, axis=1), jnp.concatenate(taps, axis=1), NT)
                back_act = sums.astype(jnp.bfloat16).astype(jnp.float32)
                slope = flat(refs[sum(sizes) + chain][...])
                grad_pre = (back_act * slope).astype(jnp.bfloat16).reshape(part)
                outs[chain][...] = grad_pre
                for ref, edge in zip(outs[len(slopes) :], edges_of(grad_pre, row_parts)):
                    ref[chain * part[0] : (chain + 1) * part[0]] = edge

    outs = [jax.ShapeDtypeStruct(part, jnp.bfloat16)] * len(slopes)
    outs += [
        jax.ShapeDtypeStruct((part[0] * len(slopes), 1) + part[2:], jnp.bfloat16)
    ] * edges
    args = [block for blocks, _ in triples for block in blocks] + list(slopes) + [taps_time]
    outs = call(body, outs, args, 6 * sum(s.size for s in slopes) * channels)
    return outs[: len(slopes)], outs[len(slopes) :]


def branches(owner, grads_pre, got, heres, taps_space, picks=None):
    part = heres[0].shape
    _, rows, cols, channels = part
    count = len(heres)
    picks = picks or list(range(count))

    def body(*refs):
        @pl.when(lax.axis_index("section") == owner)
        def _():
            out_refs = refs[2 * count + len(got) + 1 :]
            got_refs = refs[count : count + len(got)]
            here_refs = refs[count + len(got) : 2 * count + len(got)]
            w_ref = refs[2 * count + len(got)]
            taps = jnp.concatenate(
                [jnp.concatenate([w_ref[2 - i, j] for i in range(3)], axis=1) for j in range(3)],
                axis=0,
            )
            for chain in range(count):
                frames = slice(chain * part[0], (chain + 1) * part[0])
                above, below = row_sides([ref[frames] for ref in got_refs], rows)
                sides = jnp.concatenate(moved_rows(refs[chain][...], above, below), axis=1)
                sums = mul(sides, taps, NT)
                branch = (
                    moved_cols(sums[:, :channels], 1, cols)
                    + sums[:, channels : 2 * channels]
                    + moved_cols(sums[:, 2 * channels :], -1, cols)
                )
                branch = branch.astype(jnp.bfloat16).astype(jnp.float32)
                here = flat(here_refs[chain][...]).astype(jnp.float32)
                out = (here + branch).astype(jnp.bfloat16).reshape(part)
                for ref, pick in zip(out_refs, picks):
                    if callable(pick):
                        wanted = pick() if chain == 0 else jnp.logical_not(pick())
                        pl.when(wanted)(lambda ref=ref, out=out: ref.__setitem__(..., out))
                    elif pick == chain:
                        ref[...] = out

    outs = [jax.ShapeDtypeStruct(part, jnp.bfloat16)] * len(picks)
    args = [*grads_pre, *got, *heres, taps_space]
    return call(body, outs, args, 18 * sum(h.size for h in heres) * channels)


def kernel_grads(owner, x_rows, grads_pre, actives, triples, before, halve=False):
    _, rows, cols, channels = x_rows.shape
    rows -= 2
    chains = len(actives)

    def body(*refs):
        section = lax.axis_index("section")
        refs, half_refs = (refs[:-1], refs[-1:]) if halve else (refs, ())
        out_ref = refs[-1]

        if before is not None:

            @pl.when(section != owner)
            def _():
                out_ref[...] = refs[-2][...]

        @pl.when(section == owner)
        def _():
            sides = [windows(cells, rows) for cells in split_frames(refs[0][...], chains)]
            pre = []
            time = [jnp.zeros((channels, channels), jnp.float32)] * 3
            at = 1 + 2 * chains
            for chain, (blocks, early) in enumerate(triples):
                mid = flat(refs[1 + chain][...])
                wide = mid.astype(jnp.float32)
                left = moved_cols(wide, 1, cols).astype(jnp.bfloat16)
                right = moved_cols(wide, -1, cols).astype(jnp.bfloat16)
                pre.append(jnp.concatenate([left, mid, right], axis=1))
                size = len(blocks)
                values = jnp.concatenate([flat(ref[...]) for ref in refs[at : at + size]], axis=1)
                at += size
                product = mul(flat(refs[1 + chains + chain][...]), values, TN)
                terms = [product[:, k * channels : (k + 1) * channels] for k in range(size)]
                time[1] = time[1] + terms[0]
                if size > 1 and early is None:
                    time[0] = time[0] + terms[1]
                    time[2] = time[2] + terms[2]
                elif size > 1:
                    share = early()
                    other = terms[2] if size == 3 else jnp.zeros_like(terms[1])
                    time[0] = time[0] + mixed(share, terms[1], other)
                    time[2] = time[2] + mixed(share, other, terms[1])
            space = mul(jnp.concatenate(sides), jnp.concatenate(pre), TN)
            for i in range(3):
                for j in range(3):
                    out_ref[3 * i + j] = space[
                        i * channels : (i + 1) * channels, j * channels : (j + 1) * channels
                    ]
            for k in range(3):
                out_ref[9 + k] = time[k]

        for ref in half_refs:
            start = (1 - lax.axis_index("row")) * 6
            ref[...] = out_ref[pl.ds(start, 6)].astype(jnp.bfloat16)

    args = [x_rows, *grads_pre, *actives]
    args += [block for blocks, _ in triples for block in blocks]
    if before is not None:
        args.append(before)
    outs = [jax.ShapeDtypeStruct((12, channels, channels), jnp.float32)]
    if halve:
        outs.append(jax.ShapeDtypeStruct((6, channels, channels), jnp.bfloat16))
    outs = call(body, outs, args, 24 * x_rows.size * channels)
    return outs if halve else outs[0]


def place_first(section):
    place = lax.axis_index("frame")
    return jnp.where(section == 2, place // 2, jnp.where((place == 0) | (place == 3), 1, 0))


def prepare(block_input):
    row_parts = lax.axis_size("row")
    frames, rows, cols, channels = block_input.shape
    edge_count = 1 if row_parts == 2 else 2

    def body(x_ref, *out_refs):
        for ref, edge in zip(out_refs, edges_of(x_ref[...], row_parts)):
            ref[...] = edge
        out_refs[edge_count][...] = x_ref[...]

    outs = [jax.ShapeDtypeStruct((frames, 1, cols, channels), jnp.bfloat16)] * edge_count
    outs += [jax.ShapeDtypeStruct(block_input.shape, jnp.bfloat16)]
    outs = call(body, outs, [block_input], 0)
    return outs[:edge_count], outs[edge_count]


def frame_by_frame(values):
    def body(ref, *out_refs):
        for frame, out_ref in enumerate(out_refs):
            out_ref[...] = ref[frame : frame + 1]

    out = jax.ShapeDtypeStruct((1,) + values.shape[1:], values.dtype)
    return call(body, [out] * values.shape[0], [values], 0)


def frames_to_deal(block_input, got):
    _, rows, cols, channels = block_input.shape

    def body(*refs):
        section = lax.axis_index("section")

        @pl.when(is_one_of(section, (1, 2)))
        def _():
            above, below = row_sides([ref[...] for ref in refs[1 : 1 + len(got)]], rows)
            cells = jnp.concatenate([above, refs[0][...], below], axis=1)
            first = place_first(section)
            for frame in range(2):

                @pl.when(first == frame)
                def _():
                    refs[-2][...] = cells[frame : frame + 1]
                    refs[-1][...] = cells[1 - frame : 2 - frame]

    outs = [jax.ShapeDtypeStruct((1, rows + 2, cols, channels), jnp.bfloat16)] * 2
    return call(body, outs, [block_input, *got], 0)


def line_up(pieces):
    table = ((None, 0, 3, 2), (0, 1, 2, 3), (1, 2, 3, 0), (2, 1, 0, None))

    def body(*refs):
        for place, order in enumerate(table):

            @pl.when((lax.axis_index("section") == 0) & (lax.axis_index("frame") == place))
            def _():
                for ref, at in zip(refs[len(pieces) :], order):
                    ref[...] = jnp.zeros(ref.shape, ref.dtype) if at is None else refs[at][...]

    return call(body, [jax.ShapeDtypeStruct(pieces[0].shape, jnp.bfloat16)] * 4, pieces, 0)


def to_return(results):
    def body(*refs):
        section = lax.axis_index("section")
        even = lax.axis_index("frame") % 2 == 0
        cases = ((section == 2, 0, 1), ((section == 1) & even, 2, 3))
        for wanted, one, two in (*cases, ((section == 1) & jnp.logical_not(even), 3, 2)):

            @pl.when(wanted)
            def _():
                refs[4][...] = refs[one][...]
                refs[5][...] = refs[two][...]

    outs = [jax.ShapeDtypeStruct(results[0].shape, jnp.bfloat16)] * 2
    return call(body, outs, results, 0, True)


def own_result(tops, returned, lasts):
    shape = (2,) + lasts[0].shape[1:]

    def body(*refs):
        section = lax.axis_index("section")
        place = lax.axis_index("frame")
        out_ref = refs[-1]

        @pl.when(section == 3)
        def _():
            out_ref[place // 2] = refs[0][0]
            out_ref[1 - place // 2] = refs[1][0]

        @pl.when(is_one_of(section, (1, 2)))
        def _():
            first = place_first(section)
            out_ref[first] = refs[2][0]
            out_ref[1 - first] = refs[3][0]

        @pl.when(section == 0)
        def _():
            out_ref[0] = refs[4][0]
            out_ref[1] = refs[5][0]

    outs = [jax.ShapeDtypeStruct(shape, jnp.bfloat16)]
    return call(body, outs, [*tops, *returned, *lasts], 0, True)[0]


def fetch(block, source, target, frame_step):
    frame_parts = lax.axis_size("frame")
    route = [
        (source * frame_parts + z + frame_step, target * frame_parts + z)
        for z in range(frame_parts)
        if 0 <= z + frame_step < frame_parts
    ]
    if not route:
        return jnp.zeros_like(block)
    if source == target and frame_step == 0:
        return block
    return lax.ppermute(block, ("section", "frame"), route)


def shifted_from(block, source, target, offset, unmoved=None):
    own_frames = block.shape[0]
    step, rest = divmod(offset, own_frames)
    pieces = []
    for frames, move in ((slice(rest, None), step), (slice(0, rest), step + 1)):
        piece = block[frames]
        if piece.shape[0] == 0:
            continue
        if move == 0 and unmoved is not None:
            pieces.append(unmoved[frames])
        else:
            pieces.append(fetch(piece, source, target, move))
    return pieces[0] if len(pieces) == 1 else jnp.concatenate(pieces)


def pair_step_of(own_frames, distance):
    step, rest = divmod(distance, own_frames)
    frame_parts = lax.axis_size("frame")
    return step if rest == 0 and frame_parts <= 2 * step < 2 * frame_parts else 0


def triple_from(block, source, target, distance, staged):
    own_frames = block.shape[0]
    frame_parts = lax.axis_size("frame")
    own = fetch(block, source, target, 0)
    if distance >= frame_parts * own_frames:
        return [own]
    step = pair_step_of(own_frames, distance)
    if step:
        route = [
            (source * frame_parts + z + move, target * frame_parts + z)
            for z in range(frame_parts)
            for move in (step, -step)
            if 0 <= z + move < frame_parts
        ]
        return [own, lax.ppermute(block, ("section", "frame"), route)]
    if staged:
        block, source = own, target
    return [
        own,
        shifted_from(block, source, target, distance, own),
        shifted_from(block, source, target, -distance, own),
    ]


def by_pairs(axis):
    count = lax.axis_size(axis)
    return count <= 4 and count & (count - 1) == 0


def sum_over(values, axis, beside=None):
    count = lax.axis_size(axis)
    index = lax.axis_index(axis)
    if not by_pairs(axis):
        parts = values.astype(jnp.bfloat16).reshape((count, -1) + values.shape[1:])
        parts = lax.all_to_all(parts, axis, split_axis=0, concat_axis=0, tiled=True)
        return jnp.sum(parts.astype(jnp.float32), axis=0), beside and beside(values)
    size = values.shape[0] // count
    total = lax.dynamic_slice_in_dim(values, index * size, size, 0)
    parts = [
        lax.dynamic_slice_in_dim(values, (index ^ mask) * size, size, 0).astype(jnp.bfloat16)
        for mask in range(1, count)
    ]
    other = beside and beside(parts)
    parts = [
        lax.ppermute(part, axis, [(i, i ^ mask) for i in range(count)])
        for mask, part in enumerate(parts, 1)
    ]
    if beside:
        parts = after(parts, other)
    for part in parts:
        total += part.astype(jnp.float32)
    return total, other


def gather_parts(part, axis):
    if not by_pairs(axis):
        return lax.all_gather(part, axis, axis=0, tiled=True)
    count = lax.axis_size(axis)
    index = lax.axis_index(axis)
    size = part.shape[0]
    whole = jnp.zeros((count * size,) + part.shape[1:], part.dtype)
    whole = lax.dynamic_update_slice_in_dim(whole, part, index * size, 0)
    for mask in range(1, count):
        got = lax.ppermute(part, axis, [(i, i ^ mask) for i in range(count)])
        whole = lax.dynamic_update_slice_in_dim(whole, got, (index ^ mask) * size, 0)
    return whole


def after(values, *others):
    return list(lax.optimization_barrier((tuple(values), others))[0])


def shifted_chains(block_input, cotangent, taps_space, taps_time):
    own_frames = block_input.shape[0]
    section_count = lax.axis_size("section")
    chains = 1 if own_frames % 2 else 2
    x_got = swap_edges(edges_of(block_input, lax.axis_size("row")))
    top = section_count - 1

    def triples(blocks, source, target):
        dilation = 2**target
        if dilation % chains == 0:
            step = pair_step_of(own_frames // chains, dilation // chains)
            early = early_half(step) if step else None
            return [
                (triple_from(block, source, target, dilation // chains, False), early)
                for block in blocks
            ]
        even, odd = blocks
        own_even = fetch(even, source, target, 0)
        next_even = shifted_from(even, source, target, (dilation + 1) // 2, own_even)
        own_odd = fetch(odd, source, target, 0)
        last_odd = shifted_from(odd, source, target, -((dilation + 1) // 2), own_odd)
        same_odd = shifted_from(odd, source, target, (dilation - 1) // 2, own_odd)
        same_even = shifted_from(even, source, target, -((dilation - 1) // 2), own_even)
        return [([own_even, same_odd, last_odd], None), ([own_odd, next_even, same_even], None)]

    everywhere = tuple(range(section_count))
    x_rows, slopes, actives = forward(block_input, x_got, taps_space, chains, everywhere)
    ready = triples(split_frames(cotangent, chains), top, top)
    grads = None
    results = []
    for owner in reversed(range(section_count)):
        groups = [[chain] for chain in range(chains)] if owner else [list(range(chains))]
        pre, outgoing = [], []
        for group in groups:
            mine = [ready[chain] for chain in group]
            if outgoing or results:
                earlier = outgoing or results[-1]
                mine = [(after(blocks, *earlier), early) for blocks, early in mine]
            group_pre, edges = temporal(owner, mine, [slopes[chain] for chain in group], taps_time)
            pre += group_pre
            if owner:
                heres = [blocks[0] for blocks, _ in mine]
                got = swap_edges(edges)
                outgoing += branches(owner, group_pre, got, heres, taps_space)
        inputs = after(pre, *outgoing) if owner else pre
        grads = kernel_grads(owner, x_rows, inputs, actives, ready, grads)
        if owner:
            results.append(outgoing)
            ready = triples(outgoing, owner, owner - 1)

    def finish(lasts, parts):
        section_index = lax.axis_index("section")
        own = results[0] if results else lasts
        for position, values in enumerate((results + [lasts])[1:], 1):
            own = [
                jnp.where(section_index == top - position, new, old)
                for new, old in zip(values, own)
            ]
        return jnp.stack(own, 1).reshape(block_input.shape)

    return grads, (pre, edges, [blocks[0] for blocks, _ in ready]), finish


def sum_kernels(grads, other, first_beside, then_beside):
    channels = grads.shape[-1]
    eighth = 12 * channels // 8
    pieces = grads.reshape(8, eighth, channels)
    other = other.reshape(4, eighth, channels)
    half = jax.ShapeDtypeStruct((4, eighth, channels), jnp.bfloat16)
    part = jax.ShapeDtypeStruct((eighth, channels), jnp.bfloat16)
    wide = jax.ShapeDtypeStruct((eighth, channels), jnp.float32)

    def add_half(pieces_ref, got_ref, *out_refs):
        start = lax.axis_index("row") * 4
        for mask, ref in enumerate(out_refs):
            at = lax.axis_index("frame") ^ mask
            ref[...] = (pieces_ref[start + at] + got_ref[at].astype(jnp.float32)).astype(ref.dtype)

    def add_parts(*refs):
        refs[-1][...] = sum(ref[...].astype(jnp.float32) for ref in refs[:-1]).astype(jnp.bfloat16)

    def line_parts(*refs):
        for mask, ref in enumerate(refs[:-1]):
            refs[-1][lax.axis_index("frame") ^ mask] = ref[...]

    def widen(mine_ref, other_ref, space_ref, time_ref):
        for row, (low, high) in enumerate(((mine_ref, other_ref), (other_ref, mine_ref))):

            @pl.when(lax.axis_index("row") == row)
            def _():
                space_ref[:4] = low[...].astype(jnp.float32)
                space_ref[4:] = high[:2].astype(jnp.float32)
                time_ref[...] = high[2:].astype(jnp.float32)

    def over_frame(block, mask):
        return lax.ppermute(block, "frame", [(i, i ^ mask) for i in range(4)])

    swap = [(0, 1), (1, 0)]
    got = lax.ppermute(other, "row", swap)
    own, *parts = call(add_half, [wide] + [part] * 3, [pieces, got], 0)
    extra = then_beside(parts)
    came = [over_frame(block, mask) for mask, block in enumerate(parts, 1)]
    own = call(add_parts, [part], [own, *after(came, extra)], 0)[0]
    came = [over_frame(own, mask) for mask in range(1, 4)]
    mine = call(line_parts, [half], [own, *came], 0)[0]
    other = lax.ppermute(mine, "row", swap)
    outs = [
        jax.ShapeDtypeStruct((6, eighth, channels), jnp.float32),
        jax.ShapeDtypeStruct((2, eighth, channels), jnp.float32),
    ]
    space, time = call(widen, outs, [mine, other], 0)
    return space, time, extra


def dealt_chains(block_input, cotangent, taps_space, taps_time):
    def place():
        return lax.axis_index("frame")

    def even():
        return (place() % 2 == 0).astype(jnp.float32)

    def odd():
        return (place() % 2).astype(jnp.float32)

    def low():
        return (place() < 2).astype(jnp.float32)

    def outer():
        return (place() == 0) | (place() == 3)

    def inner():
        return (place() == 1) | (place() == 2)

    def send(block, *hops):
        route = [(a * 4 + i, b * 4 + j) for a, b, moves in hops for i, j in moves]
        return lax.ppermute(block, ("section", "frame"), route)

    def back(moves):
        return [(j, i) for i, j in moves]

    stay = [(i, i) for i in range(4)]
    deal = {
        2: ([(0, 0), (1, 2), (2, 1), (3, 3)], [(0, 1), (1, 3), (2, 0), (3, 2)]),
        1: ([(0, 1), (1, 0), (2, 2), (3, 3)], [(0, 0), (1, 1), (2, 3), (3, 2)]),
    }
    edges, block_input = prepare(block_input)
    x_got = swap_edges(edges)

    def step(owner, triples, slopes, picks):
        pre, edges = temporal(owner, triples, slopes, taps_time)
        heres = [blocks[0] for blocks, _ in triples]
        outs = split_branches(owner, pre, edges, heres, taps_space, picks)
        return after(pre, *outs), outs

    x_own, slopes_own, actives_own = forward(block_input, x_got, taps_space, 2, (0, 3))
    ready = [([block], None) for block in frame_by_frame(cotangent)]
    pre, tops = step(
        3, ready, slopes_own, [lambda: place() < 2, lambda: place() >= 2]
    )
    first, second = (send(block, (3, 2, deal[2][k])) for k, block in enumerate(tops))
    x_dealt = [
        send(block, *((s, s, deal[s][k]) for s in (1, 2)))
        for k, block in enumerate(frames_to_deal(block_input, x_got))
    ]
    grads = kernel_grads(3, x_own, pre, actives_own, ready, None)
    x_moved, slopes, actives = forward(
        block_input, x_got, taps_space, 2, (1, 2), x_dealt
    )

    ready = [([first, second], even), ([second, first], odd)]
    pre, outs = step(2, ready, slopes, [outer, inner, 0, 1])
    ends, others, *results = outs
    end = send(ends, (2, 1, stay))
    other = send(others, (2, 1, stay))
    cross = send(others, (2, 1, [(i, i ^ 2) for i in range(4)]))
    grads = kernel_grads(2, x_moved, pre, actives, ready, grads)

    ready = [([cross, other, end], low), ([end, cross], low)]
    pre, outs = step(1, ready, slopes, [0, 1, lambda: place() < 2, lambda: place() >= 2])
    middles, ends, ups, downs = outs
    results += [middles, ends]
    pieces = [
        send(ends, (1, 0, stay)),
        send(ups, (1, 0, [(0, 1), (1, 2), (2, 3)])),
        send(middles, (1, 0, stay)),
        send(downs, (1, 0, [(1, 0), (2, 1), (3, 2)])),
    ]
    grads = kernel_grads(1, x_moved, pre, actives, ready, grads)
    returned = [
        send(block, *((s, s, back(deal[s][k])) for s in (1, 2)))
        for k, block in enumerate(after(to_return(results), pieces[1], pieces[3]))
    ]
    before, one, two, later = line_up(after(pieces, *returned))
    ready = [([one, two, before], None), ([two, later, one], None)]
    pre, edges = temporal(0, ready, slopes_own, taps_time)
    grads = kernel_grads(0, x_own, pre, actives_own, ready, grads, True)

    def finish(lasts, parts):
        return own_result(tops, returned, lasts)

    return grads, (pre, edges, [one, two]), finish


def section_run(x_saved, cotangent, w_spatial, w_temporal):
    block_input = x_saved[0]
    taps_space = w_spatial[0]
    taps_time = w_temporal[0]
    channels = block_input.shape[-1]
    row_parts = lax.axis_size("row")
    shape = (lax.axis_size("section"), lax.axis_size("frame"), row_parts, block_input.shape[0])
    dealt = shape == (4, 4, 2, 2) and (12 * channels) % 128 == 0
    chains = dealt_chains if dealt else shifted_chains
    grads, (pre, edges, heres), finish = chains(block_input, cotangent, taps_space, taps_time)

    def last_branch(parts):
        return finish(branches(0, pre, swap_edges(after(edges, parts)), heres, taps_space), parts)

    if dealt:
        lasts = split_branches(0, pre, edges, heres, taps_space, [0, 1])

        def result(parts):
            return finish(after(lasts, *parts), parts)

        space, time, own = sum_kernels(*grads, lasts, result)
        return (
            own[None],
            space.reshape((1, 3, 3, channels, channels)),
            time.reshape((1, 3, channels, channels)),
        )
    total, _ = sum_over(grads.reshape(-1, channels), "row")

    total, own = sum_over(total, "frame", last_branch)
    total = gather_parts(total.astype(jnp.bfloat16), "frame")
    split = 9 * channels
    if row_parts == 2:
        first = lax.axis_index("row") == 0
        other = lax.ppermute(total, "row", [(0, 1), (1, 0)])
        rest = split - total.shape[0]
        space = jnp.where(
            first,
            jnp.concatenate([total, other[:rest]]),
            jnp.concatenate([other, total[:rest]]),
        )
        time = jnp.where(first, other[rest:], total[rest:])
    else:
        total = gather_parts(total, "row")
        space, time = total[:split], total[split:]
    return (
        own[None],
        space.astype(jnp.float32).reshape((1, 3, 3, channels, channels)),
        time.astype(jnp.float32).reshape((1, 3, channels, channels)),
    )


def solution(mesh):
    return jax.shard_map(
        section_run,
        mesh=mesh,
        in_specs=(
            P("section", "frame", "row", None, None),
            P("frame", "row", None, None),
            P("section", None, None, None, None),
            P("section", None, None, None),
        ),
        out_specs=(
            P("section", "frame", "row", None, None),
            P("section", None, None, None, None),
            P("section", None, None, None),
        ),
        check_vma=False,
    )
```
